32 devices in a mesh: groups: 2 (over x), seq: 16 (over z, y, core).
Axes of the slice: x: 2, y: 2, z: 4, core: 2. Of those that a mesh axis runs over, the one named last changes fastest.
Arguments:
- features: bfloat16 [4096, 2048], P(('groups', 'seq')), parts along dimension 0, may hold values from -40 to 40
- state_write: bfloat16 [4096, 64], P(('groups', 'seq')), parts along dimension 0, may hold values from -0.75 to 0.75
- state_read: bfloat16 [4096, 64], P(('groups', 'seq')), parts along dimension 0, may hold values from -0.75 to 0.75
- log_decay: float32 [4096, 32], P(('groups', 'seq')), parts along dimension 0, may hold values from -2 to 0
- skip_gain: float32 [32], replicated, may hold values from 1 to 4
- post_gain: float32 [2048], replicated, may hold values from 0.5 to 2
- start_index: int32 [4096], P(('groups', 'seq')), parts along dimension 0, may hold values from 0 to 2047, as said below
- step_noise: bfloat16 [3, 4096, 1024], P(None, ('groups', 'seq')), parts along dimension 1, may hold values from -4 to 4
- act_weight: bfloat16 [2048, 128], replicated, may hold values from -0.125 to 0.125
- dyn_weight: bfloat16 [2048, 1024], replicated, may hold values from -0.125 to 0.125
- act_in_weight: bfloat16 [128, 1024], replicated, may hold values from -0.5 to 0.5
- out_weight: bfloat16 [1024, 2048], replicated, may hold values from -0.1875 to 0.1875
- value_weight: bfloat16 [1024], replicated, may hold values from -0.1875 to 0.1875
Outputs:
- posterior: bfloat16 [4096, 2048], P(('groups', 'seq')), parts along dimension 0
- values: float32 [3, 4096], P(None, ('groups', 'seq')), parts along dimension 1
- final_latent: bfloat16 [4096, 2048], P(('groups', 'seq')), parts along dimension 0
The draws below stay inside these ranges and needn't reach their ends.
There are 2 independent parts, one for each index of `groups`. The reference program is written for one: setup_inputs(seed, part) draws one part's arguments, and reference() takes and returns one part's arrays. A program takes and returns all parts, laid end to end along the dimension named above; an argument that names none is the same for every part. Nothing has to cross between parts.
Inputs may be any that keep to these rules, and one draw needn't show every extreme that they name: `start_index`: each aligned block of 128 starts (the starts of one device) names exactly 8 time steps in every aligned range of 128 time steps.
All inputs are finite; a program needn't handle non-finite values.
Results may differ from the reference program's by a relative error of at most 0.01.
Values may be sent and summed in bfloat16 or wider, within the bound.
No kernel may reach another device: no remote copies, remote signals or barrier semaphores. Data moves between devices by JAX's collectives and lax.ppermute only.
A program may use at most 192 MiB of HBM per device.

```python
import math
import jax
import jax.numpy as jnp
from jax import lax

D = 2048
HEAD_DIM = 64
STATE = 64
HID = 1024
ACT = 128
HORIZON = 3
TOK_DEV = 128
STARTS_DEV = 128
HEAD_TOTAL = 32
TOKEN_STEPS = 2048
STARTS = 2048
CAP = 8


def draw_features(key, part):
    random_keys = jax.random.split(key, 3)
    row_scale = jnp.exp(jax.random.uniform(random_keys[0], (TOKEN_STEPS, 1), minval=0.0, maxval=jnp.log(10.0)))
    col_scale = jnp.exp(jax.random.uniform(random_keys[1], (1, D), minval=0.0, maxval=jnp.log(10.0)))
    base = jnp.clip(jax.random.normal(random_keys[2], (TOKEN_STEPS, D)), -4.0, 4.0)
    return (base * row_scale * col_scale / 10.0).astype(jnp.bfloat16)


def draw_log_decay(key, part):
    random_keys = jax.random.split(key, 5)
    fast = jax.random.uniform(random_keys[0], (HEAD_TOTAL,)) < 0.5
    fast_rate = jnp.exp(jax.random.uniform(random_keys[1], (HEAD_TOTAL,), minval=jnp.log(1.0 / 50.0), maxval=jnp.log(1.0 / 30.0)))
    slow_rate = 0.3 / TOKEN_STEPS
    baseline_rate = jnp.where(fast, fast_rate, slow_rate)
    coarse_value = jnp.exp(jax.random.uniform(random_keys[2], (TOKEN_STEPS, HEAD_TOTAL), minval=-0.7, maxval=0.7))
    spike_rows = jax.random.randint(random_keys[3], (3,), 0, TOKEN_STEPS)
    spike_loss = jax.random.uniform(random_keys[4], (3, HEAD_TOTAL), minval=0.2, maxval=0.5)
    token_positions = jnp.arange(TOKEN_STEPS, dtype=jnp.int32)
    matched_rows = (token_positions[:, None] == spike_rows[None, :]).astype(jnp.float32)
    spike_events = jnp.sum(matched_rows[:, :, None] * jnp.log1p(-spike_loss)[None, :, :], axis=1)
    return (-baseline_rate[None, :] * coarse_value + spike_events).astype(jnp.float32)


def draw_start_index(key, part):
    block_count = STARTS // STARTS_DEV
    random_keys = jax.random.split(key, 2)
    slot_ids = jnp.arange(STARTS_DEV, dtype=jnp.int32)
    owners = jnp.broadcast_to((slot_ids // CAP)[None, :], (block_count, STARTS_DEV))
    perm_keys = jax.random.split(random_keys[0], block_count)
    shuffles = jax.vmap(lambda one_key: jax.random.permutation(one_key, STARTS_DEV))(perm_keys)
    owners = jnp.take_along_axis(owners, shuffles.astype(jnp.int32), axis=1)
    offsets = jax.random.randint(random_keys[1], (block_count, STARTS_DEV), 0, TOK_DEV)
    return (owners * TOK_DEV + offsets).reshape(STARTS).astype(jnp.int32)


def steps_of(own_key, shape, shards, smallest, top_value):
    level, own = 1.0, jax.random.fold_in(own_key, 6)
    for axis_at, shards_of in shards:
        heights = jnp.exp(jax.random.uniform(jax.random.fold_in(own, axis_at), (shards_of,), jnp.float32, smallest / len(shards), top_value / len(shards)))
        level = level * jnp.repeat(heights, shape[axis_at] // shards_of).reshape([-1 if axis == axis_at else 1 for axis in range(len(shape))])
    return level


def noise(key, extent, deviation, limit, cuts=(), held_as=jnp.bfloat16):
    gain = steps_of(key, extent, cuts, -0.22, 0.18) if cuts else 1.0
    entries = jax.random.normal(key, extent, jnp.float32) * deviation * gain
    return jnp.minimum(jnp.maximum(entries, -limit), limit).astype(held_as)


def setup_inputs(seed: int = 0, part: int = 0) -> dict:
    splits = jax.random.split(jax.random.key(seed), 14)
    part_keys = jax.random.split(jax.random.fold_in(splits[13], part), 14)
    features = draw_features(jax.random.fold_in(jax.random.fold_in(splits[13], part), 71), part)
    state_write = noise(part_keys[1], (TOKEN_STEPS, STATE), STATE ** -0.5, 0.75, ((0, 16),))
    state_read = noise(part_keys[2], (TOKEN_STEPS, STATE), STATE ** -0.5, 0.75, ((0, 16),))
    log_decay = draw_log_decay(jax.random.fold_in(jax.random.fold_in(splits[13], part), 71), part)
    skip_gain = jnp.clip(jnp.exp(jax.random.uniform(splits[4], (HEAD_TOTAL,), jnp.float32, math.log(1.0), math.log(4.0))), 1.0, 4.0)
    post_gain = jnp.clip(jnp.exp(jax.random.uniform(splits[5], (D,), jnp.float32, math.log(0.5), math.log(2.0))), 0.5, 2.0)
    start_index = draw_start_index(jax.random.fold_in(jax.random.fold_in(splits[13], part), 71), part)
    step_noise = noise(part_keys[7], (HORIZON, STARTS, HID), 1.0, 4.0, ((1, 16),))
    act_weight = noise(splits[8], (D, ACT), D ** -0.5, 0.125)
    dyn_weight = noise(splits[9], (D, HID), D ** -0.5, 0.125)
    act_in_weight = noise(splits[10], (ACT, HID), ACT ** -0.5, 0.5)
    out_weight = noise(splits[11], (HID, D), HID ** -0.5, 0.1875)
    value_weight = noise(splits[12], (HID,), HID ** -0.5, 0.1875)
    return dict(features=features, state_write=state_write, state_read=state_read, log_decay=log_decay, skip_gain=skip_gain, post_gain=post_gain, start_index=start_index, step_noise=step_noise, act_weight=act_weight, dyn_weight=dyn_weight, act_in_weight=act_in_weight, out_weight=out_weight, value_weight=value_weight)


def reference(features, state_write, state_read, log_decay, skip_gain, post_gain, start_index, step_noise, act_weight, dyn_weight, act_in_weight, out_weight, value_weight):
    heads_in = features.astype(jnp.float32).reshape(TOKEN_STEPS, HEAD_TOTAL, HEAD_DIM)
    write_in = state_write.astype(jnp.float32)
    read_in = state_read.astype(jnp.float32)

    def advance(state_now, inputs):
        x_row, write_row, read_row, decay_row = inputs
        state_next = jnp.exp(decay_row)[:, None, None] * state_now + x_row[:, :, None] * write_row[None, None, :]
        read_out = jnp.einsum('hpn,n->hp', state_next, read_row, precision=lax.Precision.HIGHEST)
        return (state_next, read_out)
    start_state = jnp.zeros((HEAD_TOTAL, HEAD_DIM, STATE), jnp.float32)
    _, read_all = lax.scan(advance, start_state, (heads_in, write_in, read_in, log_decay))
    mixed = read_all + skip_gain[None, :, None] * heads_in
    square_mean = lax.optimization_barrier(jnp.mean(mixed * mixed, axis=-1, keepdims=True))
    normed_heads = mixed * lax.rsqrt(square_mean + 1e-05) * post_gain.reshape(HEAD_TOTAL, HEAD_DIM)[None]
    posterior = normed_heads.reshape(TOKEN_STEPS, D).astype(jnp.bfloat16)
    latent = jnp.take(posterior, start_index, axis=0)
    value_list = []
    for step_idx in range(HORIZON):
        wide = latent.astype(jnp.float32)
        normed = (wide * lax.rsqrt(lax.optimization_barrier(jnp.mean(wide * wide, axis=-1, keepdims=True)) + 1e-06)).astype(jnp.bfloat16)
        action = jnp.tanh(jnp.dot(normed, act_weight, preferred_element_type=jnp.float32)).astype(jnp.bfloat16)
        inner = jnp.dot(normed, dyn_weight, preferred_element_type=jnp.float32) + jnp.dot(action, act_in_weight, preferred_element_type=jnp.float32)
        hidden = (jax.nn.silu(inner) + step_noise[step_idx].astype(jnp.float32)).astype(jnp.bfloat16)
        value_list.append(jnp.dot(hidden, value_weight, preferred_element_type=jnp.float32))
        latent = (wide + jnp.dot(hidden, out_weight, preferred_element_type=jnp.float32)).astype(jnp.bfloat16)
    return (posterior, jnp.stack(value_list), latent)
```

```python
import functools
import jax
import jax.numpy as jnp
from jax import lax
from jax.experimental import pallas as pl
from jax.experimental.pallas import tpu as pltpu
from jax.sharding import PartitionSpec as P

F32 = jnp.float32
BF16 = jnp.bfloat16
LANES = 128
VMEM = pl.BlockSpec(memory_space=pltpu.VMEM)
SMEM = pl.BlockSpec(memory_space=pltpu.SMEM)


def iota(shape, dim):
    return lax.broadcasted_iota(jnp.int32, shape, dim)


def two_heads(cols, pair, head_width, shape):
    first = jnp.broadcast_to(cols[:, 2 * pair : 2 * pair + 1], shape)
    second = jnp.broadcast_to(cols[:, 2 * pair + 1 : 2 * pair + 2], shape)
    return jnp.where(iota(shape, 1) < head_width, first, second)


def before_kernel(peer_count, x_ref, write_ref, decay_ref, start_ref, send_ref, run_ref, run_t_ref, perm_ref, total_ref):
    rows, width = x_ref.shape
    head_count = decay_ref.shape[1]
    head_width = width // head_count
    state_size = write_ref.shape[1]
    half = width // 2
    lower = (iota((rows, rows), 0) >= iota((rows, rows), 1)).astype(F32)
    running = jnp.dot(lower, decay_ref[...], precision=lax.Precision.HIGHEST, preferred_element_type=F32)
    run_ref[...] = running
    run_t_ref[...] = running.T
    last = running[rows - 1 : rows, :]
    total = jnp.exp(last)
    total_ref[...] = total
    tail = jnp.exp(last - running)
    write_t = write_ref[...].T
    for pair in range(head_count // 2):
        lanes = slice(pair * LANES, (pair + 1) * LANES)
        scaled = (x_ref[:, lanes].astype(F32) * two_heads(tail, pair, head_width, (rows, LANES))).astype(BF16)
        ends = jnp.dot(write_t, scaled, preferred_element_type=F32)
        side, at = divmod(pair * LANES, half)
        send_ref[side, :, at : at + LANES] = ends
    starts = start_ref.shape[1]
    cap = starts // peer_count
    index = jnp.broadcast_to(start_ref[...].astype(F32), (starts, starts))
    index_t = index.T
    owner = jnp.floor(index * (1.0 / rows))
    owner_t = jnp.floor(index_t * (1.0 / rows))
    earlier = (iota((starts, starts), 1) < iota((starts, starts), 0)) & (owner == owner_t)
    rank = jnp.sum(earlier.astype(F32), axis=1, keepdims=True)
    slot = owner_t * cap + rank
    perm = (slot == iota((starts, starts), 1).astype(F32)).astype(F32)
    perm_ref[...] = perm.astype(BF16)
    offset = index_t - owner_t * rows
    wanted = jnp.sum(perm * offset, axis=0, keepdims=True)
    high = total.astype(BF16).astype(F32)
    meta = jnp.zeros((state_size, LANES), F32)
    row_at = iota((state_size, LANES), 0)
    pad = jnp.zeros((1, LANES - head_count), F32)
    meta = jnp.where(row_at == 0, jnp.concatenate([high, pad], axis=1), meta)
    meta = jnp.where(row_at == 1, jnp.concatenate([total - high, pad], axis=1), meta)
    meta = jnp.where(row_at == 2, wanted, meta)
    send_ref[0, :, half : half + LANES] = meta
    send_ref[1, :, half : half + LANES] = meta


def local_kernel(x_ref, write_ref, read_ref, run_ref, run_t_ref, skip_ref, out_ref):
    rows, width = x_ref.shape
    head_count = run_ref.shape[1]
    head_width = width // head_count
    gram = lax.dot_general(
        read_ref[...], write_ref[...], (((1,), (1,)), ((), ())), preferred_element_type=F32
    )
    square = (rows, rows)
    mask = iota(square, 0) >= iota(square, 1)
    lane = iota((rows, LANES), 1)
    for pair in range(head_count // 2):
        lanes = slice(pair * LANES, (pair + 1) * LANES)
        weights = []
        for head in (2 * pair, 2 * pair + 1):
            spread = run_ref[:, head : head + 1] - run_t_ref[head : head + 1, :]
            weights.append((jnp.exp(jnp.where(mask, spread, -jnp.inf)) * gram).astype(BF16))
        x = x_ref[:, lanes]
        zero = jnp.zeros_like(x)
        split = jnp.concatenate([jnp.where(lane < head_width, x, zero), jnp.where(lane < head_width, zero, x)], axis=0)
        inner = jnp.dot(jnp.concatenate(weights, axis=1), split, preferred_element_type=F32)
        out_ref[:, lanes] = inner + skip_ref[:, lanes] * x.astype(F32)


def after_kernel(core_ref, local_ref, read_ref, run_ref, keep_ref, got_ref, gain_ref, pick_ref, post_ref, sent_ref):
    rows, width = local_ref.shape
    head_count = run_ref.shape[1]
    head_width = width // head_count
    half = width // 2
    entered = jnp.exp(run_ref[...])
    read = read_ref[...]
    pick = pick_ref[...]
    mine_first = core_ref[0] == 0
    square = (LANES, LANES)
    same_head = (iota(square, 0) // head_width == iota(square, 1) // head_width).astype(BF16)
    for pair in range(head_count // 2):
        lanes = slice(pair * LANES, (pair + 1) * LANES)
        side, at = divmod(pair * LANES, half)
        keep, got = keep_ref[:, at : at + LANES], got_ref[:, at : at + LANES]
        carry = jnp.where(mine_first, keep, got) if side == 0 else jnp.where(mine_first, got, keep)
        carried = jnp.dot(read, carry, preferred_element_type=F32)
        mixed = local_ref[:, lanes] + carried * two_heads(entered, pair, head_width, (rows, LANES))
        squares = mixed * mixed
        high = squares.astype(BF16)
        low = (squares - high.astype(F32)).astype(BF16)
        total = jnp.dot(high, same_head, preferred_element_type=F32) + jnp.dot(
            low, same_head, preferred_element_type=F32
        )
        scale = lax.rsqrt(total * (1.0 / head_width) + 1e-05)
        posterior = (mixed * scale * gain_ref[:, lanes]).astype(BF16)
        post_ref[:, lanes] = posterior
        sent_ref[:, lanes] = jnp.dot(pick, posterior, preferred_element_type=F32).astype(BF16)


def imagine_kernel(landed_ref, perm_ref, noise_ref, act_ref, dyn_ref, act_in_ref, out_ref, value_ref, values_ref, final_ref):
    horizon = noise_ref.shape[0]
    latent = jnp.dot(perm_ref[...], landed_ref[...], preferred_element_type=F32)
    rows = []
    for step in range(horizon):
        scale = lax.rsqrt(jnp.mean(latent * latent, axis=1, keepdims=True) + 1e-06)
        normed = (latent * scale).astype(BF16)
        action = jnp.tanh(jnp.dot(normed, act_ref[...], preferred_element_type=F32)).astype(BF16)
        inner = jnp.dot(normed, dyn_ref[...], preferred_element_type=F32) + jnp.dot(
            action, act_in_ref[...], preferred_element_type=F32
        )
        hidden = (inner / (1.0 + jnp.exp(-inner)) + noise_ref[step].astype(F32)).astype(BF16)
        value = lax.dot_general(
            value_ref[...], hidden, (((1,), (1,)), ((), ())), preferred_element_type=F32
        )
        rows.append(value[0:1, :])
        moved = latent + jnp.dot(hidden, out_ref[...], preferred_element_type=F32)
        latent = moved.astype(BF16).astype(F32)
    final_ref[...] = latent.astype(BF16)
    values_ref[...] = jnp.concatenate(rows, axis=0)


def shape_of(shape, dtype):
    return jax.ShapeDtypeStruct(shape, dtype)


def cost(flops, read):
    return pl.CostEstimate(flops=flops, bytes_accessed=read, transcendentals=0)


def per_device(
    peer_count,
    features,
    state_write,
    state_read,
    log_decay,
    skip_gain,
    post_gain,
    start_index,
    step_noise,
    act_weight,
    dyn_weight,
    act_in_weight,
    out_weight,
    value_weight,
):
    rows, width = features.shape
    head_count = log_decay.shape[1]
    head_width = width // head_count
    state_size = state_write.shape[1]
    half = width // 2
    starts = start_index.shape[0]
    cap = starts // peer_count
    mine = lax.axis_index("seq")
    core = mine % 2
    params = pltpu.CompilerParams(vmem_limit_bytes=24 << 20)

    sides, running, running_t, perm, total = pl.pallas_call(
        functools.partial(before_kernel, peer_count),
        out_shape=(
            shape_of((2, state_size, half + LANES), F32),
            shape_of((rows, head_count), F32),
            shape_of((head_count, rows), F32),
            shape_of((starts, starts), BF16),
            shape_of((1, head_count), F32),
        ),
        in_specs=[VMEM] * 4,
        out_specs=(VMEM,) * 5,
        compiler_params=params,
    )(features, state_write, log_decay, start_index.reshape(1, starts))

    def spread_heads(per_head):
        own = lax.dynamic_slice(per_head, (core * (head_count // 2),), (head_count // 2,))
        return jnp.broadcast_to(own[:, None], (head_count // 2, head_width)).reshape(1, half)

    def swap(array, bit):
        return lax.ppermute(array, "seq", [(i, i ^ (1 << bit)) for i in range(peer_count)])

    def tagged(state, decay, wanted):
        high = decay.astype(BF16).astype(F32)
        pad = LANES - head_count
        meta = jnp.concatenate(
            [jnp.pad(high[None], ((0, 0), (0, pad))), jnp.pad((decay - high)[None], ((0, 0), (0, pad))), wanted], axis=0
        )
        blocks = -(-meta.shape[0] // state_size)
        meta = jnp.pad(meta, ((0, blocks * state_size - meta.shape[0]), (0, 0)))
        meta = [meta[k * state_size : (k + 1) * state_size] for k in range(blocks)]
        return jnp.concatenate([state] + meta, axis=1).astype(BF16)

    def untagged(array, count):
        array = array.astype(F32)
        blocks = (array.shape[1] - half) // LANES
        meta = jnp.concatenate([array[:, half + k * LANES : half + (k + 1) * LANES] for k in range(blocks)], axis=0)
        return array[:, :half], meta[0, :head_count] + meta[1, :head_count], meta[2 : 2 + count]

    upper = core == 1
    got = swap(lax.dynamic_index_in_dim(sides, 1 - core, 0, False).astype(BF16), 0)
    got_state, got_decay, got_wanted = untagged(got, 1)
    own_full = lax.dynamic_index_in_dim(sides, core, 0, False)
    own_state = own_full[:, :half]
    own_wanted = own_full[2:3, half:]
    own_decay = total[0]
    first_state = jnp.where(upper, got_state, own_state)
    first_decay = jnp.where(upper, got_decay, own_decay)
    second_state = jnp.where(upper, own_state, got_state)
    second_decay = jnp.where(upper, own_decay, got_decay)
    group_state = first_state * spread_heads(second_decay) + second_state
    group_decay = first_decay * second_decay
    wanted = jnp.where(
        upper, jnp.concatenate([got_wanted, own_wanted]), jnp.concatenate([own_wanted, got_wanted])
    )
    prefix = jnp.zeros_like(group_state)
    prefix_decay = jnp.ones_like(group_decay)

    local_out = None
    bits = peer_count.bit_length() - 1
    for bit in range(1, bits):
        later = (mine >> bit) % 2 == 1
        arrived = swap(tagged(group_state, group_decay, wanted), bit)
        if bit == 1:
            local_out = pl.pallas_call(
                local_kernel,
                out_shape=shape_of((rows, width), F32),
                in_specs=[VMEM] * 6,
                out_specs=VMEM,
                compiler_params=params,
                cost_estimate=cost(4 * rows * rows * width, 2 * rows * width),
            )(
                features,
                state_write,
                state_read,
                running,
                running_t,
                jnp.broadcast_to(skip_gain[:, None], (head_count, head_width)).reshape(1, width),
            )
        new_state, new_decay, new_wanted = untagged(arrived, wanted.shape[0])
        prefix = jnp.where(later, prefix + spread_heads(prefix_decay) * new_state, prefix)
        prefix_decay = jnp.where(later, prefix_decay * new_decay, prefix_decay)
        group_state = jnp.where(
            later,
            new_state * spread_heads(group_decay) + group_state,
            group_state * spread_heads(new_decay) + new_state,
        )
        group_decay = group_decay * new_decay
        wanted = jnp.where(
            later, jnp.concatenate([new_wanted, wanted]), jnp.concatenate([wanted, new_wanted])
        )

    second_entry = prefix * spread_heads(first_decay) + first_state
    keep = jnp.where(upper, second_entry, prefix).astype(BF16)
    back = swap(jnp.where(upper, prefix, second_entry).astype(BF16), 0)

    asked = lax.dynamic_slice(wanted, (0, mine * cap), (peer_count, cap)).reshape(starts, 1)
    pick = (asked == jnp.arange(rows, dtype=jnp.int32)[None, :].astype(F32)).astype(BF16)

    posterior, picked = pl.pallas_call(
        after_kernel,
        out_shape=(shape_of((rows, width), BF16), shape_of((starts, width), BF16)),
        in_specs=[SMEM] + [VMEM] * 7,
        out_specs=(VMEM, VMEM),
        compiler_params=params,
    )(core.reshape(1), local_out, state_read, running, keep, back, post_gain[None, :], pick)

    landed = lax.all_to_all(
        picked.reshape(peer_count, cap, width), "seq", split_axis=0, concat_axis=0, tiled=True
    ).reshape(starts, width)

    horizon = step_noise.shape[0]
    values, final_latent = pl.pallas_call(
        imagine_kernel,
        out_shape=(shape_of((horizon, starts), F32), shape_of((starts, width), BF16)),
        in_specs=[VMEM] * 8,
        out_specs=(VMEM, VMEM),
        compiler_params=pltpu.CompilerParams(vmem_limit_bytes=40 << 20),
    )(
        landed,
        perm,
        step_noise,
        act_weight,
        dyn_weight,
        act_in_weight,
        out_weight,
        jnp.broadcast_to(value_weight[None, :], (16, value_weight.shape[0])),
    )
    return (posterior, values, final_latent)


def solution(mesh):
    whole = P()
    by_row = P(("groups", "seq"), None)
    placed = (
        by_row,
        by_row,
        by_row,
        by_row,
        whole,
        whole,
        P(("groups", "seq")),
        P(None, ("groups", "seq"), None),
        whole,
        whole,
        whole,
        whole,
        whole,
    )
    return jax.shard_map(
        functools.partial(per_device, mesh.shape["seq"]),
        mesh=mesh,
        in_specs=placed,
        out_specs=(by_row, P(None, ("groups", "seq")), by_row),
        check_vma=False,
    )
```

```python
import functools
import jax
import jax.numpy as jnp
from jax import lax
from jax.experimental import pallas as pl
from jax.experimental.pallas import tpu as pltpu
from jax.sharding import PartitionSpec as P

F32 = jnp.float32
BF16 = jnp.bfloat16
LANES = 128
VMEM = pl.BlockSpec(memory_space=pltpu.VMEM)
SMEM = pl.BlockSpec(memory_space=pltpu.SMEM)


def iota(shape, dim):
    return lax.broadcasted_iota(jnp.int32, shape, dim)


def two_heads(cols, pair, head_width, shape):
    first = jnp.broadcast_to(cols[:, 2 * pair : 2 * pair + 1], shape)
    second = jnp.broadcast_to(cols[:, 2 * pair + 1 : 2 * pair + 2], shape)
    return jnp.where(iota(shape, 1) < head_width, first, second)


def before_kernel(peer_count, mine_ref, x_hbm, write_hbm, decay_hbm, start_hbm, own_ref, send_ref, run_ref, run_t_ref, perm_ref, aux_ref, expand_ref, x_ref, write_ref, decay_ref, start_ref, sems):
    copies = [
        pltpu.make_async_copy(source, target, sems.at[k])
        for k, (source, target) in enumerate(
            ((decay_hbm, decay_ref), (start_hbm, start_ref), (write_hbm, write_ref), (x_hbm, x_ref))
        )
    ]
    for copy in copies:
        copy.start()
    rows, width = x_ref.shape
    head_count = decay_ref.shape[0]
    head_width = width // head_count
    state_size = write_ref.shape[0]
    half = width // 2
    mine = mine_ref[0]
    core = mine % 2
    expand_shape = (LANES, half)
    expand_ref[...] = (
        iota(expand_shape, 0) == iota(expand_shape, 1) // head_width + core * (head_count // 2)
    ).astype(F32).astype(BF16)
    upper = (iota((rows, rows), 0) <= iota((rows, rows), 1)).astype(F32)
    copies[0].wait()
    running_t = jnp.dot(decay_ref[...], upper, precision=lax.Precision.HIGHEST, preferred_element_type=F32)
    running = running_t.T
    run_ref[...] = running
    run_t_ref[...] = running_t
    last = running[rows - 1 : rows, :]
    total = jnp.exp(last)
    tail = jnp.exp(last - running)
    copies[1].wait()
    starts = start_ref.shape[1]
    cap = starts // peer_count
    index = jnp.broadcast_to(start_ref[...].astype(F32), (starts, starts))
    index_t = index.T
    owner = jnp.floor(index * (1.0 / rows))
    owner_t = jnp.floor(index_t * (1.0 / rows))
    earlier = (iota((starts, starts), 1) < iota((starts, starts), 0)) & (owner == owner_t)
    rank = jnp.sum(earlier.astype(F32), axis=1, keepdims=True)
    slot = owner_t * cap + rank
    perm = (slot == iota((starts, starts), 1).astype(F32)).astype(F32)
    perm_ref[...] = perm.astype(BF16)
    offset = index_t - owner_t * rows
    wanted = jnp.sum(perm * offset, axis=0, keepdims=True)
    total = jnp.concatenate([total, jnp.zeros((1, LANES - head_count), F32)], axis=1)
    aux_ref[...] = stack_rows([total, wanted], aux_ref.shape[0])
    write_meta(send_ref, total, wanted, half, state_size)
    copies[2].wait()
    write_t = write_ref[...]
    copies[3].wait()
    pairs = head_count // 2
    for pair in range(pairs // 2):
        ends = []
        for at in (pair, pair + pairs // 2):
            lanes = slice(at * LANES, (at + 1) * LANES)
            scaled = x_ref[:, lanes].astype(F32) * two_heads(tail, at, head_width, (rows, LANES))
            ends.append(jnp.dot(write_t, scaled.astype(BF16), preferred_element_type=F32))
        lanes = slice(pair * LANES, (pair + 1) * LANES)
        own_ref[:, lanes] = jnp.where(core == 0, ends[0], ends[1])
        send_ref[:, lanes] = jnp.where(core == 0, ends[1], ends[0]).astype(BF16)


def stack_rows(rows, count):
    used = sum(row.shape[0] for row in rows)
    if used < count:
        rows = list(rows) + [jnp.zeros((count - used, LANES), F32)]
    return jnp.concatenate(rows, axis=0)


def write_meta(send_ref, decay, wanted, half, state_size):
    high = decay.astype(BF16).astype(F32)
    blocks = (send_ref.shape[1] - half) // LANES
    meta = stack_rows([high, decay - high, wanted], blocks * state_size).astype(BF16)
    for block in range(blocks):
        send_ref[:, half + block * LANES : half + (block + 1) * LANES] = meta[
            block * state_size : (block + 1) * state_size
        ]


def read_meta(got_ref, count, half, state_size):
    blocks = (got_ref.shape[1] - half) // LANES
    meta = jnp.concatenate(
        [got_ref[:, half + block * LANES : half + (block + 1) * LANES].astype(F32) for block in range(blocks)], axis=0
    )
    return meta[0:1] + meta[1:2], meta[2 : 2 + count]


def spread_rows(rows, expand_ref):
    pieces = []
    for row in rows:
        high = row.astype(BF16).astype(F32)
        pieces += [high, row - high]
    table = stack_rows(pieces, 16).astype(BF16)
    wide = jnp.dot(table, expand_ref[...], preferred_element_type=F32)
    return [wide[2 * k : 2 * k + 1] + wide[2 * k + 1 : 2 * k + 2] for k in range(len(rows))]


def pair_kernel(mine_ref, own_ref, got_ref, aux_ref, expand_ref, first_ref, group_ref, send_ref, aux_out_ref):
    state_size, half = own_ref.shape
    upper = mine_ref[0] % 2 == 1
    new_decay, new_wanted = read_meta(got_ref, 1, half, state_size)
    decay, wanted = aux_ref[0:1], aux_ref[1:2]
    first_decay = jnp.where(upper, new_decay, decay)
    second_decay = jnp.where(upper, decay, new_decay)
    (factor,) = spread_rows([second_decay], expand_ref)
    own, got = own_ref[...], got_ref[:, :half].astype(F32)
    first = jnp.where(upper, got, own)
    group = first * factor + jnp.where(upper, own, got)
    first_ref[...] = first
    group_ref[...] = group
    send_ref[:, :half] = group.astype(BF16)
    group_decay = first_decay * second_decay
    wanted = jnp.concatenate(
        [jnp.where(upper, new_wanted, wanted), jnp.where(upper, wanted, new_wanted)], axis=0
    )
    write_meta(send_ref, group_decay, wanted, half, state_size)
    aux_out_ref[...] = stack_rows(
        [group_decay, jnp.ones((1, LANES), F32), first_decay, wanted], aux_out_ref.shape[0]
    )


def stage_kernel(bit, mine_ref, group_ref, prefix_ref, aux_ref, got_ref, expand_ref, group_out, prefix_out, send_ref, aux_out):
    state_size, half = group_ref.shape
    count = 1 << bit
    later = (mine_ref[0] >> bit) % 2 == 1
    new_decay, new_wanted = read_meta(got_ref, count, half, state_size)
    decay, prefix_decay, first_decay = aux_ref[0:1], aux_ref[1:2], aux_ref[2:3]
    wanted = aux_ref[3 : 3 + count]
    into, across = spread_rows([prefix_decay, jnp.where(later, decay, new_decay)], expand_ref)
    group, got = group_ref[...], got_ref[:, :half].astype(F32)
    moved = into * got
    if prefix_ref is not None:
        moved = prefix_ref[...] + moved
        prefix_out[...] = jnp.where(later, moved, prefix_ref[...])
    else:
        prefix_out[...] = jnp.where(later, moved, jnp.zeros_like(moved))
    total = jnp.where(later, got, group) * across + jnp.where(later, group, got)
    group_out[...] = total
    send_ref[:, :half] = total.astype(BF16)
    wanted = jnp.concatenate(
        [jnp.where(later, new_wanted, wanted), jnp.where(later, wanted, new_wanted)], axis=0
    )
    write_meta(send_ref, decay * new_decay, wanted, half, state_size)
    aux_out[...] = stack_rows(
        [decay * new_decay, jnp.where(later, prefix_decay * new_decay, prefix_decay), first_decay, wanted],
        aux_out.shape[0],
    )


def first_stage_kernel(bit, mine_ref, group_ref, aux_ref, got_ref, expand_ref, *outs):
    stage_kernel(bit, mine_ref, group_ref, None, aux_ref, got_ref, expand_ref, *outs)


def last_stage_kernel(bit, rows, mine_ref, prefix_ref, aux_ref, got_ref, expand_ref, first_ref, keep_ref, back_ref, pick_ref):
    state_size, half = first_ref.shape
    count = 1 << bit
    mine = mine_ref[0]
    later = (mine >> bit) % 2 == 1
    upper = mine % 2 == 1
    _, new_wanted = read_meta(got_ref, count, half, state_size)
    into, across = spread_rows([aux_ref[1:2], aux_ref[2:3]], expand_ref)
    prefix = prefix_ref[...]
    prefix = jnp.where(later, prefix + into * got_ref[:, :half].astype(F32), prefix)
    entry = prefix * across + first_ref[...]
    keep_ref[...] = jnp.where(upper, entry, prefix).astype(BF16)
    back_ref[...] = jnp.where(upper, prefix, entry).astype(BF16)
    wanted = aux_ref[3 : 3 + count]
    wanted = jnp.concatenate(
        [jnp.where(later, new_wanted, wanted), jnp.where(later, wanted, new_wanted)], axis=0
    )
    peers = 2 * count
    starts = pick_ref.shape[0]
    cap = starts // peers
    table = jnp.concatenate([wanted, jnp.zeros((LANES - peers, LANES), F32)], axis=0) if peers < LANES else wanted
    asker = (iota((starts, LANES), 0) // cap == iota((starts, LANES), 1)).astype(F32).astype(BF16)
    by_slot = jnp.dot(asker, table.astype(BF16), preferred_element_type=F32)
    here = iota((starts, LANES), 1) == mine * cap + iota((starts, LANES), 0) % cap
    asked = jnp.sum(jnp.where(here, by_slot, 0.0), axis=1, keepdims=True)
    pick_ref[...] = (asked == iota((starts, rows), 1).astype(F32)).astype(F32).astype(BF16)


def local_kernel(x_ref, write_ref, read_ref, run_ref, run_t_ref, skip_ref, out_ref):
    rows, width = x_ref.shape
    head_count = run_ref.shape[1]
    head_width = width // head_count
    gram = jnp.dot(read_ref[...].T, write_ref[...], preferred_element_type=F32)
    square = (rows, rows)
    mask = iota(square, 0) >= iota(square, 1)
    lane = iota((rows, LANES), 1)
    for pair in range(head_count // 2):
        lanes = slice(pair * LANES, (pair + 1) * LANES)
        weights = []
        for head in (2 * pair, 2 * pair + 1):
            spread = run_ref[:, head : head + 1] - run_t_ref[head : head + 1, :]
            weights.append((jnp.exp(jnp.where(mask, spread, -jnp.inf)) * gram).astype(BF16))
        x = x_ref[:, lanes]
        zero = jnp.zeros_like(x)
        split = jnp.concatenate([jnp.where(lane < head_width, x, zero), jnp.where(lane < head_width, zero, x)], axis=0)
        inner = jnp.dot(jnp.concatenate(weights, axis=1), split, preferred_element_type=F32)
        out_ref[:, lanes] = inner + skip_ref[:, lanes] * x.astype(F32)


def after_kernel(mine_ref, local_ref, read_ref, run_ref, keep_ref, got_ref, gain_ref, pick_ref, post_ref, sent_ref, mixed_ref, total_ref):
    rows, width = local_ref.shape
    head_count = run_ref.shape[1]
    head_width = width // head_count
    half = width // 2
    entered = jnp.exp(run_ref[...])
    read = read_ref[...].T
    mine_first = mine_ref[0] % 2 == 0
    square = (LANES, LANES)
    same_head = (iota(square, 0) // head_width == iota(square, 1) // head_width).astype(F32).astype(BF16)
    blocks = [slice(k * LANES, (k + 1) * LANES) for k in range(width // LANES)]
    keep, got = keep_ref[...], got_ref[...]
    for side in range(2):
        carry = jnp.where(mine_first, keep, got) if side == 0 else jnp.where(mine_first, got, keep)
        total_ref[:, side * half : (side + 1) * half] = jnp.dot(read, carry, preferred_element_type=F32)
    for pair, lanes in enumerate(blocks):
        mixed_ref[:, lanes] = local_ref[:, lanes] + total_ref[:, lanes] * two_heads(
            entered, pair, head_width, (rows, LANES)
        )
    for lanes in blocks:
        mixed = mixed_ref[:, lanes]
        squares = mixed * mixed
        high = squares.astype(BF16)
        low = (squares - high.astype(F32)).astype(BF16)
        total_ref[:, lanes] = jnp.dot(high, same_head, preferred_element_type=F32) + jnp.dot(
            low, same_head, preferred_element_type=F32
        )
    for lanes in blocks:
        scale = lax.rsqrt(total_ref[:, lanes] * (1.0 / head_width) + 1e-05)
        post_ref[:, lanes] = (mixed_ref[:, lanes] * scale * gain_ref[:, lanes]).astype(BF16)
    sent_ref[...] = jnp.dot(pick_ref[...], post_ref[...], preferred_element_type=F32).astype(BF16)


def flush_kernel(from_ref, to_ref):
    to_ref[...] = from_ref[...]


def imagine_kernel(landed_ref, perm_ref, noise_ref, act_ref, dyn_ref, act_in_ref, out_ref, value_ref, values_ref, final_ref):
    horizon = noise_ref.shape[0]
    latent = jnp.dot(perm_ref[...], landed_ref[...], preferred_element_type=F32)
    rows = []
    for step in range(horizon):
        scale = lax.rsqrt(jnp.mean(latent * latent, axis=1, keepdims=True) + 1e-06)
        normed = (latent * scale).astype(BF16)
        action = jnp.tanh(jnp.dot(normed, act_ref[...], preferred_element_type=F32)).astype(BF16)
        inner = jnp.dot(normed, dyn_ref[...], preferred_element_type=F32) + jnp.dot(
            action, act_in_ref[...], preferred_element_type=F32
        )
        hidden = (inner / (1.0 + jnp.exp(-inner)) + noise_ref[step].astype(F32)).astype(BF16)
        value = lax.dot_general(
            value_ref[...], hidden, (((1,), (1,)), ((), ())), preferred_element_type=F32
        )
        rows.append(value[0:1, :])
        moved = latent + jnp.dot(hidden, out_ref[...], preferred_element_type=F32)
        latent = moved.astype(BF16).astype(F32)
    final_ref[...] = latent.astype(BF16)
    values_ref[...] = jnp.concatenate(rows, axis=0)


def shape_of(shape, dtype):
    return jax.ShapeDtypeStruct(shape, dtype)


def cost(flops, read):
    return pl.CostEstimate(flops=flops, bytes_accessed=read, transcendentals=0)


def per_device(
    peer_count,
    features,
    state_write,
    state_read,
    log_decay,
    skip_gain,
    post_gain,
    start_index,
    step_noise,
    act_weight,
    dyn_weight,
    act_in_weight,
    out_weight,
    value_weight,
):
    rows, width = features.shape
    head_count = log_decay.shape[1]
    head_width = width // head_count
    state_size = state_write.shape[1]
    half = width // 2
    starts = start_index.shape[0]
    cap = starts // peer_count
    mine = lax.axis_index("seq").reshape(1)
    params = pltpu.CompilerParams(vmem_limit_bytes=12 << 20)
    hbm = pl.BlockSpec(memory_space=pltpu.HBM)
    read_t = state_read.T
    write_t = state_write.T
    bits = peer_count.bit_length() - 1

    def payload(count):
        blocks = -(-(2 + count) // state_size)
        return shape_of((state_size, half + blocks * LANES), BF16)

    def auxiliary(count):
        return shape_of((-(-(3 + count) // 8) * 8, LANES), F32)

    own, send, running, running_t, perm, aux, expand = pl.pallas_call(
        functools.partial(before_kernel, peer_count),
        out_shape=(
            shape_of((state_size, half), F32),
            payload(1),
            shape_of((rows, head_count), F32),
            shape_of((head_count, rows), F32),
            shape_of((starts, starts), BF16),
            auxiliary(1),
            shape_of((LANES, half), BF16),
        ),
        in_specs=[SMEM] + [hbm] * 4,
        out_specs=(VMEM,) * 7,
        scratch_shapes=[
            pltpu.VMEM((rows, width), BF16),
            pltpu.VMEM((state_size, rows), BF16),
            pltpu.VMEM((head_count, rows), F32),
            pltpu.VMEM((1, starts), jnp.int32),
            pltpu.SemaphoreType.DMA((4,)),
        ],
        compiler_params=params,
    )(mine, features, write_t, log_decay.T, start_index.reshape(1, starts))

    def swap(array, bit):
        return lax.ppermute(array, "seq", [(i, i ^ (1 << bit)) for i in range(peer_count)])

    wide = shape_of((state_size, half), F32)
    got = swap(send, 0)
    first, group, send, aux = pl.pallas_call(
        pair_kernel,
        out_shape=(wide, wide, payload(2), auxiliary(2)),
        in_specs=[SMEM] + [VMEM] * 4,
        out_specs=(VMEM,) * 4,
        compiler_params=params,
    )(mine, own, got, aux, expand)

    local_out = pl.pallas_call(
        local_kernel,
        out_shape=shape_of((rows, width), F32),
        in_specs=[VMEM] * 6,
        out_specs=VMEM,
        compiler_params=params,
        cost_estimate=cost(4 * rows * rows * width, 2 * rows * width),
    )(
        features,
        write_t,
        read_t,
        running,
        running_t,
        jnp.broadcast_to(skip_gain[:, None], (head_count, head_width)).reshape(1, width),
    )

    prefix = None
    for bit in range(1, bits - 1):
        got = swap(send, bit)
        held = (group, aux, got, expand) if prefix is None else (group, prefix, aux, got, expand)
        group, prefix, send, aux = pl.pallas_call(
            functools.partial(first_stage_kernel if prefix is None else stage_kernel, bit),
            out_shape=(wide, wide, payload(2 << bit), auxiliary(2 << bit)),
            in_specs=[SMEM] + [VMEM] * len(held),
            out_specs=(VMEM,) * 4,
            compiler_params=params,
        )(mine, *held)
    got = swap(send, bits - 1)
    keep, back, pick = pl.pallas_call(
        functools.partial(last_stage_kernel, bits - 1, rows),
        out_shape=(
            shape_of((state_size, half), BF16),
            shape_of((state_size, half), BF16),
            shape_of((starts, rows), BF16),
        ),
        in_specs=[SMEM] + [VMEM] * 5,
        out_specs=(VMEM,) * 3,
        compiler_params=params,
    )(mine, prefix, aux, got, expand, first)
    got = swap(back, 0)

    posterior, picked = pl.pallas_call(
        after_kernel,
        out_shape=(shape_of((rows, width), BF16), shape_of((starts, width), BF16)),
        in_specs=[SMEM] + [VMEM] * 7,
        out_specs=(VMEM, VMEM),
        scratch_shapes=[pltpu.VMEM((rows, width), F32), pltpu.VMEM((rows, width), F32)],
        compiler_params=params,
    )(mine, local_out, read_t, running, keep, got, post_gain[None, :], pick)
    posterior = pl.pallas_call(
        flush_kernel,
        out_shape=shape_of((rows, width), BF16),
        in_specs=[VMEM],
        out_specs=VMEM,
        compiler_params=params,
        cost_estimate=cost(0, 4 * rows * width),
    )(posterior)

    landed = lax.all_to_all(
        picked.reshape(peer_count, cap, width), "seq", split_axis=0, concat_axis=0, tiled=True
    ).reshape(starts, width)

    horizon = step_noise.shape[0]
    values, final_latent = pl.pallas_call(
        imagine_kernel,
        out_shape=(shape_of((horizon, starts), F32), shape_of((starts, width), BF16)),
        in_specs=[VMEM] * 8,
        out_specs=(VMEM, VMEM),
        compiler_params=pltpu.CompilerParams(vmem_limit_bytes=16 << 20),
    )(
        landed,
        perm,
        step_noise,
        act_weight,
        dyn_weight,
        act_in_weight,
        out_weight,
        jnp.broadcast_to(value_weight[None, :], (16, value_weight.shape[0])),
    )
    return (posterior, values, final_latent)


def solution(mesh):
    whole = P()
    by_row = P(("groups", "seq"), None)
    placed = (
        by_row,
        by_row,
        by_row,
        by_row,
        whole,
        whole,
        P(("groups", "seq")),
        P(None, ("groups", "seq"), None),
        whole,
        whole,
        whole,
        whole,
        whole,
    )
    return jax.shard_map(
        functools.partial(per_device, mesh.shape["seq"]),
        mesh=mesh,
        in_specs=placed,
        out_specs=(by_row, P(None, ("groups", "seq")), by_row),
        check_vma=False,
    )
```

```python
import functools
import jax
import jax.numpy as jnp
from jax import lax
from jax.experimental import pallas as pl
from jax.experimental.pallas import tpu as pltpu
from jax.sharding import PartitionSpec as P

F32 = jnp.float32
BF16 = jnp.bfloat16
LANES = 128
VMEM = pl.BlockSpec(memory_space=pltpu.VMEM)
SMEM = pl.BlockSpec(memory_space=pltpu.SMEM)
HBM = pl.BlockSpec(memory_space=pltpu.HBM)
ANY = pl.BlockSpec(memory_space=pl.ANY)


def iota(shape, dim):
    return lax.broadcasted_iota(jnp.int32, shape, dim)


def mask16(condition):
    return condition.astype(F32).astype(BF16)


def two_heads(cols, pair, head_width, shape):
    first = jnp.broadcast_to(cols[:, 2 * pair : 2 * pair + 1], shape)
    second = jnp.broadcast_to(cols[:, 2 * pair + 1 : 2 * pair + 2], shape)
    return jnp.where(iota(shape, 1) < head_width, first, second)


def stack_rows(rows, count):
    used = sum(row.shape[0] for row in rows)
    if used < count:
        rows = list(rows) + [jnp.zeros((count - used, LANES), F32)]
    return jnp.concatenate(rows, axis=0)


def write_meta(send_ref, decay, wanted, half, state_size):
    high = decay.astype(BF16).astype(F32)
    blocks = (send_ref.shape[1] - half) // LANES
    meta = stack_rows([high, decay - high, wanted], blocks * state_size).astype(BF16)
    for block in range(blocks):
        send_ref[:, half + block * LANES : half + (block + 1) * LANES] = meta[
            block * state_size : (block + 1) * state_size
        ]


def read_meta(got_ref, count, half, state_size):
    blocks = (got_ref.shape[1] - half) // LANES
    meta = jnp.concatenate(
        [got_ref[:, half + block * LANES : half + (block + 1) * LANES].astype(F32) for block in range(blocks)], axis=0
    )
    return meta[0:1] + meta[1:2], meta[2 : 2 + count]


def spread_rows(rows, half, head_width):
    pieces = []
    for row in rows:
        high = row.astype(BF16).astype(F32)
        pieces += [high, row - high]
    expand = mask16(iota((LANES, half), 0) == iota((LANES, half), 1) // head_width)
    wide = jnp.dot(stack_rows(pieces, 16).astype(BF16), expand, preferred_element_type=F32)
    return [wide[2 * k : 2 * k + 1] + wide[2 * k + 1 : 2 * k + 2] for k in range(len(rows))]


def requests(start_row, rows, cap):
    starts = start_row.shape[1]
    square = (starts, starts)
    index = jnp.broadcast_to(start_row.astype(F32), square)
    index_t = index.T
    owner = jnp.floor(index * (1.0 / rows))
    owner_t = jnp.floor(index_t * (1.0 / rows))
    earlier = (iota(square, 1) < iota(square, 0)) & (owner == owner_t)
    rank = jnp.sum(earlier.astype(F32), axis=1, keepdims=True)
    perm = (owner_t * cap + rank == iota(square, 1).astype(F32)).astype(F32)
    wanted = jnp.sum(perm * (index_t - owner_t * rows), axis=0, keepdims=True)
    return perm, wanted


def before_kernel(
    cap, mine_ref, x_hbm, x_other_ref, write_hbm, write_other_ref, decay_hbm, decay_other_ref, start_hbm,
    start_other_ref, send_ref, ends_ref, x_ref, write_ref, run_ref, run_t_ref, perm_ref, aux_ref,
    write_own_ref, decay_own_ref, start_own_ref, sems,
):
    core = mine_ref[0] % 2
    first = core == 0
    rows, half = x_ref.shape[0] // 2, x_ref.shape[1]
    state_size = write_ref.shape[0]
    heads = run_ref.shape[1]
    head_width = half // heads
    lanes_at = pl.multiple_of(core * half, LANES)
    rows_at = pl.multiple_of(core * rows, rows)
    others_at = pl.multiple_of((1 - core) * rows, rows)
    copies = [
        pltpu.make_async_copy(source, target, sems.at[k])
        for k, (source, target) in enumerate(
            (
                (decay_hbm, decay_own_ref),
                (write_hbm, write_own_ref),
                (x_hbm.at[:, pl.ds(lanes_at, half)], x_ref.at[pl.ds(rows_at, rows), :]),
                (start_hbm, start_own_ref),
            )
        )
    ]
    for copy in copies:
        copy.start()
    x_ref[pl.ds(others_at, rows), :] = x_other_ref[:, pl.ds(lanes_at, half)]
    upper = (iota((rows, rows), 0) <= iota((rows, rows), 1)).astype(F32)
    copies[0].wait()
    own, other = decay_own_ref[...], decay_other_ref[...]
    own = jnp.where(first, own[:heads], own[heads:])
    other = jnp.where(first, other[:heads], other[heads:])
    decays = jnp.concatenate([jnp.where(first, own, other), jnp.where(first, other, own)], axis=0)
    sums = jnp.dot(decays, upper, precision=lax.Precision.HIGHEST, preferred_element_type=F32)
    run_t = jnp.concatenate([sums[:heads], sums[heads:] + sums[:heads, rows - 1 :]], axis=1)
    run_t_ref[...] = run_t
    run = run_t.T
    run_ref[...] = run
    last = run[2 * rows - 1 :]
    tail = jnp.exp(last - run)
    copies[1].wait()
    own, other = write_own_ref[...], write_other_ref[...]
    write = jnp.concatenate([jnp.where(first, own, other), jnp.where(first, other, own)], axis=1)
    write_ref[...] = write
    copies[2].wait()
    for pair in range(heads // 2):
        lanes = slice(pair * LANES, (pair + 1) * LANES)
        scaled = x_ref[:, lanes].astype(F32) * two_heads(tail, pair, head_width, (2 * rows, LANES))
        ends = jnp.dot(write, scaled.astype(BF16), preferred_element_type=F32)
        ends_ref[:, lanes] = ends
        send_ref[:, lanes] = ends.astype(BF16)
    copies[3].wait()
    perm, wanted = requests(start_own_ref[...], rows, cap)
    perm_ref[...] = perm.astype(BF16)
    _, other_wanted = requests(start_other_ref[...], rows, cap)
    wanted = jnp.concatenate(
        [jnp.where(first, wanted, other_wanted), jnp.where(first, other_wanted, wanted)], axis=0
    )
    total = jnp.concatenate([jnp.exp(last), jnp.zeros((1, LANES - heads), F32)], axis=1)
    aux_ref[...] = stack_rows([total, jnp.ones((1, LANES), F32), wanted], aux_ref.shape[0])
    write_meta(send_ref, total, wanted, half, state_size)


def local_kernel(mine_ref, x_ref, write_ref, read_ref, read_other_ref, run_ref, run_t_ref, skip_ref, out_ref, read_out):
    first = mine_ref[0] % 2 == 0
    rows, half = x_ref.shape[0] // 2, x_ref.shape[1]
    heads = run_ref.shape[1]
    head_width = half // heads
    own, other = read_ref[...], read_other_ref[...]
    read = jnp.concatenate([jnp.where(first, own, other), jnp.where(first, other, own)], axis=1).T
    read_out[...] = read
    gram = jnp.dot(read, write_ref[...], preferred_element_type=F32)
    skip = jnp.where(first, skip_ref[:, :heads], skip_ref[:, heads:])
    mask = iota((rows, rows), 0) >= iota((rows, rows), 1)
    for chunk in range(2):
        at, count = chunk * rows, (chunk + 1) * rows
        lane = iota((count, LANES), 1)
        for pair in range(heads // 2):
            lanes = slice(pair * LANES, (pair + 1) * LANES)
            weights = []
            for head in (2 * pair, 2 * pair + 1):
                for back in range(chunk + 1):
                    seen = slice(back * rows, (back + 1) * rows)
                    spread = run_ref[at:count, head : head + 1] - run_t_ref[head : head + 1, seen]
                    if back == chunk:
                        spread = jnp.where(mask, spread, -jnp.inf)
                    weights.append((jnp.exp(spread) * gram[at:count, seen]).astype(BF16))
            x = x_ref[:count, lanes]
            zero = jnp.zeros_like(x)
            split = jnp.concatenate(
                [jnp.where(lane < head_width, x, zero), jnp.where(lane < head_width, zero, x)], axis=0
            )
            inner = jnp.dot(jnp.concatenate(weights, axis=1), split, preferred_element_type=F32)
            factor = two_heads(skip, pair, head_width, (1, LANES))
            out_ref[at:count, lanes] = inner + factor * x[at:count].astype(F32)


def stage_kernel(bit, has_prefix, head_width, mine_ref, group_ref, aux_ref, got_ref, prefix_ref, prefix_out, send_ref, aux_out, *group_out):
    state_size, half = group_ref.shape
    count = 1 << bit
    later = (mine_ref[0] >> bit) % 2 == 1
    new_decay, new_wanted = read_meta(got_ref, count, half, state_size)
    decay, prefix_decay = aux_ref[0:1], aux_ref[1:2]
    wanted = aux_ref[2 : 2 + count]
    into, across = spread_rows([prefix_decay, jnp.where(later, decay, new_decay)], half, head_width)
    group, got = group_ref[...], got_ref[:, :half].astype(F32)
    moved = into * got
    if has_prefix:
        moved = prefix_ref[...] + moved
        prefix_out[...] = jnp.where(later, moved, prefix_ref[...])
    else:
        prefix_out[...] = jnp.where(later, moved, jnp.zeros_like(moved))
    total = jnp.where(later, got, group) * across + jnp.where(later, group, got)
    for ref in group_out:
        ref[...] = total
    send_ref[:, :half] = total.astype(BF16)
    wanted = jnp.concatenate(
        [jnp.where(later, new_wanted, wanted), jnp.where(later, wanted, new_wanted)], axis=0
    )
    write_meta(send_ref, decay * new_decay, wanted, half, state_size)
    aux_out[...] = stack_rows(
        [decay * new_decay, jnp.where(later, prefix_decay * new_decay, prefix_decay), wanted], aux_out.shape[0]
    )


def last_stage_kernel(bit, rows, head_width, mine_ref, prefix_ref, aux_ref, got_ref, carry_ref, pick_ref):
    state_size, half = prefix_ref.shape
    count = 1 << bit
    mine = mine_ref[0]
    later = (mine >> bit) % 2 == 1
    _, new_wanted = read_meta(got_ref, count, half, state_size)
    (into,) = spread_rows([aux_ref[1:2]], half, head_width)
    prefix = prefix_ref[...]
    carry_ref[...] = jnp.where(later, prefix + into * got_ref[:, :half].astype(F32), prefix).astype(BF16)
    wanted = aux_ref[2 : 2 + count]
    wanted = jnp.concatenate(
        [jnp.where(later, new_wanted, wanted), jnp.where(later, wanted, new_wanted)], axis=0
    )
    peers = 2 * count
    picks = pick_ref.shape[0]
    both = picks // peers
    table = stack_rows([wanted], LANES) if peers < LANES else wanted
    asker = mask16(iota((picks, LANES), 0) // both == iota((picks, LANES), 1))
    by_slot = jnp.dot(asker, table.astype(BF16), preferred_element_type=F32)
    turn = iota((picks, LANES), 0) % both
    here = iota((picks, LANES), 1) == (mine // 2) * both + turn
    asked = jnp.sum(jnp.where(here, by_slot + ((turn // (both // 2)) * rows).astype(F32), 0.0), axis=1, keepdims=True)
    pick_ref[...] = mask16(asked == iota(pick_ref.shape, 1).astype(F32))


def after_kernel(
    mine_ref, local_ref, read_ref, run_ref, carry_ref, gain_ref, pick_ref, sent_ref, stay_ref, go_ref,
    mixed_ref, total_ref, post_ref,
):
    core = mine_ref[0] % 2
    rows, half = local_ref.shape[0] // 2, local_ref.shape[1]
    heads = run_ref.shape[1]
    head_width = half // heads
    entered = jnp.exp(run_ref[...])
    square = (LANES, LANES)
    same_head = mask16(iota(square, 0) // head_width == iota(square, 1) // head_width)
    gain = jnp.where(core == 0, gain_ref[:, :half], gain_ref[:, half:])
    blocks = [slice(k * LANES, (k + 1) * LANES) for k in range(half // LANES)]
    total_ref[...] = jnp.dot(read_ref[...], carry_ref[...], preferred_element_type=F32)
    for pair, lanes in enumerate(blocks):
        mixed_ref[:, lanes] = local_ref[:, lanes] + total_ref[:, lanes] * two_heads(
            entered, pair, head_width, (2 * rows, LANES)
        )
    for lanes in blocks:
        mixed = mixed_ref[:, lanes]
        squares = mixed * mixed
        high = squares.astype(BF16)
        low = (squares - high.astype(F32)).astype(BF16)
        total_ref[:, lanes] = jnp.dot(high, same_head, preferred_element_type=F32) + jnp.dot(
            low, same_head, preferred_element_type=F32
        )
    for lanes in blocks:
        scale = lax.rsqrt(total_ref[:, lanes] * (1.0 / head_width) + 1e-05)
        post_ref[:, lanes] = (mixed_ref[:, lanes] * scale * gain[:, lanes]).astype(BF16)
    sent_ref[...] = jnp.dot(pick_ref[...], post_ref[...], preferred_element_type=F32).astype(BF16)
    stay_ref[...] = post_ref[pl.ds(pl.multiple_of(core * rows, rows), rows), :]
    go_ref[...] = post_ref[pl.ds(pl.multiple_of((1 - core) * rows, rows), rows), :]


def fetch_kernel(token_ref, act_hbm, dyn_hbm, act_ref, dyn_ref, sems):
    copies = [
        pltpu.make_async_copy(act_hbm, act_ref, sems.at[0]),
        pltpu.make_async_copy(dyn_hbm.at[: dyn_ref.shape[0], :], dyn_ref, sems.at[1]),
    ]
    for copy in copies:
        copy.start()
    for copy in copies:
        copy.wait()


def flush_kernel(mine_ref, stay_ref, got_ref, post_ref):
    first = mine_ref[0] % 2 == 0
    half = stay_ref.shape[1]
    stay, got = stay_ref[...], got_ref[...]
    post_ref[:, :half] = jnp.where(first, stay, got)
    post_ref[:, half:] = jnp.where(first, got, stay)


def imagine_kernel(
    landed_ref, perm_ref, act_ref, head_ref, value_ref, noise_hbm, dyn_hbm, act_in_hbm, out_hbm,
    values_ref, final_ref, noise_ref, dyn_ref, act_in_ref, out_ref, sems,
):
    horizon = noise_ref.shape[0]
    starts = perm_ref.shape[0]
    half = landed_ref.shape[-1]
    depth = head_ref.shape[0]
    parts = dyn_hbm.shape[0] // depth
    wide = out_hbm.shape[0] // parts

    def dyn_part(k):
        rows = slice(k * depth, (k + 1) * depth)
        return pltpu.make_async_copy(dyn_hbm.at[rows, :], dyn_ref.at[rows, :], sems.at[k])

    def out_part(k):
        rows = slice(k * wide, (k + 1) * wide)
        return pltpu.make_async_copy(out_hbm.at[rows, :], out_ref.at[rows, :], sems.at[parts + k])

    small = [
        pltpu.make_async_copy(act_in_hbm, act_in_ref, sems.at[0]),
        pltpu.make_async_copy(noise_hbm, noise_ref, sems.at[2 * parts]),
    ]
    for k in range(1, parts):
        dyn_part(k).start()
    for copy in small:
        copy.start()
    dyn_ref[:depth, :] = head_ref[...]
    perm = perm_ref[...]
    latent = jnp.concatenate(
        [
            jnp.dot(perm, landed_ref[:, side].reshape(starts, half), preferred_element_type=F32)
            for side in range(2)
        ],
        axis=1,
    )
    rows = []
    for step in range(horizon):
        scale = lax.rsqrt(jnp.mean(latent * latent, axis=1, keepdims=True) + 1e-06)
        normed = (latent * scale).astype(BF16)
        action = jnp.tanh(jnp.dot(normed, act_ref[...], preferred_element_type=F32)).astype(BF16)
        if step == 0:
            inner = jnp.dot(normed[:, :depth], head_ref[...], preferred_element_type=F32)
            for k in range(1, parts):
                dyn_part(k).wait()
                if k == parts - 1:
                    for part in range(parts):
                        out_part(part).start()
                columns = slice(k * depth, (k + 1) * depth)
                inner = inner + jnp.dot(normed[:, columns], dyn_ref[columns, :], preferred_element_type=F32)
            for copy in small:
                copy.wait()
        else:
            inner = jnp.dot(normed, dyn_ref[...], preferred_element_type=F32)
        inner = inner + jnp.dot(action, act_in_ref[...], preferred_element_type=F32)
        hidden = (inner / (1.0 + jnp.exp(-inner)) + noise_ref[step].astype(F32)).astype(BF16)
        value = lax.dot_general(
            value_ref[...], hidden, (((1,), (1,)), ((), ())), preferred_element_type=F32
        )
        rows.append(value[0:1, :])
        if step == 0:
            moved = latent
            for k in range(parts):
                out_part(k).wait()
                columns = slice(k * wide, (k + 1) * wide)
                moved = moved + jnp.dot(hidden[:, columns], out_ref[columns, :], preferred_element_type=F32)
        else:
            moved = latent + jnp.dot(hidden, out_ref[...], preferred_element_type=F32)
        latent = moved.astype(BF16).astype(F32)
    final_ref[...] = latent.astype(BF16)
    values_ref[...] = jnp.concatenate(rows, axis=0)


def cost(flops, read):
    return pl.CostEstimate(flops=flops, bytes_accessed=read, transcendentals=0)


def in_hbm(array):
    return pltpu.with_memory_space_constraint(array, pltpu.HBM)


def per_device(
    peer_count,
    features,
    state_write,
    state_read,
    log_decay,
    skip_gain,
    post_gain,
    start_index,
    step_noise,
    act_weight,
    dyn_weight,
    act_in_weight,
    out_weight,
    value_weight,
):
    rows, width = features.shape
    head_count = log_decay.shape[1]
    head_width = width // head_count
    state_size = state_write.shape[1]
    half = width // 2
    heads = head_count // 2
    starts = start_index.shape[0]
    cap = starts // peer_count
    bits = peer_count.bit_length() - 1
    mine = lax.axis_index("seq").reshape(1)
    params = pltpu.CompilerParams(vmem_limit_bytes=12 << 20)
    held = pltpu.VMEM

    def swap(array, bit):
        return lax.ppermute(array, "seq", [(i, i ^ (1 << bit)) for i in range(peer_count)])

    def payload(count):
        blocks = -(-(2 + count) // state_size)
        return held((state_size, half + blocks * LANES), BF16)

    def auxiliary(count):
        return held((-(-(2 + count) // 8) * 8, LANES), F32)

    write_t, read_t, decay_t = state_write.T, state_read.T, log_decay.T
    start_row = start_index.reshape(1, starts)
    x_other = swap(features, 0)
    decay_other, write_other = swap(decay_t, 0), swap(write_t, 0)
    start_other, read_other = swap(start_row, 0), swap(read_t, 0)

    send, group, chip_x, write, run, run_t, perm, aux = pl.pallas_call(
        functools.partial(before_kernel, cap),
        out_shape=(
            payload(2),
            held((state_size, half), F32),
            held((2 * rows, half), BF16),
            held((state_size, 2 * rows), BF16),
            held((2 * rows, heads), F32),
            held((heads, 2 * rows), F32),
            held((starts, starts), BF16),
            auxiliary(2),
        ),
        in_specs=[SMEM, HBM, VMEM, HBM, VMEM, HBM, VMEM, HBM, VMEM],
        out_specs=(VMEM,) * 8,
        scratch_shapes=[
            pltpu.VMEM((state_size, rows), BF16),
            pltpu.VMEM((head_count, rows), F32),
            pltpu.VMEM((1, starts), jnp.int32),
            pltpu.SemaphoreType.DMA((4,)),
        ],
        compiler_params=params,
    )(
        mine,
        in_hbm(features),
        x_other,
        in_hbm(write_t),
        write_other,
        in_hbm(decay_t),
        decay_other,
        in_hbm(start_row),
        start_other,
    )

    local_out, read = pl.pallas_call(
        local_kernel,
        out_shape=(held((2 * rows, half), F32), held((2 * rows, state_size), BF16)),
        in_specs=[SMEM] + [VMEM] * 7,
        out_specs=(VMEM, VMEM),
        compiler_params=params,
        cost_estimate=cost(8 * rows * rows * width, 4 * rows * width),
    )(mine, chip_x, write, read_t, read_other, run, run_t, skip_gain[None, :])

    prefix, group = local_out, [group]
    for bit in range(1, bits - 1):
        got = swap(send, bit)
        goes_on = int(bit < bits - 2)
        prefix, send, aux, *group = pl.pallas_call(
            functools.partial(stage_kernel, bit, bit > 1, head_width),
            out_shape=(
                held((state_size, half), F32),
                payload(2 << bit),
                auxiliary(2 << bit),
            )
            + (held((state_size, half), F32),) * goes_on,
            in_specs=[SMEM] + [VMEM] * 3 + [VMEM if bit > 1 else ANY],
            out_specs=(VMEM,) * (3 + goes_on),
            compiler_params=params,
        )(mine, *group, aux, got, prefix)
    got = swap(send, bits - 1)
    carry, pick = pl.pallas_call(
        functools.partial(last_stage_kernel, bits - 1, rows, head_width),
        out_shape=(held((state_size, half), BF16), held((2 * starts, 2 * rows), BF16)),
        in_specs=[SMEM] + [VMEM] * 3,
        out_specs=(VMEM,) * 2,
        compiler_params=params,
    )(mine, prefix, aux, got)

    picked, stay, go = pl.pallas_call(
        after_kernel,
        out_shape=(
            held((2 * starts, half), BF16),
            held((rows, half), BF16),
            held((rows, half), BF16),
        ),
        in_specs=[SMEM] + [VMEM] * 6,
        out_specs=(VMEM,) * 3,
        scratch_shapes=[
            pltpu.VMEM((2 * rows, half), F32),
            pltpu.VMEM((2 * rows, half), F32),
            pltpu.VMEM((2 * rows, half), BF16),
        ],
        compiler_params=params,
    )(mine, local_out, read, run, carry, post_gain[None, :], pick)

    landed = lax.all_to_all(
        picked.reshape(peer_count, 2 * cap, half), "seq", split_axis=0, concat_axis=0, tiled=True
    ).reshape(peer_count // 2, 2, 2 * cap, half)

    head_rows = width // 8
    act, dyn_head = pl.pallas_call(
        fetch_kernel,
        out_shape=(held(act_weight.shape, BF16), held((head_rows, dyn_weight.shape[1]), BF16)),
        in_specs=[ANY, HBM, HBM],
        out_specs=(VMEM, VMEM),
        scratch_shapes=[pltpu.SemaphoreType.DMA((2,))],
        compiler_params=params,
        cost_estimate=cost(0, 4 * (act_weight.size + head_rows * dyn_weight.shape[1])),
    )(picked, in_hbm(act_weight), in_hbm(dyn_weight))

    posterior = pl.pallas_call(
        flush_kernel,
        out_shape=jax.ShapeDtypeStruct((rows, width), BF16),
        in_specs=[SMEM, VMEM, VMEM],
        out_specs=VMEM,
        compiler_params=params,
        cost_estimate=cost(0, 4 * rows * width),
    )(mine, stay, swap(go, 0))

    horizon = step_noise.shape[0]
    values, final_latent = pl.pallas_call(
        imagine_kernel,
        out_shape=(
            jax.ShapeDtypeStruct((horizon, starts), F32),
            jax.ShapeDtypeStruct((starts, width), BF16),
        ),
        in_specs=[VMEM] * 5 + [HBM] * 4,
        out_specs=(VMEM, VMEM),
        scratch_shapes=[
            pltpu.VMEM(step_noise.shape, BF16),
            pltpu.VMEM(dyn_weight.shape, BF16),
            pltpu.VMEM(act_in_weight.shape, BF16),
            pltpu.VMEM(out_weight.shape, BF16),
            pltpu.SemaphoreType.DMA((17,)),
        ],
        compiler_params=pltpu.CompilerParams(vmem_limit_bytes=40 << 20),
    )(
        landed,
        perm,
        act,
        dyn_head,
        jnp.broadcast_to(value_weight[None, :], (16, value_weight.shape[0])),
        *(in_hbm(array) for array in (step_noise, dyn_weight, act_in_weight, out_weight)),
    )
    return (posterior, values, final_latent)


def solution(mesh):
    whole = P()
    by_row = P(("groups", "seq"), None)
    placed = (
        by_row,
        by_row,
        by_row,
        by_row,
        whole,
        whole,
        P(("groups", "seq")),
        P(None, ("groups", "seq"), None),
        whole,
        whole,
        whole,
        whole,
        whole,
    )
    return jax.shard_map(
        functools.partial(per_device, mesh.shape["seq"]),
        mesh=mesh,
        in_specs=placed,
        out_specs=(by_row, P(None, ("groups", "seq")), by_row),
        check_vma=False,
    )
```

```python
import functools
import jax
import jax.numpy as jnp
from jax import lax
from jax.experimental import pallas as pl
from jax.experimental.pallas import tpu as pltpu
from jax.sharding import PartitionSpec as P

F32 = jnp.float32
BF16 = jnp.bfloat16
LANES = 128
VMEM = pl.BlockSpec(memory_space=pltpu.VMEM)
SMEM = pl.BlockSpec(memory_space=pltpu.SMEM)
HBM = pl.BlockSpec(memory_space=pltpu.HBM)
ANY = pl.BlockSpec(memory_space=pl.ANY)


def iota(shape, dim):
    return lax.broadcasted_iota(jnp.int32, shape, dim)


def mask16(condition):
    return condition.astype(F32).astype(BF16)


def two_heads(cols, pair, head_width, shape):
    first = jnp.broadcast_to(cols[:, 2 * pair : 2 * pair + 1], shape)
    second = jnp.broadcast_to(cols[:, 2 * pair + 1 : 2 * pair + 2], shape)
    return jnp.where(iota(shape, 1) < head_width, first, second)


def stack_rows(rows, count):
    used = sum(row.shape[0] for row in rows)
    if used < count:
        rows = list(rows) + [jnp.zeros((count - used, LANES), F32)]
    return jnp.concatenate(rows, axis=0)


def write_meta(send_ref, decay, wanted, half, state_size):
    high = decay.astype(BF16).astype(F32)
    blocks = (send_ref.shape[1] - half) // LANES
    meta = stack_rows([high, decay - high, wanted], blocks * state_size).astype(BF16)
    for block in range(blocks):
        send_ref[:, half + block * LANES : half + (block + 1) * LANES] = meta[
            block * state_size : (block + 1) * state_size
        ]


def read_meta(got_ref, count, half, state_size):
    blocks = (got_ref.shape[1] - half) // LANES
    meta = jnp.concatenate(
        [got_ref[:, half + block * LANES : half + (block + 1) * LANES].astype(F32) for block in range(blocks)], axis=0
    )
    return meta[0:1] + meta[1:2], meta[2 : 2 + count]


def spread_rows(rows, half, head_width):
    pieces = []
    for row in rows:
        high = row.astype(BF16).astype(F32)
        pieces += [high, row - high]
    expand = mask16(iota((LANES, half), 0) == iota((LANES, half), 1) // head_width)
    wide = jnp.dot(stack_rows(pieces, 16).astype(BF16), expand, preferred_element_type=F32)
    return [wide[2 * k : 2 * k + 1] + wide[2 * k + 1 : 2 * k + 2] for k in range(len(rows))]


def requests(start_row, rows, cap):
    starts = start_row.shape[1]
    square = (starts, starts)
    index = jnp.broadcast_to(start_row.astype(F32), square)
    index_t = index.T
    owner = jnp.floor(index * (1.0 / rows))
    owner_t = jnp.floor(index_t * (1.0 / rows))
    earlier = (iota(square, 1) < iota(square, 0)) & (owner == owner_t)
    rank = jnp.sum(earlier.astype(F32), axis=1, keepdims=True)
    perm = (owner_t * cap + rank == iota(square, 1).astype(F32)).astype(F32)
    wanted = jnp.sum(perm * (index_t - owner_t * rows), axis=0, keepdims=True)
    return perm, wanted


def own_kernel(
    cap, mine_ref, x_hbm, write_hbm, decay_hbm, start_hbm, x_ref, write_ref, sums_ref, perm_ref, wanted_ref,
    decay_ref, start_ref, sems,
):
    core = mine_ref[0] % 2
    rows, half = x_ref.shape
    heads = sums_ref.shape[0]
    lanes_at = pl.multiple_of(core * half, LANES)
    copies = [
        pltpu.make_async_copy(source, target, sems.at[k])
        for k, (source, target) in enumerate(
            (
                (start_hbm, start_ref),
                (decay_hbm, decay_ref),
                (write_hbm, write_ref),
                (x_hbm.at[:, pl.ds(lanes_at, half)], x_ref),
            )
        )
    ]
    for copy in copies:
        copy.start()
    copies[0].wait()
    perm, wanted = requests(start_ref[...], rows, cap)
    perm_ref[...] = perm.astype(BF16)
    wanted_ref[...] = wanted
    copies[1].wait()
    sums_ref[...] = running_sums(jnp.where(core == 0, decay_ref[:heads], decay_ref[heads:]))
    copies[2].wait()
    copies[3].wait()


def running_sums(decays):
    rows = decays.shape[1]
    upper = (iota((rows, rows), 0) <= iota((rows, rows), 1)).astype(F32)
    return jnp.dot(decays, upper, precision=lax.Precision.HIGHEST, preferred_element_type=F32)


def before_kernel(
    cap, mine_ref, x_own_ref, x_other_ref, write_own_ref, write_other_ref, sums_ref, decay_other_ref, wanted_ref,
    start_other_ref, send_ref, ends_ref, x_ref, write_ref, run_ref, run_t_ref, aux_ref,
):
    core = mine_ref[0] % 2
    first = core == 0
    rows, half = x_own_ref.shape
    state_size = write_ref.shape[0]
    heads = run_ref.shape[1]
    head_width = half // heads
    own, other = x_own_ref[...], x_other_ref[:, pl.ds(pl.multiple_of(core * half, LANES), half)]
    x_ref[:rows, :] = jnp.where(first, own, other)
    x_ref[rows:, :] = jnp.where(first, other, own)
    own = sums_ref[...]
    other = running_sums(jnp.where(first, decay_other_ref[:heads], decay_other_ref[heads:]))
    one, two = jnp.where(first, own, other), jnp.where(first, other, own)
    run_t = jnp.concatenate([one, two + one[:, rows - 1 :]], axis=1)
    run_t_ref[...] = run_t
    run = run_t.T
    run_ref[...] = run
    last = run[2 * rows - 1 :]
    tail = jnp.exp(last - run)
    own, other = write_own_ref[...], write_other_ref[...]
    write = jnp.concatenate([jnp.where(first, own, other), jnp.where(first, other, own)], axis=1)
    write_ref[...] = write
    for pair in range(heads // 2):
        lanes = slice(pair * LANES, (pair + 1) * LANES)
        scaled = x_ref[:, lanes].astype(F32) * two_heads(tail, pair, head_width, (2 * rows, LANES))
        ends = jnp.dot(write, scaled.astype(BF16), preferred_element_type=F32)
        ends_ref[:, lanes] = ends
        send_ref[:, lanes] = ends.astype(BF16)
    _, other = requests(start_other_ref[...], rows, cap)
    own = wanted_ref[...]
    wanted = jnp.concatenate([jnp.where(first, own, other), jnp.where(first, other, own)], axis=0)
    total = jnp.concatenate([jnp.exp(last), jnp.zeros((1, LANES - heads), F32)], axis=1)
    aux_ref[...] = stack_rows([total, jnp.ones((1, LANES), F32), wanted], aux_ref.shape[0])
    write_meta(send_ref, total, wanted, half, state_size)


def local_kernel(
    mine_ref, x_ref, write_ref, read_hbm, read_other_ref, run_ref, run_t_ref, skip_hbm, out_ref, read_out,
    read_ref, skip_ref, sems,
):
    copies = [
        pltpu.make_async_copy(read_hbm, read_ref, sems.at[0]),
        pltpu.make_async_copy(skip_hbm, skip_ref, sems.at[1]),
    ]
    for copy in copies:
        copy.start()
    for copy in copies:
        copy.wait()
    first = mine_ref[0] % 2 == 0
    rows, half = x_ref.shape[0] // 2, x_ref.shape[1]
    heads = run_ref.shape[1]
    head_width = half // heads
    own, other = read_ref[...], read_other_ref[...]
    read = jnp.concatenate([jnp.where(first, own, other), jnp.where(first, other, own)], axis=1).T
    read_out[...] = read
    gram = jnp.dot(read, write_ref[...], preferred_element_type=F32)
    skip = jnp.where(first, skip_ref[:, :heads], skip_ref[:, heads:])
    mask = iota((rows, rows), 0) >= iota((rows, rows), 1)
    for chunk in range(2):
        at, count = chunk * rows, (chunk + 1) * rows
        lane = iota((count, LANES), 1)
        for pair in range(heads // 2):
            lanes = slice(pair * LANES, (pair + 1) * LANES)
            weights = []
            for head in (2 * pair, 2 * pair + 1):
                for back in range(chunk + 1):
                    seen = slice(back * rows, (back + 1) * rows)
                    spread = run_ref[at:count, head : head + 1] - run_t_ref[head : head + 1, seen]
                    if back == chunk:
                        spread = jnp.where(mask, spread, -jnp.inf)
                    weights.append((jnp.exp(spread) * gram[at:count, seen]).astype(BF16))
            x = x_ref[:count, lanes]
            zero = jnp.zeros_like(x)
            split = jnp.concatenate(
                [jnp.where(lane < head_width, x, zero), jnp.where(lane < head_width, zero, x)], axis=0
            )
            inner = jnp.dot(jnp.concatenate(weights, axis=1), split, preferred_element_type=F32)
            factor = two_heads(skip, pair, head_width, (1, LANES))
            out_ref[at:count, lanes] = inner + factor * x[at:count].astype(F32)


def stage_kernel(bit, has_prefix, head_width, mine_ref, group_ref, aux_ref, got_ref, prefix_ref, prefix_out, send_ref, aux_out, *group_out):
    state_size, half = group_ref.shape
    count = 1 << bit
    later = (mine_ref[0] >> bit) % 2 == 1
    new_decay, new_wanted = read_meta(got_ref, count, half, state_size)
    decay, prefix_decay = aux_ref[0:1], aux_ref[1:2]
    wanted = aux_ref[2 : 2 + count]
    into, across = spread_rows([prefix_decay, jnp.where(later, decay, new_decay)], half, head_width)
    group, got = group_ref[...], got_ref[:, :half].astype(F32)
    moved = into * got
    if has_prefix:
        moved = prefix_ref[...] + moved
        prefix_out[...] = jnp.where(later, moved, prefix_ref[...])
    else:
        prefix_out[...] = jnp.where(later, moved, jnp.zeros_like(moved))
    total = jnp.where(later, got, group) * across + jnp.where(later, group, got)
    for ref in group_out:
        ref[...] = total
    send_ref[:, :half] = total.astype(BF16)
    wanted = jnp.concatenate(
        [jnp.where(later, new_wanted, wanted), jnp.where(later, wanted, new_wanted)], axis=0
    )
    write_meta(send_ref, decay * new_decay, wanted, half, state_size)
    aux_out[...] = stack_rows(
        [decay * new_decay, jnp.where(later, prefix_decay * new_decay, prefix_decay), wanted], aux_out.shape[0]
    )


def last_stage_kernel(bit, rows, head_width, mine_ref, prefix_ref, aux_ref, got_ref, token_ref, carry_ref, pick_ref):
    state_size, half = prefix_ref.shape
    count = 1 << bit
    mine = mine_ref[0]
    later = (mine >> bit) % 2 == 1
    _, new_wanted = read_meta(got_ref, count, half, state_size)
    (into,) = spread_rows([aux_ref[1:2]], half, head_width)
    prefix = prefix_ref[...]
    carry_ref[...] = jnp.where(later, prefix + into * got_ref[:, :half].astype(F32), prefix).astype(BF16)
    wanted = aux_ref[2 : 2 + count]
    wanted = jnp.concatenate(
        [jnp.where(later, new_wanted, wanted), jnp.where(later, wanted, new_wanted)], axis=0
    )
    peers = 2 * count
    picks = pick_ref.shape[0]
    both = picks // peers
    table = stack_rows([wanted], LANES) if peers < LANES else wanted
    asker = mask16(iota((picks, LANES), 0) // both == iota((picks, LANES), 1))
    by_slot = jnp.dot(asker, table.astype(BF16), preferred_element_type=F32)
    turn = iota((picks, LANES), 0) % both
    here = iota((picks, LANES), 1) == (mine // 2) * both + turn
    asked = jnp.sum(jnp.where(here, by_slot + ((turn // (both // 2)) * rows).astype(F32), 0.0), axis=1, keepdims=True)
    pick_ref[...] = mask16(asked == iota(pick_ref.shape, 1).astype(F32))


def after_kernel(
    mine_ref, local_ref, read_ref, run_ref, carry_ref, gain_ref, pick_ref, sent_ref, stay_ref, go_ref,
    mixed_ref, total_ref, post_ref,
):
    core = mine_ref[0] % 2
    rows, half = local_ref.shape[0] // 2, local_ref.shape[1]
    heads = run_ref.shape[1]
    head_width = half // heads
    entered = jnp.exp(run_ref[...])
    square = (LANES, LANES)
    same_head = mask16(iota(square, 0) // head_width == iota(square, 1) // head_width)
    gain = jnp.where(core == 0, gain_ref[:, :half], gain_ref[:, half:])
    blocks = [slice(k * LANES, (k + 1) * LANES) for k in range(half // LANES)]
    total_ref[...] = jnp.dot(read_ref[...], carry_ref[...], preferred_element_type=F32)
    for pair, lanes in enumerate(blocks):
        mixed_ref[:, lanes] = local_ref[:, lanes] + total_ref[:, lanes] * two_heads(
            entered, pair, head_width, (2 * rows, LANES)
        )
    for lanes in blocks:
        mixed = mixed_ref[:, lanes]
        squares = mixed * mixed
        high = squares.astype(BF16)
        low = (squares - high.astype(F32)).astype(BF16)
        total_ref[:, lanes] = jnp.dot(high, same_head, preferred_element_type=F32) + jnp.dot(
            low, same_head, preferred_element_type=F32
        )
    for lanes in blocks:
        scale = lax.rsqrt(total_ref[:, lanes] * (1.0 / head_width) + 1e-05)
        post_ref[:, lanes] = (mixed_ref[:, lanes] * scale * gain[:, lanes]).astype(BF16)
    sent_ref[...] = jnp.dot(pick_ref[...], post_ref[...], preferred_element_type=F32).astype(BF16)
    stay_ref[...] = post_ref[pl.ds(pl.multiple_of(core * rows, rows), rows), :]
    go_ref[...] = post_ref[pl.ds(pl.multiple_of((1 - core) * rows, rows), rows), :]


def fetch_kernel(token_ref, *refs):
    count = (len(refs) - 1) // 2
    sems = refs[-1]
    copies = [pltpu.make_async_copy(refs[k], refs[count + k], sems.at[k]) for k in range(count)]
    for copy in copies:
        copy.start()
    for copy in copies:
        copy.wait()


def imagined_steps(latent, noise_ref, act_ref, dyn_ref, act_in_ref, out_ref, value_ref, steps):
    rows = []
    for step in steps:
        scale = lax.rsqrt(jnp.mean(latent * latent, axis=1, keepdims=True) + 1e-06)
        normed = (latent * scale).astype(BF16)
        action = jnp.tanh(jnp.dot(normed, act_ref[...], preferred_element_type=F32)).astype(BF16)
        inner = jnp.dot(normed, dyn_ref[...], preferred_element_type=F32) + jnp.dot(
            action, act_in_ref[...], preferred_element_type=F32
        )
        hidden = (inner / (1.0 + jnp.exp(-inner)) + noise_ref[step].astype(F32)).astype(BF16)
        value = lax.dot_general(
            value_ref[...], hidden, (((1,), (1,)), ((), ())), preferred_element_type=F32
        )
        rows.append(value[0:1, :])
        moved = latent + jnp.dot(hidden, out_ref[...], preferred_element_type=F32)
        latent = moved.astype(BF16).astype(F32)
    return latent, rows


def first_step_kernel(landed_ref, perm_ref, noise_ref, act_ref, dyn_ref, act_in_ref, out_ref, value_ref, latent_ref, row_ref):
    starts = perm_ref.shape[0]
    half = landed_ref.shape[-1]
    perm = perm_ref[...]
    latent = jnp.concatenate(
        [
            jnp.dot(perm, landed_ref[:, side].reshape(starts, half), preferred_element_type=F32)
            for side in range(2)
        ],
        axis=1,
    )
    latent, rows = imagined_steps(
        latent, noise_ref, act_ref, dyn_ref, act_in_ref, out_ref, value_ref, range(1)
    )
    latent_ref[...] = latent.astype(BF16)
    row_ref[...] = rows[0]


def later_steps_kernel(
    mine_ref, stay_ref, got_ref, latent_ref, row_ref, noise_ref, act_ref, dyn_ref, act_in_ref, out_ref, value_ref,
    post_hbm, values_ref, final_ref, sems,
):
    core = mine_ref[0] % 2
    half = stay_ref.shape[1]
    copies = [
        pltpu.make_async_copy(source, post_hbm.at[:, pl.ds(pl.multiple_of(side * half, LANES), half)], sems.at[k])
        for k, (source, side) in enumerate(((stay_ref, core), (got_ref, 1 - core)))
    ]
    for copy in copies:
        copy.start()
    latent, rows = imagined_steps(
        latent_ref[...].astype(F32),
        noise_ref,
        act_ref,
        dyn_ref,
        act_in_ref,
        out_ref,
        value_ref,
        range(1, noise_ref.shape[0]),
    )
    final_ref[...] = latent.astype(BF16)
    values_ref[...] = jnp.concatenate([row_ref[...]] + rows, axis=0)
    for copy in copies:
        copy.wait()


def cost(flops, read):
    return pl.CostEstimate(flops=flops, bytes_accessed=read, transcendentals=0)


def in_hbm(array):
    return pltpu.with_memory_space_constraint(array, pltpu.HBM)


def per_device(
    peer_count,
    features,
    state_write,
    state_read,
    log_decay,
    skip_gain,
    post_gain,
    start_index,
    step_noise,
    act_weight,
    dyn_weight,
    act_in_weight,
    out_weight,
    value_weight,
):
    rows, width = features.shape
    head_count = log_decay.shape[1]
    head_width = width // head_count
    state_size = state_write.shape[1]
    half = width // 2
    heads = head_count // 2
    starts = start_index.shape[0]
    cap = starts // peer_count
    bits = peer_count.bit_length() - 1
    mine = lax.axis_index("seq").reshape(1)
    params = pltpu.CompilerParams(vmem_limit_bytes=12 << 20)
    held = pltpu.VMEM

    def swap(array, bit):
        return lax.ppermute(array, "seq", [(i, i ^ (1 << bit)) for i in range(peer_count)])

    def payload(count):
        blocks = -(-(2 + count) // state_size)
        return held((state_size, half + blocks * LANES), BF16)

    def auxiliary(count):
        return held((-(-(2 + count) // 8) * 8, LANES), F32)

    write_t, read_t, decay_t = state_write.T, state_read.T, log_decay.T
    start_row = start_index.reshape(1, starts)
    x_other = swap(features, 0)
    decay_other, write_other = swap(decay_t, 0), swap(write_t, 0)
    start_other, read_other = swap(start_row, 0), swap(read_t, 0)

    x_own, write_own, sums, perm, wanted = pl.pallas_call(
        functools.partial(own_kernel, cap),
        out_shape=(
            held((rows, half), BF16),
            held((state_size, rows), BF16),
            held((heads, rows), F32),
            held((starts, starts), BF16),
            held((1, starts), F32),
        ),
        in_specs=[SMEM] + [HBM] * 4,
        out_specs=(VMEM,) * 5,
        scratch_shapes=[
            pltpu.VMEM((head_count, rows), F32),
            pltpu.VMEM((1, starts), jnp.int32),
            pltpu.SemaphoreType.DMA((4,)),
        ],
        compiler_params=params,
        cost_estimate=cost(0, 4 * rows * width),
    )(mine, in_hbm(features), in_hbm(write_t), in_hbm(decay_t), in_hbm(start_row))

    send, group, chip_x, write, run, run_t, aux = pl.pallas_call(
        functools.partial(before_kernel, cap),
        out_shape=(
            payload(2),
            held((state_size, half), F32),
            held((2 * rows, half), BF16),
            held((state_size, 2 * rows), BF16),
            held((2 * rows, heads), F32),
            held((heads, 2 * rows), F32),
            auxiliary(2),
        ),
        in_specs=[SMEM] + [VMEM] * 8,
        out_specs=(VMEM,) * 7,
        compiler_params=params,
    )(mine, x_own, x_other, write_own, write_other, sums, decay_other, wanted, start_other)

    local_out, read = pl.pallas_call(
        local_kernel,
        out_shape=(held((2 * rows, half), F32), held((2 * rows, state_size), BF16)),
        in_specs=[SMEM, VMEM, VMEM, HBM, VMEM, VMEM, VMEM, HBM],
        out_specs=(VMEM, VMEM),
        scratch_shapes=[
            pltpu.VMEM((state_size, rows), BF16),
            pltpu.VMEM((1, head_count), F32),
            pltpu.SemaphoreType.DMA((2,)),
        ],
        compiler_params=params,
        cost_estimate=cost(8 * rows * rows * width, 4 * rows * width),
    )(mine, chip_x, write, in_hbm(read_t), read_other, run, run_t, in_hbm(skip_gain[None, :]))

    def fetch(token, *weights):
        return pl.pallas_call(
            fetch_kernel,
            out_shape=tuple(held(weight.shape, weight.dtype) for weight in weights),
            in_specs=[ANY] + [HBM] * len(weights),
            out_specs=(VMEM,) * len(weights),
            scratch_shapes=[pltpu.SemaphoreType.DMA((len(weights),))],
            compiler_params=params,
            cost_estimate=cost(0, 2 * sum(weight.size * 2 for weight in weights)),
        )(token, *(in_hbm(weight) for weight in weights))

    prefix, group = local_out, [group]
    for bit in range(1, bits - 1):
        got = swap(send, bit)
        if bit == 2:
            (dyn,) = fetch(aux, dyn_weight)
            aux, _ = lax.optimization_barrier((aux, dyn))
        goes_on = int(bit < bits - 2)
        prefix, send, aux, *group = pl.pallas_call(
            functools.partial(stage_kernel, bit, bit > 1, head_width),
            out_shape=(
                held((state_size, half), F32),
                payload(2 << bit),
                auxiliary(2 << bit),
            )
            + (held((state_size, half), F32),) * goes_on,
            in_specs=[SMEM] + [VMEM] * 3 + [VMEM if bit > 1 else ANY],
            out_specs=(VMEM,) * (3 + goes_on),
            compiler_params=params,
        )(mine, *group, aux, got, prefix)
    got = swap(send, bits - 1)
    out, act, act_in, noise = fetch(aux, out_weight, act_weight, act_in_weight, step_noise)
    carry, pick = pl.pallas_call(
        functools.partial(last_stage_kernel, bits - 1, rows, head_width),
        out_shape=(held((state_size, half), BF16), held((2 * starts, 2 * rows), BF16)),
        in_specs=[SMEM] + [VMEM] * 3 + [ANY],
        out_specs=(VMEM,) * 2,
        compiler_params=params,
    )(mine, prefix, aux, got, act_in)

    picked, stay, go = pl.pallas_call(
        after_kernel,
        out_shape=(
            held((2 * starts, half), BF16),
            held((rows, half), BF16),
            held((rows, half), BF16),
        ),
        in_specs=[SMEM] + [VMEM] * 6,
        out_specs=(VMEM,) * 3,
        scratch_shapes=[
            pltpu.VMEM((2 * rows, half), F32),
            pltpu.VMEM((2 * rows, half), F32),
            pltpu.VMEM((2 * rows, half), BF16),
        ],
        compiler_params=params,
    )(mine, local_out, read, run, carry, post_gain[None, :], pick)

    landed = lax.all_to_all(
        picked.reshape(peer_count, 2 * cap, half), "seq", split_axis=0, concat_axis=0, tiled=True
    ).reshape(peer_count // 2, 2, 2 * cap, half)

    value_rows = jnp.broadcast_to(value_weight[None, :], (16, value_weight.shape[0]))
    go, landed = lax.optimization_barrier((go, landed))
    got = swap(go, 0)
    horizon = step_noise.shape[0]
    big = pltpu.CompilerParams(vmem_limit_bytes=16 << 20)
    latent, row = pl.pallas_call(
        first_step_kernel,
        out_shape=(held((starts, width), BF16), held((1, starts), F32)),
        in_specs=[VMEM] * 8,
        out_specs=(VMEM, VMEM),
        compiler_params=big,
        cost_estimate=cost(2 * starts * 2 * dyn_weight.size, 4 * dyn_weight.size),
    )(landed, perm, noise, act, dyn, act_in, out, value_rows)
    posterior, values, final_latent = pl.pallas_call(
        later_steps_kernel,
        out_shape=(
            jax.ShapeDtypeStruct((rows, width), BF16),
            jax.ShapeDtypeStruct((horizon, starts), F32),
            jax.ShapeDtypeStruct((starts, width), BF16),
        ),
        in_specs=[SMEM] + [VMEM] * 10,
        out_specs=(HBM, VMEM, VMEM),
        scratch_shapes=[pltpu.SemaphoreType.DMA((2,))],
        compiler_params=big,
    )(mine, stay, got, latent, row, noise, act, dyn, act_in, out, value_rows)
    return (posterior, values, final_latent)


def solution(mesh):
    whole = P()
    by_row = P(("groups", "seq"), None)
    placed = (
        by_row,
        by_row,
        by_row,
        by_row,
        whole,
        whole,
        P(("groups", "seq")),
        P(None, ("groups", "seq"), None),
        whole,
        whole,
        whole,
        whole,
        whole,
    )
    return jax.shard_map(
        functools.partial(per_device, mesh.shape["seq"]),
        mesh=mesh,
        in_specs=placed,
        out_specs=(by_row, P(None, ("groups", "seq")), by_row),
        check_vma=False,
    )
```

```python
import functools
import jax
import jax.numpy as jnp
from jax import lax
from jax.experimental import pallas as pl
from jax.experimental.pallas import tpu as pltpu
from jax.sharding import PartitionSpec as P

F32 = jnp.float32
BF16 = jnp.bfloat16
LANES = 128
VMEM = pl.BlockSpec(memory_space=pltpu.VMEM)
SMEM = pl.BlockSpec(memory_space=pltpu.SMEM)
HBM = pl.BlockSpec(memory_space=pltpu.HBM)
ANY = pl.BlockSpec(memory_space=pl.ANY)


def iota(shape, dim):
    return lax.broadcasted_iota(jnp.int32, shape, dim)


def mask16(condition):
    return condition.astype(F32).astype(BF16)


def two_heads(cols, pair, head_width, shape):
    first = jnp.broadcast_to(cols[:, 2 * pair : 2 * pair + 1], shape)
    second = jnp.broadcast_to(cols[:, 2 * pair + 1 : 2 * pair + 2], shape)
    return jnp.where(iota(shape, 1) < head_width, first, second)


def stack_rows(rows, count):
    used = sum(row.shape[0] for row in rows)
    if used < count:
        rows = list(rows) + [jnp.zeros((count - used, LANES), F32)]
    return jnp.concatenate(rows, axis=0)


def write_meta(send_ref, decay, wanted, half, state_size):
    high = decay.astype(BF16).astype(F32)
    blocks = (send_ref.shape[1] - half) // LANES
    meta = stack_rows([high, decay - high, wanted], blocks * state_size).astype(BF16)
    for block in range(blocks):
        send_ref[:, half + block * LANES : half + (block + 1) * LANES] = meta[
            block * state_size : (block + 1) * state_size
        ]


def read_meta(got_ref, count, half, state_size):
    blocks = (got_ref.shape[1] - half) // LANES
    meta = jnp.concatenate(
        [got_ref[:, half + block * LANES : half + (block + 1) * LANES].astype(F32) for block in range(blocks)], axis=0
    )
    return meta[0:1] + meta[1:2], meta[2 : 2 + count]


def spread_rows(rows, half, head_width):
    pieces = []
    for row in rows:
        high = row.astype(BF16).astype(F32)
        pieces += [high, row - high]
    expand = mask16(iota((LANES, half), 0) == iota((LANES, half), 1) // head_width)
    wide = jnp.dot(stack_rows(pieces, 16).astype(BF16), expand, preferred_element_type=F32)
    return [wide[2 * k : 2 * k + 1] + wide[2 * k + 1 : 2 * k + 2] for k in range(len(rows))]


def requests(start_row, rows, cap):
    starts = start_row.shape[1]
    square = (starts, starts)
    index = jnp.broadcast_to(start_row.astype(F32), square)
    index_t = index.T
    owner = jnp.floor(index * (1.0 / rows))
    owner_t = jnp.floor(index_t * (1.0 / rows))
    earlier = (iota(square, 1) < iota(square, 0)) & (owner == owner_t)
    rank = jnp.sum(earlier.astype(F32), axis=1, keepdims=True)
    perm = (owner_t * cap + rank == iota(square, 1).astype(F32)).astype(F32)
    wanted = jnp.sum(perm * (index_t - owner_t * rows), axis=0, keepdims=True)
    return perm, wanted


def own_kernel(
    cap, mine_ref, x_hbm, write_hbm, decay_hbm, start_hbm, x_ref, write_ref, sums_ref, perm_ref, wanted_ref,
    decay_ref, start_ref, sems,
):
    core = mine_ref[0] % 2
    rows, half = x_ref.shape
    heads = sums_ref.shape[0]
    lanes_at = pl.multiple_of(core * half, LANES)
    copies = [
        pltpu.make_async_copy(source, target, sems.at[k])
        for k, (source, target) in enumerate(
            (
                (start_hbm, start_ref),
                (decay_hbm, decay_ref),
                (write_hbm, write_ref),
                (x_hbm.at[:, pl.ds(lanes_at, half)], x_ref),
            )
        )
    ]
    for copy in copies:
        copy.start()
    copies[0].wait()
    perm, wanted = requests(start_ref[...], rows, cap)
    perm_ref[...] = perm.astype(BF16)
    wanted_ref[...] = wanted
    copies[1].wait()
    sums_ref[...] = running_sums(jnp.where(core == 0, decay_ref[:heads], decay_ref[heads:]))
    copies[2].wait()
    copies[3].wait()


def running_sums(decays):
    rows = decays.shape[1]
    upper = (iota((rows, rows), 0) <= iota((rows, rows), 1)).astype(F32)
    return jnp.dot(decays, upper, precision=lax.Precision.HIGHEST, preferred_element_type=F32)


def before_kernel(
    cap, mine_ref, x_own_ref, x_other_ref, write_own_ref, write_other_ref, sums_ref, decay_other_ref, wanted_ref,
    start_other_ref, send_ref, ends_ref, x_ref, write_ref, run_ref, run_t_ref, aux_ref,
):
    core = mine_ref[0] % 2
    first = core == 0
    rows, half = x_own_ref.shape
    state_size = write_ref.shape[0]
    heads = run_ref.shape[1]
    head_width = half // heads
    own, other = x_own_ref[...], x_other_ref[:, pl.ds(pl.multiple_of(core * half, LANES), half)]
    x_ref[:rows, :] = jnp.where(first, own, other)
    x_ref[rows:, :] = jnp.where(first, other, own)
    own = sums_ref[...]
    other = running_sums(jnp.where(first, decay_other_ref[:heads], decay_other_ref[heads:]))
    one, two = jnp.where(first, own, other), jnp.where(first, other, own)
    run_t = jnp.concatenate([one, two + one[:, rows - 1 :]], axis=1)
    run_t_ref[...] = run_t
    run = run_t.T
    run_ref[...] = run
    last = run[2 * rows - 1 :]
    tail = jnp.exp(last - run)
    own, other = write_own_ref[...], write_other_ref[...]
    write = jnp.concatenate([jnp.where(first, own, other), jnp.where(first, other, own)], axis=1)
    write_ref[...] = write
    for pair in range(heads // 2):
        lanes = slice(pair * LANES, (pair + 1) * LANES)
        scaled = x_ref[:, lanes].astype(F32) * two_heads(tail, pair, head_width, (2 * rows, LANES))
        ends = jnp.dot(write, scaled.astype(BF16), preferred_element_type=F32)
        ends_ref[:, lanes] = ends
        send_ref[:, lanes] = ends.astype(BF16)
    _, other = requests(start_other_ref[...], rows, cap)
    own = wanted_ref[...]
    wanted = jnp.concatenate([jnp.where(first, own, other), jnp.where(first, other, own)], axis=0)
    total = jnp.concatenate([jnp.exp(last), jnp.zeros((1, LANES - heads), F32)], axis=1)
    aux_ref[...] = stack_rows([total, jnp.ones((1, LANES), F32), wanted], aux_ref.shape[0])
    write_meta(send_ref, total, wanted, half, state_size)


def local_kernel(
    mine_ref, x_ref, write_ref, read_hbm, read_other_ref, run_ref, run_t_ref, skip_hbm, out_ref, read_out,
    read_ref, skip_ref, sems,
):
    copies = [
        pltpu.make_async_copy(read_hbm, read_ref, sems.at[0]),
        pltpu.make_async_copy(skip_hbm, skip_ref, sems.at[1]),
    ]
    for copy in copies:
        copy.start()
    for copy in copies:
        copy.wait()
    first = mine_ref[0] % 2 == 0
    rows, half = x_ref.shape[0] // 2, x_ref.shape[1]
    heads = run_ref.shape[1]
    head_width = half // heads
    own, other = read_ref[...], read_other_ref[...]
    read = jnp.concatenate([jnp.where(first, own, other), jnp.where(first, other, own)], axis=1).T
    read_out[...] = read
    gram = jnp.dot(read, write_ref[...], preferred_element_type=F32)
    skip = jnp.where(first, skip_ref[:, :heads], skip_ref[:, heads:])
    mask = iota((rows, rows), 0) >= iota((rows, rows), 1)
    for chunk in range(2):
        at, count = chunk * rows, (chunk + 1) * rows
        lane = iota((count, LANES), 1)
        for pair in range(heads // 2):
            lanes = slice(pair * LANES, (pair + 1) * LANES)
            weights = []
            for head in (2 * pair, 2 * pair + 1):
                for back in range(chunk + 1):
                    seen = slice(back * rows, (back + 1) * rows)
                    spread = run_ref[at:count, head : head + 1] - run_t_ref[head : head + 1, seen]
                    if back == chunk:
                        spread = jnp.where(mask, spread, -jnp.inf)
                    weights.append((jnp.exp(spread) * gram[at:count, seen]).astype(BF16))
            x = x_ref[:count, lanes]
            zero = jnp.zeros_like(x)
            split = jnp.concatenate(
                [jnp.where(lane < head_width, x, zero), jnp.where(lane < head_width, zero, x)], axis=0
            )
            inner = jnp.dot(jnp.concatenate(weights, axis=1), split, preferred_element_type=F32)
            factor = two_heads(skip, pair, head_width, (1, LANES))
            out_ref[at:count, lanes] = inner + factor * x[at:count].astype(F32)


def stage_kernel(bit, has_prefix, head_width, mine_ref, group_ref, aux_ref, got_ref, prefix_ref, prefix_out, send_ref, aux_out, *group_out):
    state_size, half = group_ref.shape
    count = 1 << bit
    later = (mine_ref[0] >> bit) % 2 == 1
    new_decay, new_wanted = read_meta(got_ref, count, half, state_size)
    decay, prefix_decay = aux_ref[0:1], aux_ref[1:2]
    wanted = aux_ref[2 : 2 + count]
    into, across = spread_rows([prefix_decay, jnp.where(later, decay, new_decay)], half, head_width)
    group, got = group_ref[...], got_ref[:, :half].astype(F32)
    moved = into * got
    if has_prefix:
        moved = prefix_ref[...] + moved
        prefix_out[...] = jnp.where(later, moved, prefix_ref[...])
    else:
        prefix_out[...] = jnp.where(later, moved, jnp.zeros_like(moved))
    total = jnp.where(later, got, group) * across + jnp.where(later, group, got)
    for ref in group_out:
        ref[...] = total
    send_ref[:, :half] = total.astype(BF16)
    wanted = jnp.concatenate(
        [jnp.where(later, new_wanted, wanted), jnp.where(later, wanted, new_wanted)], axis=0
    )
    write_meta(send_ref, decay * new_decay, wanted, half, state_size)
    aux_out[...] = stack_rows(
        [decay * new_decay, jnp.where(later, prefix_decay * new_decay, prefix_decay), wanted], aux_out.shape[0]
    )


def last_stage_kernel(bit, rows, head_width, mine_ref, prefix_ref, aux_ref, got_ref, token_ref, carry_ref, pick_ref):
    state_size, half = prefix_ref.shape
    count = 1 << bit
    mine = mine_ref[0]
    later = (mine >> bit) % 2 == 1
    _, new_wanted = read_meta(got_ref, count, half, state_size)
    (into,) = spread_rows([aux_ref[1:2]], half, head_width)
    prefix = prefix_ref[...]
    carry_ref[...] = jnp.where(later, prefix + into * got_ref[:, :half].astype(F32), prefix).astype(BF16)
    wanted = aux_ref[2 : 2 + count]
    wanted = jnp.concatenate(
        [jnp.where(later, new_wanted, wanted), jnp.where(later, wanted, new_wanted)], axis=0
    )
    peers = 2 * count
    picks = pick_ref.shape[0]
    both = picks // peers
    table = stack_rows([wanted], LANES) if peers < LANES else wanted
    asker = mask16(iota((picks, LANES), 0) // both == iota((picks, LANES), 1))
    by_slot = jnp.dot(asker, table.astype(BF16), preferred_element_type=F32)
    turn = iota((picks, LANES), 0) % both
    here = iota((picks, LANES), 1) == (mine // 2) * both + turn
    asked = jnp.sum(jnp.where(here, by_slot + ((turn // (both // 2)) * rows).astype(F32), 0.0), axis=1, keepdims=True)
    pick_ref[...] = mask16(asked == iota(pick_ref.shape, 1).astype(F32))


def after_kernel(
    mine_ref, local_ref, read_ref, run_ref, carry_ref, gain_ref, pick_ref, sent_ref, stay_ref, go_ref,
    mixed_ref, total_ref, post_ref,
):
    core = mine_ref[0] % 2
    rows, half = local_ref.shape[0] // 2, local_ref.shape[1]
    heads = run_ref.shape[1]
    head_width = half // heads
    entered = jnp.exp(run_ref[...])
    square = (LANES, LANES)
    same_head = mask16(iota(square, 0) // head_width == iota(square, 1) // head_width)
    gain = jnp.where(core == 0, gain_ref[:, :half], gain_ref[:, half:])
    blocks = [slice(k * LANES, (k + 1) * LANES) for k in range(half // LANES)]
    total_ref[...] = jnp.dot(read_ref[...], carry_ref[...], preferred_element_type=F32)
    for pair, lanes in enumerate(blocks):
        mixed_ref[:, lanes] = local_ref[:, lanes] + total_ref[:, lanes] * two_heads(
            entered, pair, head_width, (2 * rows, LANES)
        )
    for lanes in blocks:
        mixed = mixed_ref[:, lanes]
        squares = mixed * mixed
        high = squares.astype(BF16)
        low = (squares - high.astype(F32)).astype(BF16)
        total_ref[:, lanes] = jnp.dot(high, same_head, preferred_element_type=F32) + jnp.dot(
            low, same_head, preferred_element_type=F32
        )
    for lanes in blocks:
        scale = lax.rsqrt(total_ref[:, lanes] * (1.0 / head_width) + 1e-05)
        post_ref[:, lanes] = (mixed_ref[:, lanes] * scale * gain[:, lanes]).astype(BF16)
    sent_ref[...] = jnp.dot(pick_ref[...], post_ref[...], preferred_element_type=F32).astype(BF16)
    stay_ref[...] = post_ref[pl.ds(pl.multiple_of(core * rows, rows), rows), :]
    go_ref[...] = post_ref[pl.ds(pl.multiple_of((1 - core) * rows, rows), rows), :]


def fetch_kernel(token_ref, *refs):
    count = (len(refs) - 1) // 2
    sems = refs[-1]
    copies = [pltpu.make_async_copy(refs[k], refs[count + k], sems.at[k]) for k in range(count)]
    for copy in copies:
        copy.start()
    for copy in copies:
        copy.wait()


def folded(array):
    total = array[:, :LANES]
    for k in range(1, array.shape[1] // LANES):
        total = total + array[:, k * LANES : (k + 1) * LANES]
    return total


def imagined_steps(held_refs, squares, noise_ref, act_ref, dyn_ref, act_in_ref, out_ref, value_ref, hidden_ref, steps):
    width, inside = dyn_ref.shape
    chunk = 256
    columns = []
    for step in steps:
        latent_ref, next_ref = held_refs
        scale = lax.rsqrt(jnp.sum(squares, axis=1, keepdims=True) * (1.0 / width) + 1e-06)
        latent = latent_ref[...]
        action = jnp.dot(latent, act_ref[...], preferred_element_type=F32)
        action = jnp.tanh(action * scale).astype(BF16)
        value = None
        for at in range(0, inside, chunk):
            part = slice(at, at + chunk)
            inner = jnp.dot(latent, dyn_ref[:, part], preferred_element_type=F32) * scale + jnp.dot(
                action, act_in_ref[:, part], preferred_element_type=F32
            )
            hidden = (inner / (1.0 + jnp.exp(-inner)) + noise_ref[step, :, part].astype(F32)).astype(BF16)
            hidden_ref[:, part] = hidden
            worth = folded(hidden.astype(F32) * value_ref[:, part].astype(F32))
            value = worth if value is None else value + worth
        columns.append(jnp.sum(value, axis=1, keepdims=True))
        hidden = hidden_ref[...]
        squares = None
        for at in range(0, width, chunk):
            part = slice(at, at + chunk)
            moved = latent_ref[:, part].astype(F32) + jnp.dot(hidden, out_ref[:, part], preferred_element_type=F32)
            rounded = moved.astype(BF16)
            next_ref[:, part] = rounded
            wide = rounded.astype(F32)
            square = folded(wide * wide)
            squares = square if squares is None else squares + square
        held_refs = (next_ref, latent_ref)
    return held_refs, squares, columns


def first_step_kernel(
    landed_ref, perm_ref, noise_ref, act_ref, dyn_ref, act_in_ref, out_ref, value_ref, latent_ref, squares_ref,
    column_ref, start_ref, hidden_ref,
):
    starts = perm_ref.shape[0]
    half = landed_ref.shape[-1]
    perm = perm_ref[...]
    squares = None
    for side in range(2):
        wide = jnp.dot(perm, landed_ref[:, side].reshape(starts, half), preferred_element_type=F32)
        start_ref[:, side * half : (side + 1) * half] = wide.astype(BF16)
        square = folded(wide * wide)
        squares = square if squares is None else squares + square
    _, squares, columns = imagined_steps(
        (start_ref, latent_ref),
        squares,
        noise_ref,
        act_ref,
        dyn_ref,
        act_in_ref,
        out_ref,
        value_ref,
        hidden_ref,
        range(1),
    )
    squares_ref[...] = squares
    column_ref[...] = jnp.broadcast_to(columns[0], column_ref.shape)


def later_steps_kernel(
    mine_ref, stay_ref, got_ref, latent_ref, squares_ref, column_ref, noise_ref, act_ref, dyn_ref, act_in_ref,
    out_ref, value_ref, post_hbm, values_ref, final_ref, spare_ref, hidden_ref, sems,
):
    core = mine_ref[0] % 2
    half = stay_ref.shape[1]
    copies = [
        pltpu.make_async_copy(source, post_hbm.at[:, pl.ds(pl.multiple_of(side * half, LANES), half)], sems.at[k])
        for k, (source, side) in enumerate(((stay_ref, core), (got_ref, 1 - core)))
    ]
    for copy in copies:
        copy.start()
    horizon = noise_ref.shape[0]
    refs, squares, columns = (latent_ref, None), squares_ref[...], []
    for step in range(1, horizon):
        target = final_ref if step == horizon - 1 else spare_ref.at[step % 2]
        refs, squares, new = imagined_steps(
            (refs[0], target),
            squares,
            noise_ref,
            act_ref,
            dyn_ref,
            act_in_ref,
            out_ref,
            value_ref,
            hidden_ref,
            range(step, step + 1),
        )
        columns += new
    lane = iota(column_ref.shape, 1)
    table = column_ref[...]
    for k, column in enumerate(columns):
        table = jnp.where(lane == k + 1, column, table)
    values_ref[...] = table.T[:horizon]
    for copy in copies:
        copy.wait()


def cost(flops, read):
    return pl.CostEstimate(flops=flops, bytes_accessed=read, transcendentals=0)


def in_hbm(array):
    return pltpu.with_memory_space_constraint(array, pltpu.HBM)


def per_device(
    peer_count,
    features,
    state_write,
    state_read,
    log_decay,
    skip_gain,
    post_gain,
    start_index,
    step_noise,
    act_weight,
    dyn_weight,
    act_in_weight,
    out_weight,
    value_weight,
):
    rows, width = features.shape
    head_count = log_decay.shape[1]
    head_width = width // head_count
    state_size = state_write.shape[1]
    half = width // 2
    heads = head_count // 2
    starts = start_index.shape[0]
    cap = starts // peer_count
    bits = peer_count.bit_length() - 1
    mine = lax.axis_index("seq").reshape(1)
    params = pltpu.CompilerParams(vmem_limit_bytes=12 << 20)
    held = pltpu.VMEM

    def swap(array, bit):
        return lax.ppermute(array, "seq", [(i, i ^ (1 << bit)) for i in range(peer_count)])

    def payload(count):
        blocks = -(-(2 + count) // state_size)
        return held((state_size, half + blocks * LANES), BF16)

    def auxiliary(count):
        return held((-(-(2 + count) // 8) * 8, LANES), F32)

    write_t, read_t, decay_t = state_write.T, state_read.T, log_decay.T
    start_row = start_index.reshape(1, starts)
    x_other = swap(features, 0)
    decay_other, write_other = swap(decay_t, 0), swap(write_t, 0)
    start_other, read_other = swap(start_row, 0), swap(read_t, 0)

    x_own, write_own, sums, perm, wanted = pl.pallas_call(
        functools.partial(own_kernel, cap),
        out_shape=(
            held((rows, half), BF16),
            held((state_size, rows), BF16),
            held((heads, rows), F32),
            held((starts, starts), BF16),
            held((1, starts), F32),
        ),
        in_specs=[SMEM] + [HBM] * 4,
        out_specs=(VMEM,) * 5,
        scratch_shapes=[
            pltpu.VMEM((head_count, rows), F32),
            pltpu.VMEM((1, starts), jnp.int32),
            pltpu.SemaphoreType.DMA((4,)),
        ],
        compiler_params=params,
        cost_estimate=cost(0, 4 * rows * width),
    )(mine, in_hbm(features), in_hbm(write_t), in_hbm(decay_t), in_hbm(start_row))

    send, group, chip_x, write, run, run_t, aux = pl.pallas_call(
        functools.partial(before_kernel, cap),
        out_shape=(
            payload(2),
            held((state_size, half), F32),
            held((2 * rows, half), BF16),
            held((state_size, 2 * rows), BF16),
            held((2 * rows, heads), F32),
            held((heads, 2 * rows), F32),
            auxiliary(2),
        ),
        in_specs=[SMEM] + [VMEM] * 8,
        out_specs=(VMEM,) * 7,
        compiler_params=params,
    )(mine, x_own, x_other, write_own, write_other, sums, decay_other, wanted, start_other)

    local_out, read = pl.pallas_call(
        local_kernel,
        out_shape=(held((2 * rows, half), F32), held((2 * rows, state_size), BF16)),
        in_specs=[SMEM, VMEM, VMEM, HBM, VMEM, VMEM, VMEM, HBM],
        out_specs=(VMEM, VMEM),
        scratch_shapes=[
            pltpu.VMEM((state_size, rows), BF16),
            pltpu.VMEM((1, head_count), F32),
            pltpu.SemaphoreType.DMA((2,)),
        ],
        compiler_params=params,
        cost_estimate=cost(8 * rows * rows * width, 4 * rows * width),
    )(mine, chip_x, write, in_hbm(read_t), read_other, run, run_t, in_hbm(skip_gain[None, :]))

    def fetch(token, *weights):
        return pl.pallas_call(
            fetch_kernel,
            out_shape=tuple(held(weight.shape, weight.dtype) for weight in weights),
            in_specs=[ANY] + [HBM] * len(weights),
            out_specs=(VMEM,) * len(weights),
            scratch_shapes=[pltpu.SemaphoreType.DMA((len(weights),))],
            compiler_params=params,
            cost_estimate=cost(0, 2 * sum(weight.size * 2 for weight in weights)),
        )(token, *(in_hbm(weight) for weight in weights))

    prefix, group = local_out, [group]
    for bit in range(1, bits - 1):
        got = swap(send, bit)
        if bit == 2:
            (dyn,) = fetch(aux, dyn_weight)
            aux, _ = lax.optimization_barrier((aux, dyn))
        goes_on = int(bit < bits - 2)
        prefix, send, aux, *group = pl.pallas_call(
            functools.partial(stage_kernel, bit, bit > 1, head_width),
            out_shape=(
                held((state_size, half), F32),
                payload(2 << bit),
                auxiliary(2 << bit),
            )
            + (held((state_size, half), F32),) * goes_on,
            in_specs=[SMEM] + [VMEM] * 3 + [VMEM if bit > 1 else ANY],
            out_specs=(VMEM,) * (3 + goes_on),
            compiler_params=params,
        )(mine, *group, aux, got, prefix)
    got = swap(send, bits - 1)
    out, act, act_in, noise = fetch(aux, out_weight, act_weight, act_in_weight, step_noise)
    carry, pick = pl.pallas_call(
        functools.partial(last_stage_kernel, bits - 1, rows, head_width),
        out_shape=(held((state_size, half), BF16), held((2 * starts, 2 * rows), BF16)),
        in_specs=[SMEM] + [VMEM] * 3 + [ANY],
        out_specs=(VMEM,) * 2,
        compiler_params=params,
    )(mine, prefix, aux, got, act_in)

    picked, stay, go = pl.pallas_call(
        after_kernel,
        out_shape=(
            held((2 * starts, half), BF16),
            held((rows, half), BF16),
            held((rows, half), BF16),
        ),
        in_specs=[SMEM] + [VMEM] * 6,
        out_specs=(VMEM,) * 3,
        scratch_shapes=[
            pltpu.VMEM((2 * rows, half), F32),
            pltpu.VMEM((2 * rows, half), F32),
            pltpu.VMEM((2 * rows, half), BF16),
        ],
        compiler_params=params,
    )(mine, local_out, read, run, carry, post_gain[None, :], pick)

    landed = lax.all_to_all(
        picked.reshape(peer_count, 2 * cap, half), "seq", split_axis=0, concat_axis=0, tiled=True
    ).reshape(peer_count // 2, 2, 2 * cap, half)

    go, landed = lax.optimization_barrier((go, landed))
    got = swap(go, 0)
    horizon = step_noise.shape[0]
    big = pltpu.CompilerParams(vmem_limit_bytes=16 << 20)
    weights = (noise, act, dyn, act_in, out, value_weight[None, :])
    hidden = pltpu.VMEM((starts, dyn_weight.shape[1]), BF16)
    latent, squares, column = pl.pallas_call(
        first_step_kernel,
        out_shape=(held((starts, width), BF16), held((starts, LANES), F32), held((starts, LANES), F32)),
        in_specs=[VMEM] * 8,
        out_specs=(VMEM,) * 3,
        scratch_shapes=[pltpu.VMEM((starts, width), BF16), hidden],
        compiler_params=big,
        cost_estimate=cost(2 * starts * 2 * dyn_weight.size, 4 * dyn_weight.size),
    )(landed, perm, *weights)
    posterior, values, final_latent = pl.pallas_call(
        later_steps_kernel,
        out_shape=(
            jax.ShapeDtypeStruct((rows, width), BF16),
            jax.ShapeDtypeStruct((horizon, starts), F32),
            jax.ShapeDtypeStruct((starts, width), BF16),
        ),
        in_specs=[SMEM] + [VMEM] * 11,
        out_specs=(HBM, VMEM, VMEM),
        scratch_shapes=[pltpu.VMEM((2, starts, width), BF16), hidden, pltpu.SemaphoreType.DMA((2,))],
        compiler_params=big,
    )(mine, stay, got, latent, squares, column, *weights)
    return (posterior, values, final_latent)


def solution(mesh):
    whole = P()
    by_row = P(("groups", "seq"), None)
    placed = (
        by_row,
        by_row,
        by_row,
        by_row,
        whole,
        whole,
        P(("groups", "seq")),
        P(None, ("groups", "seq"), None),
        whole,
        whole,
        whole,
        whole,
        whole,
    )
    return jax.shard_map(
        functools.partial(per_device, mesh.shape["seq"]),
        mesh=mesh,
        in_specs=placed,
        out_specs=(by_row, P(None, ("groups", "seq")), by_row),
        check_vma=False,
    )
```

```python
import functools
import jax
import jax.numpy as jnp
from jax import lax
from jax.experimental import pallas as pl
from jax.experimental.pallas import tpu as pltpu
from jax.sharding import PartitionSpec as P

F32 = jnp.float32
BF16 = jnp.bfloat16
LANES = 128
VMEM = pl.BlockSpec(memory_space=pltpu.VMEM)
SMEM = pl.BlockSpec(memory_space=pltpu.SMEM)
HBM = pl.BlockSpec(memory_space=pltpu.HBM)
ANY = pl.BlockSpec(memory_space=pl.ANY)


def iota(shape, dim):
    return lax.broadcasted_iota(jnp.int32, shape, dim)


def mask16(condition):
    return condition.astype(F32).astype(BF16)


def two_heads(cols, pair, head_width, shape):
    first = jnp.broadcast_to(cols[:, 2 * pair : 2 * pair + 1], shape)
    second = jnp.broadcast_to(cols[:, 2 * pair + 1 : 2 * pair + 2], shape)
    return jnp.where(iota(shape, 1) < head_width, first, second)


def stack_rows(rows, count):
    used = sum(row.shape[0] for row in rows)
    if used < count:
        rows = list(rows) + [jnp.zeros((count - used, LANES), F32)]
    return jnp.concatenate(rows, axis=0)


def write_meta(send_ref, decay, wanted, half, state_size):
    high = decay.astype(BF16).astype(F32)
    blocks = (send_ref.shape[1] - half) // LANES
    meta = stack_rows([high, decay - high, wanted], blocks * state_size).astype(BF16)
    for block in range(blocks):
        send_ref[:, half + block * LANES : half + (block + 1) * LANES] = meta[
            block * state_size : (block + 1) * state_size
        ]


def read_meta(got_ref, count, half, state_size):
    blocks = (got_ref.shape[1] - half) // LANES
    meta = jnp.concatenate(
        [got_ref[:, half + block * LANES : half + (block + 1) * LANES].astype(F32) for block in range(blocks)], axis=0
    )
    return meta[0:1] + meta[1:2], meta[2 : 2 + count]


def spread_rows(rows, half, head_width):
    pieces = []
    for row in rows:
        high = row.astype(BF16).astype(F32)
        pieces += [high, row - high]
    expand = mask16(iota((LANES, half), 0) == iota((LANES, half), 1) // head_width)
    wide = jnp.dot(stack_rows(pieces, 16).astype(BF16), expand, preferred_element_type=F32)
    return [wide[2 * k : 2 * k + 1] + wide[2 * k + 1 : 2 * k + 2] for k in range(len(rows))]


def partner_order(chips):
    middle = chips // 2
    far = sorted(range(middle, chips), key=lambda k: (k & 1, k))
    near = sorted(range(1, middle), key=lambda k: (-(k >> 1), k))
    return far, near + [0]


def looked_up(index, table):
    found = jnp.zeros_like(index)
    for k, value in enumerate(table):
        if value:
            found = jnp.where(index == k, value, found)
    return found


def requests(start_row, rows, cap):
    starts = start_row.shape[1]
    square = (starts, starts)
    index = jnp.broadcast_to(start_row.astype(F32), square)
    index_t = index.T
    owner = jnp.floor(index * (1.0 / rows))
    owner_t = jnp.floor(index_t * (1.0 / rows))
    earlier = (iota(square, 1) < iota(square, 0)) & (owner == owner_t)
    rank = jnp.sum(earlier.astype(F32), axis=1, keepdims=True)
    perm = (owner_t * cap + rank == iota(square, 1).astype(F32)).astype(F32)
    wanted = jnp.sum(perm * (index_t - owner_t * rows), axis=0, keepdims=True)
    return perm, wanted, owner_t.astype(jnp.int32), rank.astype(jnp.int32)


def own_kernel(
    cap, places, mine_ref, x_hbm, write_hbm, decay_hbm, start_hbm, x_ref, write_ref, sums_ref, perm_ref, wanted_ref,
    decay_ref, start_ref, sems,
):
    core = mine_ref[0] % 2
    rows, half = x_ref.shape
    heads = sums_ref.shape[0]
    lanes_at = pl.multiple_of(core * half, LANES)
    copies = [
        pltpu.make_async_copy(source, target, sems.at[k])
        for k, (source, target) in enumerate(
            (
                (start_hbm, start_ref),
                (decay_hbm, decay_ref),
                (write_hbm, write_ref),
                (x_hbm.at[:, pl.ds(lanes_at, half)], x_ref),
            )
        )
    ]
    for copy in copies:
        copy.start()
    copies[0].wait()
    perm, wanted, owner, rank = requests(start_ref[...], rows, cap)
    if places:
        place = looked_up((owner // 2) ^ (mine_ref[0] // 2), places)
        perm = mask16((place * 2 + owner % 2) * cap + rank == iota(perm.shape, 1))
    perm_ref[...] = perm.astype(BF16)
    wanted_ref[...] = wanted
    copies[1].wait()
    sums_ref[...] = running_sums(jnp.where(core == 0, decay_ref[:heads], decay_ref[heads:]))
    copies[2].wait()
    copies[3].wait()


def running_sums(decays):
    rows = decays.shape[1]
    upper = (iota((rows, rows), 0) <= iota((rows, rows), 1)).astype(F32)
    return jnp.dot(decays, upper, precision=lax.Precision.HIGHEST, preferred_element_type=F32)


def before_kernel(
    cap, mine_ref, x_own_ref, x_other_ref, write_own_ref, write_other_ref, sums_ref, decay_other_ref, wanted_ref,
    start_other_ref, send_ref, ends_ref, x_ref, write_ref, run_ref, run_t_ref, aux_ref,
):
    core = mine_ref[0] % 2
    first = core == 0
    rows, half = x_own_ref.shape
    state_size = write_ref.shape[0]
    heads = run_ref.shape[1]
    head_width = half // heads
    own, other = x_own_ref[...], x_other_ref[:, pl.ds(pl.multiple_of(core * half, LANES), half)]
    x_ref[:rows, :] = jnp.where(first, own, other)
    x_ref[rows:, :] = jnp.where(first, other, own)
    own = sums_ref[...]
    other = running_sums(jnp.where(first, decay_other_ref[:heads], decay_other_ref[heads:]))
    one, two = jnp.where(first, own, other), jnp.where(first, other, own)
    run_t = jnp.concatenate([one, two + one[:, rows - 1 :]], axis=1)
    run_t_ref[...] = run_t
    run = run_t.T
    run_ref[...] = run
    last = run[2 * rows - 1 :]
    tail = jnp.exp(last - run)
    own, other = write_own_ref[...], write_other_ref[...]
    write = jnp.concatenate([jnp.where(first, own, other), jnp.where(first, other, own)], axis=1)
    write_ref[...] = write
    for pair in range(heads // 2):
        lanes = slice(pair * LANES, (pair + 1) * LANES)
        scaled = x_ref[:, lanes].astype(F32) * two_heads(tail, pair, head_width, (2 * rows, LANES))
        ends = jnp.dot(write, scaled.astype(BF16), preferred_element_type=F32)
        ends_ref[:, lanes] = ends
        send_ref[:, lanes] = ends.astype(BF16)
    _, other, _, _ = requests(start_other_ref[...], rows, cap)
    own = wanted_ref[...]
    wanted = jnp.concatenate([jnp.where(first, own, other), jnp.where(first, other, own)], axis=0)
    total = jnp.concatenate([jnp.exp(last), jnp.zeros((1, LANES - heads), F32)], axis=1)
    aux_ref[...] = stack_rows([total, jnp.ones((1, LANES), F32), wanted], aux_ref.shape[0])
    write_meta(send_ref, total, wanted, half, state_size)


def local_kernel(
    mine_ref, x_ref, write_ref, read_hbm, read_other_ref, run_ref, run_t_ref, skip_hbm, out_ref, read_out,
    read_ref, skip_ref, sems,
):
    copies = [
        pltpu.make_async_copy(read_hbm, read_ref, sems.at[0]),
        pltpu.make_async_copy(skip_hbm, skip_ref, sems.at[1]),
    ]
    for copy in copies:
        copy.start()
    for copy in copies:
        copy.wait()
    first = mine_ref[0] % 2 == 0
    rows, half = x_ref.shape[0] // 2, x_ref.shape[1]
    heads = run_ref.shape[1]
    head_width = half // heads
    own, other = read_ref[...], read_other_ref[...]
    read = jnp.concatenate([jnp.where(first, own, other), jnp.where(first, other, own)], axis=1).T
    read_out[...] = read
    gram = jnp.dot(read, write_ref[...], preferred_element_type=F32)
    skip = jnp.where(first, skip_ref[:, :heads], skip_ref[:, heads:])
    mask = iota((rows, rows), 0) >= iota((rows, rows), 1)
    for chunk in range(2):
        at, count = chunk * rows, (chunk + 1) * rows
        lane = iota((count, LANES), 1)
        for pair in range(heads // 2):
            lanes = slice(pair * LANES, (pair + 1) * LANES)
            weights = []
            for head in (2 * pair, 2 * pair + 1):
                for back in range(chunk + 1):
                    seen = slice(back * rows, (back + 1) * rows)
                    spread = run_ref[at:count, head : head + 1] - run_t_ref[head : head + 1, seen]
                    if back == chunk:
                        spread = jnp.where(mask, spread, -jnp.inf)
                    weights.append((jnp.exp(spread) * gram[at:count, seen]).astype(BF16))
            x = x_ref[:count, lanes]
            zero = jnp.zeros_like(x)
            split = jnp.concatenate(
                [jnp.where(lane < head_width, x, zero), jnp.where(lane < head_width, zero, x)], axis=0
            )
            inner = jnp.dot(jnp.concatenate(weights, axis=1), split, preferred_element_type=F32)
            factor = two_heads(skip, pair, head_width, (1, LANES))
            out_ref[at:count, lanes] = inner + factor * x[at:count].astype(F32)


def stage_kernel(bit, has_prefix, head_width, mine_ref, group_ref, aux_ref, got_ref, prefix_ref, prefix_out, send_ref, aux_out, *group_out):
    state_size, half = group_ref.shape
    count = 1 << bit
    later = (mine_ref[0] >> bit) % 2 == 1
    new_decay, new_wanted = read_meta(got_ref, count, half, state_size)
    decay, prefix_decay = aux_ref[0:1], aux_ref[1:2]
    wanted = aux_ref[2 : 2 + count]
    into, across = spread_rows([prefix_decay, jnp.where(later, decay, new_decay)], half, head_width)
    group, got = group_ref[...], got_ref[:, :half].astype(F32)
    moved = into * got
    if has_prefix:
        moved = prefix_ref[...] + moved
        prefix_out[...] = jnp.where(later, moved, prefix_ref[...])
    else:
        prefix_out[...] = jnp.where(later, moved, jnp.zeros_like(moved))
    total = jnp.where(later, got, group) * across + jnp.where(later, group, got)
    for ref in group_out:
        ref[...] = total
    send_ref[:, :half] = total.astype(BF16)
    wanted = jnp.concatenate(
        [jnp.where(later, new_wanted, wanted), jnp.where(later, wanted, new_wanted)], axis=0
    )
    write_meta(send_ref, decay * new_decay, wanted, half, state_size)
    aux_out[...] = stack_rows(
        [decay * new_decay, jnp.where(later, prefix_decay * new_decay, prefix_decay), wanted], aux_out.shape[0]
    )


def last_stage_kernel(bit, rows, head_width, order, mine_ref, prefix_ref, aux_ref, got_ref, token_ref, carry_ref, pick_ref):
    state_size, half = prefix_ref.shape
    count = 1 << bit
    mine = mine_ref[0]
    later = (mine >> bit) % 2 == 1
    _, new_wanted = read_meta(got_ref, count, half, state_size)
    (into,) = spread_rows([aux_ref[1:2]], half, head_width)
    prefix = prefix_ref[...]
    carry_ref[...] = jnp.where(later, prefix + into * got_ref[:, :half].astype(F32), prefix).astype(BF16)
    wanted = aux_ref[2 : 2 + count]
    wanted = jnp.concatenate(
        [jnp.where(later, new_wanted, wanted), jnp.where(later, wanted, new_wanted)], axis=0
    )
    peers = 2 * count
    picks = pick_ref.shape[0]
    both = picks // peers
    table = stack_rows([wanted], LANES) if peers < LANES else wanted
    device = iota((picks, LANES), 0) // both
    if order:
        chip = looked_up(device % len(order), order) ^ (mine // 2)
        device = chip * 2 + (device // len(order) + mine) % 2
    asker = mask16(device == iota((picks, LANES), 1))
    by_slot = jnp.dot(asker, table.astype(BF16), preferred_element_type=F32)
    turn = iota((picks, LANES), 0) % both
    here = iota((picks, LANES), 1) == (mine // 2) * both + turn
    asked = jnp.sum(jnp.where(here, by_slot + ((turn // (both // 2)) * rows).astype(F32), 0.0), axis=1, keepdims=True)
    pick_ref[...] = mask16(asked == iota(pick_ref.shape, 1).astype(F32))


def normalize(mine_ref, local_ref, read_ref, run_ref, carry_ref, gain_ref, mixed_ref, total_ref, post_ref):
    core = mine_ref[0] % 2
    rows, half = local_ref.shape
    heads = run_ref.shape[1]
    head_width = half // heads
    entered = jnp.exp(run_ref[...])
    square = (LANES, LANES)
    same_head = mask16(iota(square, 0) // head_width == iota(square, 1) // head_width)
    gain = jnp.where(core == 0, gain_ref[:, :half], gain_ref[:, half:])
    blocks = [slice(k * LANES, (k + 1) * LANES) for k in range(half // LANES)]
    total_ref[...] = jnp.dot(read_ref[...], carry_ref[...], preferred_element_type=F32)
    for pair, lanes in enumerate(blocks):
        mixed_ref[:, lanes] = local_ref[:, lanes] + total_ref[:, lanes] * two_heads(
            entered, pair, head_width, (rows, LANES)
        )
    for lanes in blocks:
        mixed = mixed_ref[:, lanes]
        squares = mixed * mixed
        high = squares.astype(BF16)
        low = (squares - high.astype(F32)).astype(BF16)
        total_ref[:, lanes] = jnp.dot(high, same_head, preferred_element_type=F32) + jnp.dot(
            low, same_head, preferred_element_type=F32
        )
    for lanes in blocks:
        scale = lax.rsqrt(total_ref[:, lanes] * (1.0 / head_width) + 1e-05)
        post_ref[:, lanes] = (mixed_ref[:, lanes] * scale * gain[:, lanes]).astype(BF16)


def picked_rows(pick, post_ref):
    return jnp.dot(pick, post_ref[...], preferred_element_type=F32).astype(BF16)


def after_kernel(
    mine_ref, local_ref, read_ref, run_ref, carry_ref, gain_ref, pick_ref, post_ref, sent_ref, mixed_ref, total_ref
):
    normalize(mine_ref, local_ref, read_ref, run_ref, carry_ref, gain_ref, mixed_ref, total_ref, post_ref)
    count = sent_ref.shape[0]
    first = 0 if count == pick_ref.shape[0] else pick_ref.shape[0] // 2
    sent_ref[...] = picked_rows(pick_ref[first : first + count, :], post_ref)


def share_kernel(mine_ref, post_ref, stay_ref, go_ref):
    core = mine_ref[0] % 2
    rows = stay_ref.shape[0]
    stay_ref[...] = post_ref[pl.ds(pl.multiple_of(core * rows, rows), rows), :]
    go_ref[...] = post_ref[pl.ds(pl.multiple_of((1 - core) * rows, rows), rows), :]


def rest_kernel(mine_ref, post_ref, pick_ref, keep_ref, stay_ref, go_ref):
    keep_ref[...] = picked_rows(pick_ref[: keep_ref.shape[0], :], post_ref)
    share_kernel(mine_ref, post_ref, stay_ref, go_ref)


def merge_kernel(mine_ref, keep_ref, got_ref, *block_refs):
    first = mine_ref[0] % 2 == 0
    half = keep_ref.shape[1]
    keep, got = keep_ref[...], got_ref[...]
    left, right = jnp.where(first, keep, got), jnp.where(first, got, keep)
    size = block_refs[0].shape[0]
    for k, ref in enumerate(block_refs):
        ref[:, :half] = left[k * size : (k + 1) * size]
        ref[:, half:] = right[k * size : (k + 1) * size]


def fetch_kernel(token_ref, *refs):
    count = (len(refs) - 1) // 2
    sems = refs[-1]
    copies = [pltpu.make_async_copy(refs[k], refs[count + k], sems.at[k]) for k in range(count)]
    for copy in copies:
        copy.start()
    for copy in copies:
        copy.wait()


def folded(array):
    total = array[:, :LANES]
    for k in range(1, array.shape[1] // LANES):
        total = total + array[:, k * LANES : (k + 1) * LANES]
    return total


def imagined_steps(held_refs, squares, noise_ref, act_ref, dyn_ref, act_in_ref, out_ref, value_ref, hidden_ref, steps):
    width, inside = dyn_ref.shape
    chunk = 256
    columns = []
    for step in steps:
        latent_ref, next_ref = held_refs
        scale = lax.rsqrt(jnp.sum(squares, axis=1, keepdims=True) * (1.0 / width) + 1e-06)
        latent = latent_ref[...]
        action = jnp.dot(latent, act_ref[...], preferred_element_type=F32)
        action = jnp.tanh(action * scale).astype(BF16)
        value = None
        for at in range(0, inside, chunk):
            part = slice(at, at + chunk)
            inner = jnp.dot(latent, dyn_ref[:, part], preferred_element_type=F32) * scale + jnp.dot(
                action, act_in_ref[:, part], preferred_element_type=F32
            )
            hidden = (inner / (1.0 + jnp.exp(-inner)) + noise_ref[step, :, part].astype(F32)).astype(BF16)
            hidden_ref[:, part] = hidden
            worth = folded(hidden.astype(F32) * value_ref[:, part].astype(F32))
            value = worth if value is None else value + worth
        columns.append(jnp.sum(value, axis=1, keepdims=True))
        hidden = hidden_ref[...]
        squares = None
        for at in range(0, width, chunk):
            part = slice(at, at + chunk)
            moved = latent_ref[:, part].astype(F32) + jnp.dot(hidden, out_ref[:, part], preferred_element_type=F32)
            rounded = moved.astype(BF16)
            next_ref[:, part] = rounded
            wide = rounded.astype(F32)
            square = folded(wide * wide)
            squares = square if squares is None else squares + square
        held_refs = (next_ref, latent_ref)
    return held_refs, squares, columns


def imagine_kernel(
    mine_ref, stay_ref, got_ref, perm_ref, noise_ref, act_ref, dyn_ref, act_in_ref, out_ref, value_ref, *refs
):
    *landed_refs, post_hbm, values_ref, final_ref, spare_ref, hidden_ref, sems = refs
    core = mine_ref[0] % 2
    half = stay_ref.shape[1]
    copies = [
        pltpu.make_async_copy(source, post_hbm.at[:, pl.ds(pl.multiple_of(side * half, LANES), half)], sems.at[k])
        for k, (source, side) in enumerate(((stay_ref, core), (got_ref, 1 - core)))
    ]
    for copy in copies:
        copy.start()
    starts = perm_ref.shape[0]
    perm = perm_ref[...]
    squares = None
    for side in range(2):
        lanes = slice(side * half, (side + 1) * half)
        if len(landed_refs) == 1:
            landed = landed_refs[0][:, side].reshape(starts, half)
        else:
            landed = jnp.concatenate([ref[:, lanes] for ref in landed_refs], axis=0)
        wide = jnp.dot(perm, landed, preferred_element_type=F32)
        spare_ref[1, :, lanes] = wide.astype(BF16)
        square = folded(wide * wide)
        squares = square if squares is None else squares + square
    horizon = noise_ref.shape[0]
    refs, columns = (spare_ref.at[1], None), []
    for step in range(horizon):
        target = final_ref if step == horizon - 1 else spare_ref.at[step % 2]
        refs, squares, new = imagined_steps(
            (refs[0], target),
            squares,
            noise_ref,
            act_ref,
            dyn_ref,
            act_in_ref,
            out_ref,
            value_ref,
            hidden_ref,
            range(step, step + 1),
        )
        columns += new
    lane = iota((starts, LANES), 1)
    table = jnp.zeros((starts, LANES), F32)
    for k, column in enumerate(columns):
        table = jnp.where(lane == k, column, table)
    values_ref[...] = table.T[:horizon]
    for copy in copies:
        copy.wait()


def cost(flops, read):
    return pl.CostEstimate(flops=flops, bytes_accessed=read, transcendentals=0)


def in_hbm(array):
    return pltpu.with_memory_space_constraint(array, pltpu.HBM)


def per_device(
    peer_count,
    features,
    state_write,
    state_read,
    log_decay,
    skip_gain,
    post_gain,
    start_index,
    step_noise,
    act_weight,
    dyn_weight,
    act_in_weight,
    out_weight,
    value_weight,
):
    rows, width = features.shape
    head_count = log_decay.shape[1]
    head_width = width // head_count
    state_size = state_write.shape[1]
    half = width // 2
    heads = head_count // 2
    starts = start_index.shape[0]
    cap = starts // peer_count
    bits = peer_count.bit_length() - 1
    mine = lax.axis_index("seq").reshape(1)
    params = pltpu.CompilerParams(vmem_limit_bytes=12 << 20)
    held = pltpu.VMEM

    chips = peer_count // 2
    direct = chips <= 8 and cap % 8 == 0
    far, near = partner_order(chips) if direct else ([], [])
    order = far + near
    places = [order.index(k) for k in range(len(order))]

    def exchange(array, mask):
        return lax.ppermute(array, "seq", [(i, i ^ mask) for i in range(peer_count)])

    def swap(array, bit):
        return exchange(array, 1 << bit)

    def payload(count):
        blocks = -(-(2 + count) // state_size)
        return held((state_size, half + blocks * LANES), BF16)

    def auxiliary(count):
        return held((-(-(2 + count) // 8) * 8, LANES), F32)

    write_t, read_t, decay_t = state_write.T, state_read.T, log_decay.T
    start_row = start_index.reshape(1, starts)
    x_other = swap(features, 0)
    decay_other, write_other = swap(decay_t, 0), swap(write_t, 0)
    start_other, read_other = swap(start_row, 0), swap(read_t, 0)

    x_own, write_own, sums, perm, wanted = pl.pallas_call(
        functools.partial(own_kernel, cap, places),
        out_shape=(
            held((rows, half), BF16),
            held((state_size, rows), BF16),
            held((heads, rows), F32),
            held((starts, starts), BF16),
            held((1, starts), F32),
        ),
        in_specs=[SMEM] + [HBM] * 4,
        out_specs=(VMEM,) * 5,
        scratch_shapes=[
            pltpu.VMEM((head_count, rows), F32),
            pltpu.VMEM((1, starts), jnp.int32),
            pltpu.SemaphoreType.DMA((4,)),
        ],
        compiler_params=params,
        cost_estimate=cost(0, 4 * rows * width),
    )(mine, in_hbm(features), in_hbm(write_t), in_hbm(decay_t), in_hbm(start_row))

    send, group, chip_x, write, run, run_t, aux = pl.pallas_call(
        functools.partial(before_kernel, cap),
        out_shape=(
            payload(2),
            held((state_size, half), F32),
            held((2 * rows, half), BF16),
            held((state_size, 2 * rows), BF16),
            held((2 * rows, heads), F32),
            held((heads, 2 * rows), F32),
            auxiliary(2),
        ),
        in_specs=[SMEM] + [VMEM] * 8,
        out_specs=(VMEM,) * 7,
        compiler_params=params,
    )(mine, x_own, x_other, write_own, write_other, sums, decay_other, wanted, start_other)

    local_out, read = pl.pallas_call(
        local_kernel,
        out_shape=(held((2 * rows, half), F32), held((2 * rows, state_size), BF16)),
        in_specs=[SMEM, VMEM, VMEM, HBM, VMEM, VMEM, VMEM, HBM],
        out_specs=(VMEM, VMEM),
        scratch_shapes=[
            pltpu.VMEM((state_size, rows), BF16),
            pltpu.VMEM((1, head_count), F32),
            pltpu.SemaphoreType.DMA((2,)),
        ],
        compiler_params=params,
        cost_estimate=cost(8 * rows * rows * width, 4 * rows * width),
    )(mine, chip_x, write, in_hbm(read_t), read_other, run, run_t, in_hbm(skip_gain[None, :]))

    def fetch(token, *weights):
        return pl.pallas_call(
            fetch_kernel,
            out_shape=tuple(held(weight.shape, weight.dtype) for weight in weights),
            in_specs=[ANY] + [HBM] * len(weights),
            out_specs=(VMEM,) * len(weights),
            scratch_shapes=[pltpu.SemaphoreType.DMA((len(weights),))],
            compiler_params=params,
            cost_estimate=cost(0, 2 * sum(weight.size * 2 for weight in weights)),
        )(token, *(in_hbm(weight) for weight in weights))

    prefix, group = local_out, [group]
    for bit in range(1, bits - 1):
        got = swap(send, bit)
        if bit == 2:
            (dyn,) = fetch(aux, dyn_weight)
            aux, _ = lax.optimization_barrier((aux, dyn))
        goes_on = int(bit < bits - 2)
        prefix, send, aux, *group = pl.pallas_call(
            functools.partial(stage_kernel, bit, bit > 1, head_width),
            out_shape=(
                held((state_size, half), F32),
                payload(2 << bit),
                auxiliary(2 << bit),
            )
            + (held((state_size, half), F32),) * goes_on,
            in_specs=[SMEM] + [VMEM] * 3 + [VMEM if bit > 1 else ANY],
            out_specs=(VMEM,) * (3 + goes_on),
            compiler_params=params,
        )(mine, *group, aux, got, prefix)
    got = swap(send, bits - 1)
    out, act, act_in, noise = fetch(aux, out_weight, act_weight, act_in_weight, step_noise)
    carry, pick = pl.pallas_call(
        functools.partial(last_stage_kernel, bits - 1, rows, head_width, order),
        out_shape=(held((state_size, half), BF16), held((2 * starts, 2 * rows), BF16)),
        in_specs=[SMEM] + [VMEM] * 3 + [ANY],
        out_specs=(VMEM,) * 2,
        compiler_params=params,
    )(mine, prefix, aux, got, act_in)

    block = 2 * cap
    now = starts if direct else 2 * starts
    post, sent = pl.pallas_call(
        after_kernel,
        out_shape=(held((2 * rows, half), BF16), held((now, half), BF16)),
        in_specs=[SMEM] + [VMEM] * 6,
        out_specs=(VMEM,) * 2,
        scratch_shapes=[pltpu.VMEM((2 * rows, half), F32), pltpu.VMEM((2 * rows, half), F32)],
        compiler_params=params,
    )(mine, local_out, read, run, carry, post_gain[None, :], pick)
    shares = (held((rows, half), BF16),) * 2
    if direct:
        given = swap(sent, 0)
        keep, stay, go = pl.pallas_call(
            rest_kernel,
            out_shape=(held((starts, half), BF16),) + shares,
            in_specs=[SMEM, VMEM, VMEM],
            out_specs=(VMEM,) * 3,
            compiler_params=params,
            cost_estimate=cost(4 * starts * rows * half, 2 * rows * width),
        )(mine, post, pick)
        blocks = pl.pallas_call(
            merge_kernel,
            out_shape=(held((block, width), BF16),) * chips,
            in_specs=[SMEM, VMEM, VMEM],
            out_specs=(VMEM,) * chips,
            compiler_params=params,
        )(mine, keep, given)
        landed = [exchange(array, 2 * k) if k else array for array, k in zip(blocks, order)]
    else:
        stay, go = pl.pallas_call(
            share_kernel,
            out_shape=shares,
            in_specs=[SMEM, VMEM],
            out_specs=(VMEM,) * 2,
            compiler_params=params,
        )(mine, post)
        landed = [
            lax.all_to_all(
                sent.reshape(peer_count, block, half), "seq", split_axis=0, concat_axis=0, tiled=True
            ).reshape(chips, 2, block, half)
        ]
    horizon = step_noise.shape[0]
    posterior, values, final_latent = pl.pallas_call(
        imagine_kernel,
        out_shape=(
            jax.ShapeDtypeStruct((rows, width), BF16),
            jax.ShapeDtypeStruct((horizon, starts), F32),
            jax.ShapeDtypeStruct((starts, width), BF16),
        ),
        in_specs=[SMEM] + [VMEM] * (9 + len(landed)),
        out_specs=(HBM, VMEM, VMEM),
        scratch_shapes=[
            pltpu.VMEM((2, starts, width), BF16),
            pltpu.VMEM((starts, dyn_weight.shape[1]), BF16),
            pltpu.SemaphoreType.DMA((2,)),
        ],
        compiler_params=pltpu.CompilerParams(vmem_limit_bytes=16 << 20),
    )(mine, stay, swap(go, 0), perm, noise, act, dyn, act_in, out, value_weight[None, :], *landed)
    return (posterior, values, final_latent)


def solution(mesh):
    whole = P()
    by_row = P(("groups", "seq"), None)
    placed = (
        by_row,
        by_row,
        by_row,
        by_row,
        whole,
        whole,
        P(("groups", "seq")),
        P(None, ("groups", "seq"), None),
        whole,
        whole,
        whole,
        whole,
        whole,
    )
    return jax.shard_map(
        functools.partial(per_device, mesh.shape["seq"]),
        mesh=mesh,
        in_specs=placed,
        out_specs=(by_row, P(None, ("groups", "seq")), by_row),
        check_vma=False,
    )
```

```python
import functools
import jax
import jax.numpy as jnp
from jax import lax
from jax.experimental import pallas as pl
from jax.experimental.pallas import tpu as pltpu
from jax.sharding import PartitionSpec as P

F32 = jnp.float32
BF16 = jnp.bfloat16
LANES = 128
VMEM = pl.BlockSpec(memory_space=pltpu.VMEM)
SMEM = pl.BlockSpec(memory_space=pltpu.SMEM)
HBM = pl.BlockSpec(memory_space=pltpu.HBM)
ANY = pl.BlockSpec(memory_space=pl.ANY)


def iota(shape, dim):
    return lax.broadcasted_iota(jnp.int32, shape, dim)


def mask16(condition):
    return condition.astype(F32).astype(BF16)


def two_heads(cols, pair, head_width, shape):
    first = jnp.broadcast_to(cols[:, 2 * pair : 2 * pair + 1], shape)
    second = jnp.broadcast_to(cols[:, 2 * pair + 1 : 2 * pair + 2], shape)
    return jnp.where(iota(shape, 1) < head_width, first, second)


def stack_rows(rows, count):
    used = sum(row.shape[0] for row in rows)
    if used < count:
        rows = list(rows) + [jnp.zeros((count - used, LANES), F32)]
    return jnp.concatenate(rows, axis=0)


def write_meta(send_ref, decay, wanted, half, state_size):
    high = decay.astype(BF16).astype(F32)
    blocks = (send_ref.shape[1] - half) // LANES
    meta = stack_rows([high, decay - high, wanted], blocks * state_size).astype(BF16)
    for block in range(blocks):
        send_ref[:, half + block * LANES : half + (block + 1) * LANES] = meta[
            block * state_size : (block + 1) * state_size
        ]


def read_meta(got_ref, count, half, state_size):
    blocks = (got_ref.shape[1] - half) // LANES
    meta = jnp.concatenate(
        [got_ref[:, half + block * LANES : half + (block + 1) * LANES].astype(F32) for block in range(blocks)], axis=0
    )
    return meta[0:1] + meta[1:2], meta[2 : 2 + count]


def spread_rows(rows, half, head_width):
    pieces = []
    for row in rows:
        high = row.astype(BF16).astype(F32)
        pieces += [high, row - high]
    expand = mask16(iota((LANES, half), 0) == iota((LANES, half), 1) // head_width)
    wide = jnp.dot(stack_rows(pieces, 16).astype(BF16), expand, preferred_element_type=F32)
    return [wide[2 * k : 2 * k + 1] + wide[2 * k + 1 : 2 * k + 2] for k in range(len(rows))]


def partner_order(chips):
    middle = chips // 2
    far = sorted(range(middle, chips), key=lambda k: (-(k & 1), -k))
    return far, list(range(middle - 1, -1, -1))


def looked_up(index, table):
    found = jnp.zeros_like(index)
    for k, value in enumerate(table):
        if value:
            found = jnp.where(index == k, value, found)
    return found


def requests(start_row, rows, cap):
    starts = start_row.shape[1]
    square = (starts, starts)
    index = jnp.broadcast_to(start_row.astype(F32), square)
    index_t = index.T
    owner = jnp.floor(index * (1.0 / rows))
    owner_t = jnp.floor(index_t * (1.0 / rows))
    earlier = (iota(square, 1) < iota(square, 0)) & (owner == owner_t)
    rank = jnp.sum(earlier.astype(F32), axis=1, keepdims=True)
    perm = (owner_t * cap + rank == iota(square, 1).astype(F32)).astype(F32)
    wanted = jnp.sum(perm * (index_t - owner_t * rows), axis=0, keepdims=True)
    return perm, wanted, owner_t.astype(jnp.int32), rank.astype(jnp.int32)


def own_kernel(
    cap, places, mine_ref, x_hbm, write_hbm, decay_hbm, start_hbm, x_ref, write_ref, sums_ref, perm_ref, wanted_ref,
    decay_ref, start_ref, sems,
):
    core = mine_ref[0] % 2
    rows, half = x_ref.shape
    heads = sums_ref.shape[0]
    lanes_at = pl.multiple_of(core * half, LANES)
    copies = [
        pltpu.make_async_copy(source, target, sems.at[k])
        for k, (source, target) in enumerate(
            (
                (start_hbm, start_ref),
                (decay_hbm, decay_ref),
                (write_hbm, write_ref),
                (x_hbm.at[:, pl.ds(lanes_at, half)], x_ref),
            )
        )
    ]
    for copy in copies:
        copy.start()
    copies[0].wait()
    perm, wanted, owner, rank = requests(start_ref[...], rows, cap)
    if places:
        place = looked_up((owner // 2) ^ (mine_ref[0] // 2), places)
        perm = mask16((place * 2 + owner % 2) * cap + rank == iota(perm.shape, 1))
    perm_ref[...] = perm.astype(BF16)
    wanted_ref[...] = wanted
    copies[1].wait()
    sums_ref[...] = running_sums(jnp.where(core == 0, decay_ref[:heads], decay_ref[heads:]))
    copies[2].wait()
    copies[3].wait()


def running_sums(decays):
    rows = decays.shape[1]
    upper = (iota((rows, rows), 0) <= iota((rows, rows), 1)).astype(F32)
    return jnp.dot(decays, upper, precision=lax.Precision.HIGHEST, preferred_element_type=F32)


def before_kernel(
    cap, mine_ref, x_own_ref, x_other_ref, write_own_ref, write_other_ref, sums_ref, decay_other_ref, wanted_ref,
    start_other_ref, send_ref, ends_ref, x_ref, write_ref, run_ref, run_t_ref, aux_ref,
):
    core = mine_ref[0] % 2
    first = core == 0
    rows, half = x_own_ref.shape
    state_size = write_ref.shape[0]
    heads = run_ref.shape[1]
    head_width = half // heads
    own, other = x_own_ref[...], x_other_ref[:, pl.ds(pl.multiple_of(core * half, LANES), half)]
    x_ref[:rows, :] = jnp.where(first, own, other)
    x_ref[rows:, :] = jnp.where(first, other, own)
    own = sums_ref[...]
    other = running_sums(jnp.where(first, decay_other_ref[:heads], decay_other_ref[heads:]))
    one, two = jnp.where(first, own, other), jnp.where(first, other, own)
    run_t = jnp.concatenate([one, two + one[:, rows - 1 :]], axis=1)
    run_t_ref[...] = run_t
    run = run_t.T
    run_ref[...] = run
    last = run[2 * rows - 1 :]
    tail = jnp.exp(last - run)
    own, other = write_own_ref[...], write_other_ref[...]
    write = jnp.concatenate([jnp.where(first, own, other), jnp.where(first, other, own)], axis=1)
    write_ref[...] = write
    for pair in range(heads // 2):
        lanes = slice(pair * LANES, (pair + 1) * LANES)
        scaled = x_ref[:, lanes].astype(F32) * two_heads(tail, pair, head_width, (2 * rows, LANES))
        ends = jnp.dot(write, scaled.astype(BF16), preferred_element_type=F32)
        ends_ref[:, lanes] = ends
        send_ref[:, lanes] = ends.astype(BF16)
    _, other, _, _ = requests(start_other_ref[...], rows, cap)
    own = wanted_ref[...]
    wanted = jnp.concatenate([jnp.where(first, own, other), jnp.where(first, other, own)], axis=0)
    total = jnp.concatenate([jnp.exp(last), jnp.zeros((1, LANES - heads), F32)], axis=1)
    aux_ref[...] = stack_rows([total, jnp.ones((1, LANES), F32), wanted], aux_ref.shape[0])
    write_meta(send_ref, total, wanted, half, state_size)


def local_kernel(
    mine_ref, x_ref, write_ref, read_hbm, read_other_ref, run_ref, run_t_ref, skip_hbm, out_ref, read_out,
    read_ref, skip_ref, sems,
):
    copies = [
        pltpu.make_async_copy(read_hbm, read_ref, sems.at[0]),
        pltpu.make_async_copy(skip_hbm, skip_ref, sems.at[1]),
    ]
    for copy in copies:
        copy.start()
    for copy in copies:
        copy.wait()
    first = mine_ref[0] % 2 == 0
    rows, half = x_ref.shape[0] // 2, x_ref.shape[1]
    heads = run_ref.shape[1]
    head_width = half // heads
    own, other = read_ref[...], read_other_ref[...]
    read = jnp.concatenate([jnp.where(first, own, other), jnp.where(first, other, own)], axis=1).T
    read_out[...] = read
    gram = jnp.dot(read, write_ref[...], preferred_element_type=F32)
    skip = jnp.where(first, skip_ref[:, :heads], skip_ref[:, heads:])
    mask = iota((rows, rows), 0) >= iota((rows, rows), 1)
    for chunk in range(2):
        at, count = chunk * rows, (chunk + 1) * rows
        lane = iota((count, LANES), 1)
        for pair in range(heads // 2):
            lanes = slice(pair * LANES, (pair + 1) * LANES)
            weights = []
            for head in (2 * pair, 2 * pair + 1):
                for back in range(chunk + 1):
                    seen = slice(back * rows, (back + 1) * rows)
                    spread = run_ref[at:count, head : head + 1] - run_t_ref[head : head + 1, seen]
                    if back == chunk:
                        spread = jnp.where(mask, spread, -jnp.inf)
                    weights.append((jnp.exp(spread) * gram[at:count, seen]).astype(BF16))
            x = x_ref[:count, lanes]
            zero = jnp.zeros_like(x)
            split = jnp.concatenate(
                [jnp.where(lane < head_width, x, zero), jnp.where(lane < head_width, zero, x)], axis=0
            )
            inner = jnp.dot(jnp.concatenate(weights, axis=1), split, preferred_element_type=F32)
            factor = two_heads(skip, pair, head_width, (1, LANES))
            out_ref[at:count, lanes] = inner + factor * x[at:count].astype(F32)


def stage_kernel(bit, has_prefix, head_width, mine_ref, group_ref, aux_ref, got_ref, prefix_ref, prefix_out, send_ref, aux_out, *group_out):
    state_size, half = group_ref.shape
    count = 1 << bit
    later = (mine_ref[0] >> bit) % 2 == 1
    new_decay, new_wanted = read_meta(got_ref, count, half, state_size)
    decay, prefix_decay = aux_ref[0:1], aux_ref[1:2]
    wanted = aux_ref[2 : 2 + count]
    into, across = spread_rows([prefix_decay, jnp.where(later, decay, new_decay)], half, head_width)
    group, got = group_ref[...], got_ref[:, :half].astype(F32)
    moved = into * got
    if has_prefix:
        moved = prefix_ref[...] + moved
        prefix_out[...] = jnp.where(later, moved, prefix_ref[...])
    else:
        prefix_out[...] = jnp.where(later, moved, jnp.zeros_like(moved))
    total = jnp.where(later, got, group) * across + jnp.where(later, group, got)
    for ref in group_out:
        ref[...] = total
    send_ref[:, :half] = total.astype(BF16)
    wanted = jnp.concatenate(
        [jnp.where(later, new_wanted, wanted), jnp.where(later, wanted, new_wanted)], axis=0
    )
    write_meta(send_ref, decay * new_decay, wanted, half, state_size)
    aux_out[...] = stack_rows(
        [decay * new_decay, jnp.where(later, prefix_decay * new_decay, prefix_decay), wanted], aux_out.shape[0]
    )


def last_stage_kernel(bit, rows, head_width, order, mine_ref, prefix_ref, aux_ref, got_ref, token_ref, carry_ref, pick_ref):
    state_size, half = prefix_ref.shape
    count = 1 << bit
    mine = mine_ref[0]
    later = (mine >> bit) % 2 == 1
    _, new_wanted = read_meta(got_ref, count, half, state_size)
    (into,) = spread_rows([aux_ref[1:2]], half, head_width)
    prefix = prefix_ref[...]
    carry_ref[...] = jnp.where(later, prefix + into * got_ref[:, :half].astype(F32), prefix).astype(BF16)
    wanted = aux_ref[2 : 2 + count]
    wanted = jnp.concatenate(
        [jnp.where(later, new_wanted, wanted), jnp.where(later, wanted, new_wanted)], axis=0
    )
    peers = 2 * count
    picks = pick_ref.shape[0]
    both = picks // peers
    table = stack_rows([wanted], LANES) if peers < LANES else wanted
    device = iota((picks, LANES), 0) // both
    if order:
        chip = looked_up(device % len(order), order) ^ (mine // 2)
        device = chip * 2 + (device // len(order) + mine) % 2
    asker = mask16(device == iota((picks, LANES), 1))
    by_slot = jnp.dot(asker, table.astype(BF16), preferred_element_type=F32)
    turn = iota((picks, LANES), 0) % both
    here = iota((picks, LANES), 1) == (mine // 2) * both + turn
    asked = jnp.sum(jnp.where(here, by_slot + ((turn // (both // 2)) * rows).astype(F32), 0.0), axis=1, keepdims=True)
    pick_ref[...] = mask16(asked == iota(pick_ref.shape, 1).astype(F32))


def normalize(mine_ref, local_ref, read_ref, run_ref, carry_ref, gain_ref, mixed_ref, total_ref, post_ref):
    core = mine_ref[0] % 2
    rows, half = local_ref.shape
    heads = run_ref.shape[1]
    head_width = half // heads
    entered = jnp.exp(run_ref[...])
    square = (LANES, LANES)
    same_head = mask16(iota(square, 0) // head_width == iota(square, 1) // head_width)
    gain = jnp.where(core == 0, gain_ref[:, :half], gain_ref[:, half:])
    blocks = [slice(k * LANES, (k + 1) * LANES) for k in range(half // LANES)]
    total_ref[...] = jnp.dot(read_ref[...], carry_ref[...], preferred_element_type=F32)
    for pair, lanes in enumerate(blocks):
        mixed_ref[:, lanes] = local_ref[:, lanes] + total_ref[:, lanes] * two_heads(
            entered, pair, head_width, (rows, LANES)
        )
    for lanes in blocks:
        mixed = mixed_ref[:, lanes]
        squares = mixed * mixed
        high = squares.astype(BF16)
        low = (squares - high.astype(F32)).astype(BF16)
        total_ref[:, lanes] = jnp.dot(high, same_head, preferred_element_type=F32) + jnp.dot(
            low, same_head, preferred_element_type=F32
        )
    for lanes in blocks:
        scale = lax.rsqrt(total_ref[:, lanes] * (1.0 / head_width) + 1e-05)
        post_ref[:, lanes] = (mixed_ref[:, lanes] * scale * gain[:, lanes]).astype(BF16)


def picked_rows(pick, post_ref):
    return jnp.dot(pick, post_ref[...], preferred_element_type=F32).astype(BF16)


def after_kernel(
    mine_ref, local_ref, read_ref, run_ref, carry_ref, gain_ref, pick_ref, post_ref, sent_ref, mixed_ref, total_ref
):
    normalize(mine_ref, local_ref, read_ref, run_ref, carry_ref, gain_ref, mixed_ref, total_ref, post_ref)
    count = sent_ref.shape[0]
    first = 0 if count == pick_ref.shape[0] else pick_ref.shape[0] // 2
    sent_ref[...] = picked_rows(pick_ref[first : first + count, :], post_ref)


def share_kernel(mine_ref, post_ref, stay_ref, go_ref):
    core = mine_ref[0] % 2
    rows = stay_ref.shape[0]
    stay_ref[...] = post_ref[pl.ds(pl.multiple_of(core * rows, rows), rows), :]
    go_ref[...] = post_ref[pl.ds(pl.multiple_of((1 - core) * rows, rows), rows), :]


def rest_kernel(mine_ref, post_ref, pick_ref, keep_ref, stay_ref, go_ref):
    keep_ref[...] = picked_rows(pick_ref[: keep_ref.shape[0], :], post_ref)
    share_kernel(mine_ref, post_ref, stay_ref, go_ref)


def merge_kernel(mine_ref, keep_ref, got_ref, *block_refs):
    first = mine_ref[0] % 2 == 0
    half = keep_ref.shape[1]
    keep, got = keep_ref[...], got_ref[...]
    left, right = jnp.where(first, keep, got), jnp.where(first, got, keep)
    size = block_refs[0].shape[0]
    for k, ref in enumerate(block_refs):
        ref[:, :half] = left[k * size : (k + 1) * size]
        ref[:, half:] = right[k * size : (k + 1) * size]


def fetch_kernel(token_ref, *refs):
    count = (len(refs) - 1) // 2
    sems = refs[-1]
    copies = [pltpu.make_async_copy(refs[k], refs[count + k], sems.at[k]) for k in range(count)]
    for copy in copies:
        copy.start()
    for copy in copies:
        copy.wait()


def folded(array):
    total = array[:, :LANES]
    for k in range(1, array.shape[1] // LANES):
        total = total + array[:, k * LANES : (k + 1) * LANES]
    return total


def imagined_steps(held_refs, squares, noise_ref, act_ref, dyn_ref, act_in_ref, out_ref, value_ref, hidden_ref, steps):
    width, inside = dyn_ref.shape
    chunk = 256
    columns = []
    for step in steps:
        latent_ref, next_ref = held_refs
        scale = lax.rsqrt(jnp.sum(squares, axis=1, keepdims=True) * (1.0 / width) + 1e-06)
        latent = latent_ref[...]
        action = jnp.dot(latent, act_ref[...], preferred_element_type=F32)
        action = jnp.tanh(action * scale).astype(BF16)
        value = None
        for at in range(0, inside, chunk):
            part = slice(at, at + chunk)
            inner = jnp.dot(latent, dyn_ref[:, part], preferred_element_type=F32) * scale + jnp.dot(
                action, act_in_ref[:, part], preferred_element_type=F32
            )
            hidden = (inner / (1.0 + jnp.exp(-inner)) + noise_ref[step, :, part].astype(F32)).astype(BF16)
            hidden_ref[:, part] = hidden
            worth = folded(hidden.astype(F32) * value_ref[:, part].astype(F32))
            value = worth if value is None else value + worth
        columns.append(jnp.sum(value, axis=1, keepdims=True))
        hidden = hidden_ref[...]
        squares = None
        for at in range(0, width, chunk):
            part = slice(at, at + chunk)
            moved = latent_ref[:, part].astype(F32) + jnp.dot(hidden, out_ref[:, part], preferred_element_type=F32)
            rounded = moved.astype(BF16)
            next_ref[:, part] = rounded
            wide = rounded.astype(F32)
            square = folded(wide * wide)
            squares = square if squares is None else squares + square
        held_refs = (next_ref, latent_ref)
    return held_refs, squares, columns


def imagine_kernel(
    mine_ref, stay_ref, got_ref, perm_ref, noise_ref, act_ref, dyn_ref, act_in_ref, out_ref, value_ref, *refs
):
    *landed_refs, post_hbm, values_ref, final_ref, spare_ref, hidden_ref, sems = refs
    core = mine_ref[0] % 2
    half = stay_ref.shape[1]
    copies = [
        pltpu.make_async_copy(source, post_hbm.at[:, pl.ds(pl.multiple_of(side * half, LANES), half)], sems.at[k])
        for k, (source, side) in enumerate(((stay_ref, core), (got_ref, 1 - core)))
    ]
    for copy in copies:
        copy.start()
    starts = perm_ref.shape[0]
    perm = perm_ref[...]
    squares = None
    for side in range(2):
        lanes = slice(side * half, (side + 1) * half)
        if len(landed_refs) == 1:
            landed = landed_refs[0][:, side].reshape(starts, half)
        else:
            landed = jnp.concatenate([ref[:, lanes] for ref in landed_refs], axis=0)
        wide = jnp.dot(perm, landed, preferred_element_type=F32)
        spare_ref[1, :, lanes] = wide.astype(BF16)
        square = folded(wide * wide)
        squares = square if squares is None else squares + square
    horizon = noise_ref.shape[0]
    refs, columns = (spare_ref.at[1], None), []
    for step in range(horizon):
        target = final_ref if step == horizon - 1 else spare_ref.at[step % 2]
        refs, squares, new = imagined_steps(
            (refs[0], target),
            squares,
            noise_ref,
            act_ref,
            dyn_ref,
            act_in_ref,
            out_ref,
            value_ref,
            hidden_ref,
            range(step, step + 1),
        )
        columns += new
    lane = iota((starts, LANES), 1)
    table = jnp.zeros((starts, LANES), F32)
    for k, column in enumerate(columns):
        table = jnp.where(lane == k, column, table)
    values_ref[...] = table.T[:horizon]
    for copy in copies:
        copy.wait()


def cost(flops, read):
    return pl.CostEstimate(flops=flops, bytes_accessed=read, transcendentals=0)


def in_hbm(array):
    return pltpu.with_memory_space_constraint(array, pltpu.HBM)


def per_device(
    peer_count,
    features,
    state_write,
    state_read,
    log_decay,
    skip_gain,
    post_gain,
    start_index,
    step_noise,
    act_weight,
    dyn_weight,
    act_in_weight,
    out_weight,
    value_weight,
):
    rows, width = features.shape
    head_count = log_decay.shape[1]
    head_width = width // head_count
    state_size = state_write.shape[1]
    half = width // 2
    heads = head_count // 2
    starts = start_index.shape[0]
    cap = starts // peer_count
    bits = peer_count.bit_length() - 1
    mine = lax.axis_index("seq").reshape(1)
    params = pltpu.CompilerParams(vmem_limit_bytes=12 << 20)
    held = pltpu.VMEM

    chips = peer_count // 2
    direct = chips <= 8 and cap % 8 == 0
    far, near = partner_order(chips) if direct else ([], [])
    order = far + near
    places = [order.index(k) for k in range(len(order))]

    def exchange(array, mask):
        return lax.ppermute(array, "seq", [(i, i ^ mask) for i in range(peer_count)])

    def swap(array, bit):
        return exchange(array, 1 << bit)

    def payload(count):
        blocks = -(-(2 + count) // state_size)
        return held((state_size, half + blocks * LANES), BF16)

    def auxiliary(count):
        return held((-(-(2 + count) // 8) * 8, LANES), F32)

    write_t, read_t, decay_t = state_write.T, state_read.T, log_decay.T
    start_row = start_index.reshape(1, starts)
    x_other = swap(features, 0)
    decay_other, write_other = swap(decay_t, 0), swap(write_t, 0)
    start_other, read_other = swap(start_row, 0), swap(read_t, 0)

    x_own, write_own, sums, perm, wanted = pl.pallas_call(
        functools.partial(own_kernel, cap, places),
        out_shape=(
            held((rows, half), BF16),
            held((state_size, rows), BF16),
            held((heads, rows), F32),
            held((starts, starts), BF16),
            held((1, starts), F32),
        ),
        in_specs=[SMEM] + [HBM] * 4,
        out_specs=(VMEM,) * 5,
        scratch_shapes=[
            pltpu.VMEM((head_count, rows), F32),
            pltpu.VMEM((1, starts), jnp.int32),
            pltpu.SemaphoreType.DMA((4,)),
        ],
        compiler_params=params,
        cost_estimate=cost(0, 4 * rows * width),
    )(mine, in_hbm(features), in_hbm(write_t), in_hbm(decay_t), in_hbm(start_row))

    send, group, chip_x, write, run, run_t, aux = pl.pallas_call(
        functools.partial(before_kernel, cap),
        out_shape=(
            payload(2),
            held((state_size, half), F32),
            held((2 * rows, half), BF16),
            held((state_size, 2 * rows), BF16),
            held((2 * rows, heads), F32),
            held((heads, 2 * rows), F32),
            auxiliary(2),
        ),
        in_specs=[SMEM] + [VMEM] * 8,
        out_specs=(VMEM,) * 7,
        compiler_params=params,
    )(mine, x_own, x_other, write_own, write_other, sums, decay_other, wanted, start_other)

    local_out, read = pl.pallas_call(
        local_kernel,
        out_shape=(held((2 * rows, half), F32), held((2 * rows, state_size), BF16)),
        in_specs=[SMEM, VMEM, VMEM, HBM, VMEM, VMEM, VMEM, HBM],
        out_specs=(VMEM, VMEM),
        scratch_shapes=[
            pltpu.VMEM((state_size, rows), BF16),
            pltpu.VMEM((1, head_count), F32),
            pltpu.SemaphoreType.DMA((2,)),
        ],
        compiler_params=params,
        cost_estimate=cost(8 * rows * rows * width, 4 * rows * width),
    )(mine, chip_x, write, in_hbm(read_t), read_other, run, run_t, in_hbm(skip_gain[None, :]))

    def fetch(token, *weights):
        return pl.pallas_call(
            fetch_kernel,
            out_shape=tuple(held(weight.shape, weight.dtype) for weight in weights),
            in_specs=[ANY] + [HBM] * len(weights),
            out_specs=(VMEM,) * len(weights),
            scratch_shapes=[pltpu.SemaphoreType.DMA((len(weights),))],
            compiler_params=params,
            cost_estimate=cost(0, 2 * sum(weight.size * 2 for weight in weights)),
        )(token, *(in_hbm(weight) for weight in weights))

    prefix, group = local_out, [group]
    for bit in range(1, bits - 1):
        got = swap(send, bit)
        if bit == 2:
            (dyn,) = fetch(aux, dyn_weight)
            aux, _ = lax.optimization_barrier((aux, dyn))
        goes_on = int(bit < bits - 2)
        prefix, send, aux, *group = pl.pallas_call(
            functools.partial(stage_kernel, bit, bit > 1, head_width),
            out_shape=(
                held((state_size, half), F32),
                payload(2 << bit),
                auxiliary(2 << bit),
            )
            + (held((state_size, half), F32),) * goes_on,
            in_specs=[SMEM] + [VMEM] * 3 + [VMEM if bit > 1 else ANY],
            out_specs=(VMEM,) * (3 + goes_on),
            compiler_params=params,
        )(mine, *group, aux, got, prefix)
    got = swap(send, bits - 1)
    out, act, act_in, noise = fetch(aux, out_weight, act_weight, act_in_weight, step_noise)
    carry, pick = pl.pallas_call(
        functools.partial(last_stage_kernel, bits - 1, rows, head_width, order),
        out_shape=(held((state_size, half), BF16), held((2 * starts, 2 * rows), BF16)),
        in_specs=[SMEM] + [VMEM] * 3 + [ANY],
        out_specs=(VMEM,) * 2,
        compiler_params=params,
    )(mine, prefix, aux, got, act_in)

    block = 2 * cap
    now = starts if direct else 2 * starts
    post, sent = pl.pallas_call(
        after_kernel,
        out_shape=(held((2 * rows, half), BF16), held((now, half), BF16)),
        in_specs=[SMEM] + [VMEM] * 6,
        out_specs=(VMEM,) * 2,
        scratch_shapes=[pltpu.VMEM((2 * rows, half), F32), pltpu.VMEM((2 * rows, half), F32)],
        compiler_params=params,
    )(mine, local_out, read, run, carry, post_gain[None, :], pick)
    shares = (held((rows, half), BF16),) * 2
    if direct:
        given = swap(sent, 0)
        keep, stay, go = pl.pallas_call(
            rest_kernel,
            out_shape=(held((starts, half), BF16),) + shares,
            in_specs=[SMEM, VMEM, VMEM],
            out_specs=(VMEM,) * 3,
            compiler_params=params,
            cost_estimate=cost(4 * starts * rows * half, 2 * rows * width),
        )(mine, post, pick)
        blocks = pl.pallas_call(
            merge_kernel,
            out_shape=(held((block, width), BF16),) * chips,
            in_specs=[SMEM, VMEM, VMEM],
            out_specs=(VMEM,) * chips,
            compiler_params=params,
        )(mine, keep, given)
        landed = [exchange(array, 2 * k) if k else array for array, k in zip(blocks, order)]
    else:
        stay, go = pl.pallas_call(
            share_kernel,
            out_shape=shares,
            in_specs=[SMEM, VMEM],
            out_specs=(VMEM,) * 2,
            compiler_params=params,
        )(mine, post)
        landed = [
            lax.all_to_all(
                sent.reshape(peer_count, block, half), "seq", split_axis=0, concat_axis=0, tiled=True
            ).reshape(chips, 2, block, half)
        ]
    horizon = step_noise.shape[0]
    posterior, values, final_latent = pl.pallas_call(
        imagine_kernel,
        out_shape=(
            jax.ShapeDtypeStruct((rows, width), BF16),
            jax.ShapeDtypeStruct((horizon, starts), F32),
            jax.ShapeDtypeStruct((starts, width), BF16),
        ),
        in_specs=[SMEM] + [VMEM] * (9 + len(landed)),
        out_specs=(HBM, VMEM, VMEM),
        scratch_shapes=[
            pltpu.VMEM((2, starts, width), BF16),
            pltpu.VMEM((starts, dyn_weight.shape[1]), BF16),
            pltpu.SemaphoreType.DMA((2,)),
        ],
        compiler_params=pltpu.CompilerParams(vmem_limit_bytes=16 << 20),
    )(mine, stay, swap(go, 0), perm, noise, act, dyn, act_in, out, value_weight[None, :], *landed)
    return (posterior, values, final_latent)


def solution(mesh):
    whole = P()
    by_row = P(("groups", "seq"), None)
    placed = (
        by_row,
        by_row,
        by_row,
        by_row,
        whole,
        whole,
        P(("groups", "seq")),
        P(None, ("groups", "seq"), None),
        whole,
        whole,
        whole,
        whole,
        whole,
    )
    return jax.shard_map(
        functools.partial(per_device, mesh.shape["seq"]),
        mesh=mesh,
        in_specs=placed,
        out_specs=(by_row, P(None, ("groups", "seq")), by_row),
        check_vma=False,
    )
```

```python
import functools
import jax
import jax.numpy as jnp
from jax import lax
from jax.experimental import pallas as pl
from jax.experimental.pallas import tpu as pltpu
from jax.sharding import PartitionSpec as P

F32 = jnp.float32
BF16 = jnp.bfloat16
LANES = 128
VMEM = pl.BlockSpec(memory_space=pltpu.VMEM)
SMEM = pl.BlockSpec(memory_space=pltpu.SMEM)
HBM = pl.BlockSpec(memory_space=pltpu.HBM)
ANY = pl.BlockSpec(memory_space=pl.ANY)


def iota(shape, dim):
    return lax.broadcasted_iota(jnp.int32, shape, dim)


def mask16(condition):
    return condition.astype(F32).astype(BF16)


def two_heads(cols, pair, head_width, shape):
    first = jnp.broadcast_to(cols[:, 2 * pair : 2 * pair + 1], shape)
    second = jnp.broadcast_to(cols[:, 2 * pair + 1 : 2 * pair + 2], shape)
    return jnp.where(iota(shape, 1) < head_width, first, second)


def stack_rows(rows, count):
    used = sum(row.shape[0] for row in rows)
    if used < count:
        rows = list(rows) + [jnp.zeros((count - used, LANES), F32)]
    return jnp.concatenate(rows, axis=0)


def write_meta(send_ref, decay, wanted, half, state_size):
    high = decay.astype(BF16).astype(F32)
    blocks = (send_ref.shape[1] - half) // LANES
    meta = stack_rows([high, decay - high, wanted], blocks * state_size).astype(BF16)
    for block in range(blocks):
        send_ref[:, half + block * LANES : half + (block + 1) * LANES] = meta[
            block * state_size : (block + 1) * state_size
        ]


def read_meta(got_ref, count, half, state_size):
    blocks = (got_ref.shape[1] - half) // LANES
    meta = jnp.concatenate(
        [got_ref[:, half + block * LANES : half + (block + 1) * LANES].astype(F32) for block in range(blocks)], axis=0
    )
    return meta[0:1] + meta[1:2], meta[2 : 2 + count]


def spread_rows(rows, half, head_width):
    pieces = []
    for row in rows:
        high = row.astype(BF16).astype(F32)
        pieces += [high, row - high]
    expand = mask16(iota((LANES, half), 0) == iota((LANES, half), 1) // head_width)
    wide = jnp.dot(stack_rows(pieces, 16).astype(BF16), expand, preferred_element_type=F32)
    return [wide[2 * k : 2 * k + 1] + wide[2 * k + 1 : 2 * k + 2] for k in range(len(rows))]


def partner_order(chips):
    middle = chips // 2
    far = sorted(range(middle, chips), key=lambda k: (-(k & 1), -k))
    return far, list(range(middle - 1, -1, -1))


def looked_up(index, table):
    found = jnp.zeros_like(index)
    for k, value in enumerate(table):
        if value:
            found = jnp.where(index == k, value, found)
    return found


def requests(start_row, rows, cap):
    starts = start_row.shape[1]
    square = (starts, starts)
    index = jnp.broadcast_to(start_row.astype(F32), square)
    index_t = index.T
    owner = jnp.floor(index * (1.0 / rows))
    owner_t = jnp.floor(index_t * (1.0 / rows))
    earlier = (iota(square, 1) < iota(square, 0)) & (owner == owner_t)
    rank = jnp.sum(earlier.astype(F32), axis=1, keepdims=True)
    perm = (owner_t * cap + rank == iota(square, 1).astype(F32)).astype(F32)
    wanted = jnp.sum(perm * (index_t - owner_t * rows), axis=0, keepdims=True)
    return perm, wanted, owner_t.astype(jnp.int32), rank.astype(jnp.int32)


def own_kernel(
    cap, places, mine_ref, x_hbm, write_hbm, decay_hbm, start_hbm, x_ref, write_ref, sums_ref, perm_ref, wanted_ref,
    decay_ref, start_ref, sems,
):
    core = mine_ref[0] % 2
    rows, half = x_ref.shape
    heads = sums_ref.shape[0]
    lanes_at = pl.multiple_of(core * half, LANES)
    copies = [
        pltpu.make_async_copy(source, target, sems.at[k])
        for k, (source, target) in enumerate(
            (
                (start_hbm, start_ref),
                (decay_hbm, decay_ref),
                (write_hbm, write_ref),
                (x_hbm.at[:, pl.ds(lanes_at, half)], x_ref),
            )
        )
    ]
    for copy in copies:
        copy.start()
    copies[0].wait()
    perm, wanted, owner, rank = requests(start_ref[...], rows, cap)
    if places:
        place = looked_up((owner // 2) ^ (mine_ref[0] // 2), places)
        perm = mask16((place * 2 + owner % 2) * cap + rank == iota(perm.shape, 1))
    perm_ref[...] = perm.astype(BF16)
    wanted_ref[...] = wanted
    copies[1].wait()
    sums_ref[...] = running_sums(jnp.where(core == 0, decay_ref[:heads], decay_ref[heads:]))
    copies[2].wait()
    copies[3].wait()


def running_sums(decays):
    rows = decays.shape[1]
    upper = (iota((rows, rows), 0) <= iota((rows, rows), 1)).astype(F32)
    return jnp.dot(decays, upper, precision=lax.Precision.HIGHEST, preferred_element_type=F32)


def before_kernel(
    cap, mine_ref, x_own_ref, x_other_ref, write_own_ref, write_other_ref, sums_ref, decay_other_ref, wanted_ref,
    start_other_ref, send_ref, ends_ref, x_ref, write_ref, run_ref, run_t_ref, aux_ref,
):
    core = mine_ref[0] % 2
    first = core == 0
    rows, half = x_own_ref.shape
    state_size = write_ref.shape[0]
    heads = run_ref.shape[1]
    head_width = half // heads
    own, other = x_own_ref[...], x_other_ref[:, pl.ds(pl.multiple_of(core * half, LANES), half)]
    x_ref[:rows, :] = jnp.where(first, own, other)
    x_ref[rows:, :] = jnp.where(first, other, own)
    own = sums_ref[...]
    other = running_sums(jnp.where(first, decay_other_ref[:heads], decay_other_ref[heads:]))
    one, two = jnp.where(first, own, other), jnp.where(first, other, own)
    run_t = jnp.concatenate([one, two + one[:, rows - 1 :]], axis=1)
    run_t_ref[...] = run_t
    run = run_t.T
    run_ref[...] = run
    last = run[2 * rows - 1 :]
    tail = jnp.exp(last - run)
    own, other = write_own_ref[...], write_other_ref[...]
    write = jnp.concatenate([jnp.where(first, own, other), jnp.where(first, other, own)], axis=1)
    write_ref[...] = write
    for pair in range(heads // 2):
        lanes = slice(pair * LANES, (pair + 1) * LANES)
        scaled = x_ref[:, lanes].astype(F32) * two_heads(tail, pair, head_width, (2 * rows, LANES))
        ends = jnp.dot(write, scaled.astype(BF16), preferred_element_type=F32)
        ends_ref[:, lanes] = ends
        send_ref[:, lanes] = ends.astype(BF16)
    _, other, _, _ = requests(start_other_ref[...], rows, cap)
    own = wanted_ref[...]
    wanted = jnp.concatenate([jnp.where(first, own, other), jnp.where(first, other, own)], axis=0)
    total = jnp.concatenate([jnp.exp(last), jnp.zeros((1, LANES - heads), F32)], axis=1)
    aux_ref[...] = stack_rows([total, jnp.ones((1, LANES), F32), wanted], aux_ref.shape[0])
    write_meta(send_ref, total, wanted, half, state_size)


def local_kernel(
    mine_ref, x_ref, write_ref, read_hbm, read_other_ref, run_ref, run_t_ref, skip_hbm, out_ref, read_out,
    read_ref, skip_ref, sems,
):
    copies = [
        pltpu.make_async_copy(read_hbm, read_ref, sems.at[0]),
        pltpu.make_async_copy(skip_hbm, skip_ref, sems.at[1]),
    ]
    for copy in copies:
        copy.start()
    for copy in copies:
        copy.wait()
    first = mine_ref[0] % 2 == 0
    rows, half = x_ref.shape[0] // 2, x_ref.shape[1]
    heads = run_ref.shape[1]
    head_width = half // heads
    own, other = read_ref[...], read_other_ref[...]
    read = jnp.concatenate([jnp.where(first, own, other), jnp.where(first, other, own)], axis=1).T
    read_out[...] = read
    gram = jnp.dot(read, write_ref[...], preferred_element_type=F32)
    skip = jnp.where(first, skip_ref[:, :heads], skip_ref[:, heads:])
    mask = iota((rows, rows), 0) >= iota((rows, rows), 1)
    for chunk in range(2):
        at, count = chunk * rows, (chunk + 1) * rows
        lane = iota((count, LANES), 1)
        for pair in range(heads // 2):
            lanes = slice(pair * LANES, (pair + 1) * LANES)
            weights = []
            for head in (2 * pair, 2 * pair + 1):
                for back in range(chunk + 1):
                    seen = slice(back * rows, (back + 1) * rows)
                    spread = run_ref[at:count, head : head + 1] - run_t_ref[head : head + 1, seen]
                    if back == chunk:
                        spread = jnp.where(mask, spread, -jnp.inf)
                    weights.append((jnp.exp(spread) * gram[at:count, seen]).astype(BF16))
            x = x_ref[:count, lanes]
            zero = jnp.zeros_like(x)
            split = jnp.concatenate(
                [jnp.where(lane < head_width, x, zero), jnp.where(lane < head_width, zero, x)], axis=0
            )
            inner = jnp.dot(jnp.concatenate(weights, axis=1), split, preferred_element_type=F32)
            factor = two_heads(skip, pair, head_width, (1, LANES))
            out_ref[at:count, lanes] = inner + factor * x[at:count].astype(F32)


def stage_kernel(bit, has_prefix, head_width, mine_ref, group_ref, aux_ref, got_ref, prefix_ref, prefix_out, send_ref, aux_out, *group_out):
    state_size, half = group_ref.shape
    count = 1 << bit
    later = (mine_ref[0] >> bit) % 2 == 1
    new_decay, new_wanted = read_meta(got_ref, count, half, state_size)
    decay, prefix_decay = aux_ref[0:1], aux_ref[1:2]
    wanted = aux_ref[2 : 2 + count]
    into, across = spread_rows([prefix_decay, jnp.where(later, decay, new_decay)], half, head_width)
    group, got = group_ref[...], got_ref[:, :half].astype(F32)
    moved = into * got
    if has_prefix:
        moved = prefix_ref[...] + moved
        prefix_out[...] = jnp.where(later, moved, prefix_ref[...])
    else:
        prefix_out[...] = jnp.where(later, moved, jnp.zeros_like(moved))
    total = jnp.where(later, got, group) * across + jnp.where(later, group, got)
    for ref in group_out:
        ref[...] = total
    send_ref[:, :half] = total.astype(BF16)
    wanted = jnp.concatenate(
        [jnp.where(later, new_wanted, wanted), jnp.where(later, wanted, new_wanted)], axis=0
    )
    write_meta(send_ref, decay * new_decay, wanted, half, state_size)
    aux_out[...] = stack_rows(
        [decay * new_decay, jnp.where(later, prefix_decay * new_decay, prefix_decay), wanted], aux_out.shape[0]
    )


def last_stage(bit, rows, head_width, order, mine_ref, prefix_ref, aux_ref, got_ref, carry_ref, pick_ref):
    state_size, half = prefix_ref.shape
    count = 1 << bit
    mine = mine_ref[0]
    later = (mine >> bit) % 2 == 1
    _, new_wanted = read_meta(got_ref, count, half, state_size)
    (into,) = spread_rows([aux_ref[1:2]], half, head_width)
    prefix = prefix_ref[...]
    carry_ref[...] = jnp.where(later, prefix + into * got_ref[:, :half].astype(F32), prefix).astype(BF16)
    wanted = aux_ref[2 : 2 + count]
    wanted = jnp.concatenate(
        [jnp.where(later, new_wanted, wanted), jnp.where(later, wanted, new_wanted)], axis=0
    )
    peers = 2 * count
    picks = pick_ref.shape[0]
    both = picks // peers
    table = stack_rows([wanted], LANES) if peers < LANES else wanted
    device = iota((picks, LANES), 0) // both
    if order:
        chip = looked_up(device % len(order), order) ^ (mine // 2)
        device = chip * 2 + (device // len(order) + mine) % 2
    asker = mask16(device == iota((picks, LANES), 1))
    by_slot = jnp.dot(asker, table.astype(BF16), preferred_element_type=F32)
    turn = iota((picks, LANES), 0) % both
    here = iota((picks, LANES), 1) == (mine // 2) * both + turn
    asked = jnp.sum(jnp.where(here, by_slot + ((turn // (both // 2)) * rows).astype(F32), 0.0), axis=1, keepdims=True)
    pick_ref[...] = mask16(asked == iota(pick_ref.shape, 1).astype(F32))


def normalize(mine_ref, local_ref, read_ref, run_ref, carry_ref, gain_ref, mixed_ref, total_ref, post_ref):
    core = mine_ref[0] % 2
    rows, half = local_ref.shape
    heads = run_ref.shape[1]
    head_width = half // heads
    entered = jnp.exp(run_ref[...])
    square = (LANES, LANES)
    same_head = mask16(iota(square, 0) // head_width == iota(square, 1) // head_width)
    gain = jnp.where(core == 0, gain_ref[:, :half], gain_ref[:, half:])
    blocks = [slice(k * LANES, (k + 1) * LANES) for k in range(half // LANES)]
    total_ref[...] = jnp.dot(read_ref[...], carry_ref[...], preferred_element_type=F32)
    for pair, lanes in enumerate(blocks):
        mixed_ref[:, lanes] = local_ref[:, lanes] + total_ref[:, lanes] * two_heads(
            entered, pair, head_width, (rows, LANES)
        )
    for lanes in blocks:
        mixed = mixed_ref[:, lanes]
        squares = mixed * mixed
        high = squares.astype(BF16)
        low = (squares - high.astype(F32)).astype(BF16)
        total_ref[:, lanes] = jnp.dot(high, same_head, preferred_element_type=F32) + jnp.dot(
            low, same_head, preferred_element_type=F32
        )
    for lanes in blocks:
        scale = lax.rsqrt(total_ref[:, lanes] * (1.0 / head_width) + 1e-05)
        post_ref[:, lanes] = (mixed_ref[:, lanes] * scale * gain[:, lanes]).astype(BF16)


def picked_rows(pick, post_ref):
    return jnp.dot(pick, post_ref[...], preferred_element_type=F32).astype(BF16)


def after_kernel(
    bit, order, mine_ref, prefix_ref, aux_ref, arrived_ref, token_ref, local_ref, read_ref, run_ref, gain_ref,
    pick_ref, post_ref, sent_ref, carry_ref, mixed_ref, total_ref,
):
    rows, half = local_ref.shape
    last_stage(
        bit, rows // 2, half // run_ref.shape[1], order, mine_ref, prefix_ref, aux_ref, arrived_ref, carry_ref, pick_ref
    )
    normalize(mine_ref, local_ref, read_ref, run_ref, carry_ref, gain_ref, mixed_ref, total_ref, post_ref)
    count = sent_ref.shape[0]
    first = 0 if count == pick_ref.shape[0] else pick_ref.shape[0] // 2
    sent_ref[...] = picked_rows(pick_ref[first : first + count, :], post_ref)


def share_kernel(mine_ref, post_ref, stay_ref, go_ref):
    core = mine_ref[0] % 2
    rows = stay_ref.shape[0]
    stay_ref[...] = post_ref[pl.ds(pl.multiple_of(core * rows, rows), rows), :]
    go_ref[...] = post_ref[pl.ds(pl.multiple_of((1 - core) * rows, rows), rows), :]


def rest_kernel(mine_ref, post_ref, pick_ref, keep_ref, stay_ref, go_ref):
    keep_ref[...] = picked_rows(pick_ref[: keep_ref.shape[0], :], post_ref)
    share_kernel(mine_ref, post_ref, stay_ref, go_ref)


def merge_kernel(mine_ref, keep_ref, got_ref, *block_refs):
    first = mine_ref[0] % 2 == 0
    half = keep_ref.shape[1]
    keep, got = keep_ref[...], got_ref[...]
    left, right = jnp.where(first, keep, got), jnp.where(first, got, keep)
    size = block_refs[0].shape[0]
    for k, ref in enumerate(block_refs):
        ref[:, :half] = left[k * size : (k + 1) * size]
        ref[:, half:] = right[k * size : (k + 1) * size]


def fetch_kernel(token_ref, *refs):
    count = (len(refs) - 1) // 2
    sems = refs[-1]
    copies = [pltpu.make_async_copy(refs[k], refs[count + k], sems.at[k]) for k in range(count)]
    for copy in copies:
        copy.start()
    for copy in copies:
        copy.wait()


def folded(array):
    total = array[:, :LANES]
    for k in range(1, array.shape[1] // LANES):
        total = total + array[:, k * LANES : (k + 1) * LANES]
    return total


def imagined_steps(held_refs, squares, noise_ref, act_ref, dyn_ref, act_in_ref, out_ref, value_ref, hidden_ref, steps, emit=None, announce=None):
    width, inside = dyn_ref.shape
    chunk = 256
    columns = []
    for step in steps:
        latent_ref, next_ref = held_refs
        scale = lax.rsqrt(jnp.sum(squares, axis=1, keepdims=True) * (1.0 / width) + 1e-06)
        latent = latent_ref[...]
        action = jnp.dot(latent, act_ref[...], preferred_element_type=F32)
        action = jnp.tanh(action * scale).astype(BF16)
        value = None
        for at in range(0, inside, chunk):
            part = slice(at, at + chunk)
            inner = jnp.dot(latent, dyn_ref[:, part], preferred_element_type=F32) * scale + jnp.dot(
                action, act_in_ref[:, part], preferred_element_type=F32
            )
            hidden = (inner / (1.0 + jnp.exp(-inner)) + noise_ref[step, :, part].astype(F32)).astype(BF16)
            hidden_ref[:, part] = hidden
            worth = folded(hidden.astype(F32) * value_ref[:, part].astype(F32))
            value = worth if value is None else value + worth
        columns.append(jnp.sum(value, axis=1, keepdims=True))
        if announce is not None:
            announce(columns)
        hidden = hidden_ref[...]
        squares = None
        for at in range(0, width, chunk):
            part = slice(at, at + chunk)
            moved = latent_ref[:, part].astype(F32) + jnp.dot(hidden, out_ref[:, part], preferred_element_type=F32)
            rounded = moved.astype(BF16)
            next_ref[:, part] = rounded
            wide = rounded.astype(F32)
            square = folded(wide * wide)
            squares = square if squares is None else squares + square
            if emit is not None and at:
                emit(at - chunk, chunk)
        if emit is not None:
            emit(width - chunk, chunk)
        held_refs = (next_ref, latent_ref)
    return held_refs, squares, columns


def imagine_kernel(
    mine_ref, stay_ref, got_ref, perm_ref, noise_ref, act_ref, dyn_ref, act_in_ref, out_ref, value_ref, *refs
):
    *landed_refs, post_hbm, values_hbm, final_hbm, spare_ref, hidden_ref, values_ref, sems, final_sems = refs
    core = mine_ref[0] % 2
    half = stay_ref.shape[1]
    copies = [
        pltpu.make_async_copy(source, post_hbm.at[:, pl.ds(pl.multiple_of(side * half, LANES), half)], sems.at[k])
        for k, (source, side) in enumerate(((stay_ref, core), (got_ref, 1 - core)))
    ]
    for copy in copies:
        copy.start()
    starts = perm_ref.shape[0]
    perm = perm_ref[...]
    squares = None
    for side in range(2):
        lanes = slice(side * half, (side + 1) * half)
        if len(landed_refs) == 1:
            landed = landed_refs[0][:, side].reshape(starts, half)
        else:
            landed = jnp.concatenate([ref[:, lanes] for ref in landed_refs], axis=0)
        wide = jnp.dot(perm, landed, preferred_element_type=F32)
        spare_ref[1, :, lanes] = wide.astype(BF16)
        square = folded(wide * wide)
        squares = square if squares is None else squares + square
    horizon = noise_ref.shape[0]
    refs, columns = (spare_ref.at[1], None), []

    def emit(at, count):
        columns_here = slice(at, at + count)
        copies.append(
            pltpu.make_async_copy(
                spare_ref.at[(horizon - 1) % 2, :, columns_here],
                final_hbm.at[:, columns_here],
                final_sems.at[at // count],
            )
        )
        copies[-1].start()

    def announce(last):
        lane = iota((starts, LANES), 1)
        table = jnp.zeros((starts, LANES), F32)
        for k, column in enumerate(columns + last):
            table = jnp.where(lane == k, column, table)
        values_ref[...] = table.T[:horizon]
        copies.append(pltpu.make_async_copy(values_ref, values_hbm, sems.at[2]))
        copies[-1].start()

    for step in range(horizon):
        target = spare_ref.at[step % 2]
        refs, squares, new = imagined_steps(
            (refs[0], target),
            squares,
            noise_ref,
            act_ref,
            dyn_ref,
            act_in_ref,
            out_ref,
            value_ref,
            hidden_ref,
            range(step, step + 1),
            *((emit, announce) if step == horizon - 1 else ()),
        )
        columns += new
    for copy in copies:
        copy.wait()


def cost(flops, read):
    return pl.CostEstimate(flops=flops, bytes_accessed=read, transcendentals=0)


def in_hbm(array):
    return pltpu.with_memory_space_constraint(array, pltpu.HBM)


def per_device(
    peer_count,
    features,
    state_write,
    state_read,
    log_decay,
    skip_gain,
    post_gain,
    start_index,
    step_noise,
    act_weight,
    dyn_weight,
    act_in_weight,
    out_weight,
    value_weight,
):
    rows, width = features.shape
    head_count = log_decay.shape[1]
    head_width = width // head_count
    state_size = state_write.shape[1]
    half = width // 2
    heads = head_count // 2
    starts = start_index.shape[0]
    cap = starts // peer_count
    bits = peer_count.bit_length() - 1
    mine = lax.axis_index("seq").reshape(1)
    params = pltpu.CompilerParams(vmem_limit_bytes=12 << 20)
    held = pltpu.VMEM

    chips = peer_count // 2
    direct = chips <= 8 and cap % 8 == 0
    far, near = partner_order(chips) if direct else ([], [])
    order = far + near
    places = [order.index(k) for k in range(len(order))]

    def exchange(array, mask):
        return lax.ppermute(array, "seq", [(i, i ^ mask) for i in range(peer_count)])

    def swap(array, bit):
        return exchange(array, 1 << bit)

    def payload(count):
        blocks = -(-(2 + count) // state_size)
        return held((state_size, half + blocks * LANES), BF16)

    def auxiliary(count):
        return held((-(-(2 + count) // 8) * 8, LANES), F32)

    write_t, read_t, decay_t = state_write.T, state_read.T, log_decay.T
    start_row = start_index.reshape(1, starts)
    x_other = swap(features, 0)
    decay_other, write_other = swap(decay_t, 0), swap(write_t, 0)
    start_other, read_other = swap(start_row, 0), swap(read_t, 0)

    x_own, write_own, sums, perm, wanted = pl.pallas_call(
        functools.partial(own_kernel, cap, places),
        out_shape=(
            held((rows, half), BF16),
            held((state_size, rows), BF16),
            held((heads, rows), F32),
            held((starts, starts), BF16),
            held((1, starts), F32),
        ),
        in_specs=[SMEM] + [HBM] * 4,
        out_specs=(VMEM,) * 5,
        scratch_shapes=[
            pltpu.VMEM((head_count, rows), F32),
            pltpu.VMEM((1, starts), jnp.int32),
            pltpu.SemaphoreType.DMA((4,)),
        ],
        compiler_params=params,
        cost_estimate=cost(0, 4 * rows * width),
    )(mine, in_hbm(features), in_hbm(write_t), in_hbm(decay_t), in_hbm(start_row))

    send, group, chip_x, write, run, run_t, aux = pl.pallas_call(
        functools.partial(before_kernel, cap),
        out_shape=(
            payload(2),
            held((state_size, half), F32),
            held((2 * rows, half), BF16),
            held((state_size, 2 * rows), BF16),
            held((2 * rows, heads), F32),
            held((heads, 2 * rows), F32),
            auxiliary(2),
        ),
        in_specs=[SMEM] + [VMEM] * 8,
        out_specs=(VMEM,) * 7,
        compiler_params=params,
    )(mine, x_own, x_other, write_own, write_other, sums, decay_other, wanted, start_other)

    local_out, read = pl.pallas_call(
        local_kernel,
        out_shape=(held((2 * rows, half), F32), held((2 * rows, state_size), BF16)),
        in_specs=[SMEM, VMEM, VMEM, HBM, VMEM, VMEM, VMEM, HBM],
        out_specs=(VMEM, VMEM),
        scratch_shapes=[
            pltpu.VMEM((state_size, rows), BF16),
            pltpu.VMEM((1, head_count), F32),
            pltpu.SemaphoreType.DMA((2,)),
        ],
        compiler_params=params,
        cost_estimate=cost(8 * rows * rows * width, 4 * rows * width),
    )(mine, chip_x, write, in_hbm(read_t), read_other, run, run_t, in_hbm(skip_gain[None, :]))

    def fetch(token, *weights):
        return pl.pallas_call(
            fetch_kernel,
            out_shape=tuple(held(weight.shape, weight.dtype) for weight in weights),
            in_specs=[ANY] + [HBM] * len(weights),
            out_specs=(VMEM,) * len(weights),
            scratch_shapes=[pltpu.SemaphoreType.DMA((len(weights),))],
            compiler_params=params,
            cost_estimate=cost(0, 2 * sum(weight.size * 2 for weight in weights)),
        )(token, *(in_hbm(weight) for weight in weights))

    prefix, group = local_out, [group]
    for bit in range(1, bits - 1):
        got = swap(send, bit)
        if bit == 2:
            (dyn,) = fetch(aux, dyn_weight)
            aux, _ = lax.optimization_barrier((aux, dyn))
        goes_on = int(bit < bits - 2)
        prefix, send, aux, *group = pl.pallas_call(
            functools.partial(stage_kernel, bit, bit > 1, head_width),
            out_shape=(
                held((state_size, half), F32),
                payload(2 << bit),
                auxiliary(2 << bit),
            )
            + (held((state_size, half), F32),) * goes_on,
            in_specs=[SMEM] + [VMEM] * 3 + [VMEM if bit > 1 else ANY],
            out_specs=(VMEM,) * (3 + goes_on),
            compiler_params=params,
        )(mine, *group, aux, got, prefix)
    got = swap(send, bits - 1)
    out, act, act_in, noise = fetch(aux, out_weight, act_weight, act_in_weight, step_noise)
    block = 2 * cap
    now = starts if direct else 2 * starts
    pick, post, sent = pl.pallas_call(
        functools.partial(after_kernel, bits - 1, order),
        out_shape=(
            held((2 * starts, 2 * rows), BF16),
            held((2 * rows, half), BF16),
            held((now, half), BF16),
        ),
        in_specs=[SMEM] + [VMEM] * 3 + [ANY] + [VMEM] * 4,
        out_specs=(VMEM,) * 3,
        scratch_shapes=[
            pltpu.VMEM((state_size, half), BF16),
            pltpu.VMEM((2 * rows, half), F32),
            pltpu.VMEM((2 * rows, half), F32),
        ],
        compiler_params=params,
    )(mine, prefix, aux, got, act_in, local_out, read, run, post_gain[None, :])
    shares = (held((rows, half), BF16),) * 2
    if direct:
        given = swap(sent, 0)
        keep, stay, go = pl.pallas_call(
            rest_kernel,
            out_shape=(held((starts, half), BF16),) + shares,
            in_specs=[SMEM, VMEM, VMEM],
            out_specs=(VMEM,) * 3,
            compiler_params=params,
            cost_estimate=cost(4 * starts * rows * half, 2 * rows * width),
        )(mine, post, pick)
        blocks = pl.pallas_call(
            merge_kernel,
            out_shape=(held((block, width), BF16),) * chips,
            in_specs=[SMEM, VMEM, VMEM],
            out_specs=(VMEM,) * chips,
            compiler_params=params,
        )(mine, keep, given)
        landed = [exchange(array, 2 * k) if k else array for array, k in zip(blocks, order)]
    else:
        stay, go = pl.pallas_call(
            share_kernel,
            out_shape=shares,
            in_specs=[SMEM, VMEM],
            out_specs=(VMEM,) * 2,
            compiler_params=params,
        )(mine, post)
        landed = [
            lax.all_to_all(
                sent.reshape(peer_count, block, half), "seq", split_axis=0, concat_axis=0, tiled=True
            ).reshape(chips, 2, block, half)
        ]
    horizon = step_noise.shape[0]
    posterior, values, final_latent = pl.pallas_call(
        imagine_kernel,
        out_shape=(
            jax.ShapeDtypeStruct((rows, width), BF16),
            jax.ShapeDtypeStruct((horizon, starts), F32),
            jax.ShapeDtypeStruct((starts, width), BF16),
        ),
        in_specs=[SMEM] + [VMEM] * (9 + len(landed)),
        out_specs=(HBM, HBM, HBM),
        scratch_shapes=[
            pltpu.VMEM((2, starts, width), BF16),
            pltpu.VMEM((starts, dyn_weight.shape[1]), BF16),
            pltpu.VMEM((horizon, starts), F32),
            pltpu.SemaphoreType.DMA((3,)),
            pltpu.SemaphoreType.DMA((width // 256,)),
        ],
        compiler_params=pltpu.CompilerParams(vmem_limit_bytes=16 << 20),
    )(mine, stay, swap(go, 0), perm, noise, act, dyn, act_in, out, value_weight[None, :], *landed)
    return (posterior, values, final_latent)


def solution(mesh):
    whole = P()
    by_row = P(("groups", "seq"), None)
    placed = (
        by_row,
        by_row,
        by_row,
        by_row,
        whole,
        whole,
        P(("groups", "seq")),
        P(None, ("groups", "seq"), None),
        whole,
        whole,
        whole,
        whole,
        whole,
    )
    return jax.shard_map(
        functools.partial(per_device, mesh.shape["seq"]),
        mesh=mesh,
        in_specs=placed,
        out_specs=(by_row, P(None, ("groups", "seq")), by_row),
        check_vma=False,
    )
```

```python
import functools
import jax
import jax.numpy as jnp
from jax import lax
from jax.experimental import pallas as pl
from jax.experimental.pallas import tpu as pltpu
from jax.sharding import PartitionSpec as P

F32 = jnp.float32
BF16 = jnp.bfloat16
LANES = 128
VMEM = pl.BlockSpec(memory_space=pltpu.VMEM)
SMEM = pl.BlockSpec(memory_space=pltpu.SMEM)
HBM = pl.BlockSpec(memory_space=pltpu.HBM)
ANY = pl.BlockSpec(memory_space=pl.ANY)


def iota(shape, dim):
    return lax.broadcasted_iota(jnp.int32, shape, dim)


def mask16(condition):
    return condition.astype(F32).astype(BF16)


def two_heads(cols, pair, head_width, shape):
    first = jnp.broadcast_to(cols[:, 2 * pair : 2 * pair + 1], shape)
    second = jnp.broadcast_to(cols[:, 2 * pair + 1 : 2 * pair + 2], shape)
    return jnp.where(iota(shape, 1) < head_width, first, second)


def stack_rows(rows, count):
    used = sum(row.shape[0] for row in rows)
    if used < count:
        rows = list(rows) + [jnp.zeros((count - used, LANES), F32)]
    return jnp.concatenate(rows, axis=0)


def write_meta(send_ref, decay, wanted, half, state_size):
    high = decay.astype(BF16).astype(F32)
    blocks = (send_ref.shape[1] - half) // LANES
    meta = stack_rows([high, decay - high, wanted], blocks * state_size).astype(BF16)
    for block in range(blocks):
        send_ref[:, half + block * LANES : half + (block + 1) * LANES] = meta[
            block * state_size : (block + 1) * state_size
        ]


def read_meta(got_ref, count, half, state_size):
    blocks = (got_ref.shape[1] - half) // LANES
    meta = jnp.concatenate(
        [got_ref[:, half + block * LANES : half + (block + 1) * LANES].astype(F32) for block in range(blocks)], axis=0
    )
    return meta[0:1] + meta[1:2], meta[2 : 2 + count]


def spread_rows(rows, half, head_width):
    pieces = []
    for row in rows:
        high = row.astype(BF16).astype(F32)
        pieces += [high, row - high]
    expand = mask16(iota((LANES, half), 0) == iota((LANES, half), 1) // head_width)
    wide = jnp.dot(stack_rows(pieces, 16).astype(BF16), expand, preferred_element_type=F32)
    return [wide[2 * k : 2 * k + 1] + wide[2 * k + 1 : 2 * k + 2] for k in range(len(rows))]


def partner_order(chips):
    order = sorted(range(1, chips), key=lambda k: (k == 1, -(k & 1), -k))
    return order, [0]


def looked_up(index, table):
    found = jnp.zeros_like(index)
    for k, value in enumerate(table):
        if value:
            found = jnp.where(index == k, value, found)
    return found


def requests(start_row, rows, cap):
    starts = start_row.shape[1]
    square = (starts, starts)
    index = jnp.broadcast_to(start_row.astype(F32), square)
    index_t = index.T
    owner = jnp.floor(index * (1.0 / rows))
    owner_t = jnp.floor(index_t * (1.0 / rows))
    earlier = (iota(square, 1) < iota(square, 0)) & (owner == owner_t)
    rank = jnp.sum(earlier.astype(F32), axis=1, keepdims=True)
    perm = (owner_t * cap + rank == iota(square, 1).astype(F32)).astype(F32)
    wanted = jnp.sum(perm * (index_t - owner_t * rows), axis=0, keepdims=True)
    return perm, wanted, owner_t.astype(jnp.int32), rank.astype(jnp.int32)


def own_kernel(
    cap, places, mine_ref, x_hbm, write_hbm, decay_hbm, start_hbm, x_ref, write_ref, sums_ref, perm_ref, wanted_ref,
    decay_ref, start_ref, sems,
):
    core = mine_ref[0] % 2
    rows, half = x_ref.shape
    heads = sums_ref.shape[0]
    lanes_at = pl.multiple_of(core * half, LANES)
    copies = [
        pltpu.make_async_copy(source, target, sems.at[k])
        for k, (source, target) in enumerate(
            (
                (x_hbm.at[:, pl.ds(lanes_at, half)], x_ref),
                (start_hbm, start_ref),
                (decay_hbm, decay_ref),
                (write_hbm, write_ref),
            )
        )
    ]
    for copy in copies:
        copy.start()
    copies[1].wait()
    perm, wanted, owner, rank = requests(start_ref[...], rows, cap)
    if places:
        place = looked_up((owner // 2) ^ (mine_ref[0] // 2), places)
        perm = mask16((place * 2 + owner % 2) * cap + rank == iota(perm.shape, 1))
    perm_ref[...] = perm.astype(BF16)
    wanted_ref[...] = wanted
    copies[2].wait()
    sums_ref[...] = running_sums(jnp.where(core == 0, decay_ref[:heads], decay_ref[heads:]))
    copies[0].wait()
    copies[3].wait()


def running_sums(decays):
    rows = decays.shape[1]
    upper = mask16(iota((rows, rows), 0) <= iota((rows, rows), 1))
    high = decays.astype(BF16).astype(F32)
    middle = (decays - high).astype(BF16).astype(F32)
    terms = jnp.concatenate([high, middle, decays - high - middle], axis=0).astype(BF16)
    sums = jnp.dot(terms, upper, preferred_element_type=F32)
    heads = decays.shape[0]
    return sums[:heads] + (sums[heads : 2 * heads] + sums[2 * heads :])


def before_kernel(
    cap, mine_ref, x_own_ref, x_other_ref, write_own_ref, write_other_ref, sums_ref, decay_other_ref, wanted_ref,
    start_other_ref, send_ref, ends_ref, x_ref, write_ref, run_ref, run_t_ref, aux_ref,
):
    core = mine_ref[0] % 2
    first = core == 0
    rows, half = x_own_ref.shape
    state_size = write_ref.shape[0]
    heads = run_ref.shape[1]
    head_width = half // heads
    own, other = x_own_ref[...], x_other_ref[:, pl.ds(pl.multiple_of(core * half, LANES), half)]
    x_ref[:rows, :] = jnp.where(first, own, other)
    x_ref[rows:, :] = jnp.where(first, other, own)
    own = sums_ref[...]
    other = running_sums(jnp.where(first, decay_other_ref[:heads], decay_other_ref[heads:]))
    one, two = jnp.where(first, own, other), jnp.where(first, other, own)
    run_t = jnp.concatenate([one, two + one[:, rows - 1 :]], axis=1)
    run_t_ref[...] = run_t
    run = run_t.T
    run_ref[...] = run
    last = run[2 * rows - 1 :]
    tail = jnp.exp(last - run)
    own, other = write_own_ref[...], write_other_ref[...]
    write = jnp.concatenate([jnp.where(first, own, other), jnp.where(first, other, own)], axis=1)
    write_ref[...] = write
    for pair in range(heads // 2):
        lanes = slice(pair * LANES, (pair + 1) * LANES)
        scaled = x_ref[:, lanes].astype(F32) * two_heads(tail, pair, head_width, (2 * rows, LANES))
        ends = jnp.dot(write, scaled.astype(BF16), preferred_element_type=F32)
        ends_ref[:, lanes] = ends
        send_ref[:, lanes] = ends.astype(BF16)
    _, other, _, _ = requests(start_other_ref[...], rows, cap)
    own = wanted_ref[...]
    wanted = jnp.concatenate([jnp.where(first, own, other), jnp.where(first, other, own)], axis=0)
    total = jnp.concatenate([jnp.exp(last), jnp.zeros((1, LANES - heads), F32)], axis=1)
    aux_ref[...] = stack_rows([total, jnp.ones((1, LANES), F32), wanted], aux_ref.shape[0])
    write_meta(send_ref, total, wanted, half, state_size)


def local_kernel(
    mine_ref, x_ref, write_ref, read_hbm, read_other_ref, run_ref, run_t_ref, skip_hbm, out_ref, read_out,
    read_ref, skip_ref, sems,
):
    copies = [
        pltpu.make_async_copy(read_hbm, read_ref, sems.at[0]),
        pltpu.make_async_copy(skip_hbm, skip_ref, sems.at[1]),
    ]
    for copy in copies:
        copy.start()
    for copy in copies:
        copy.wait()
    first = mine_ref[0] % 2 == 0
    rows, half = x_ref.shape[0] // 2, x_ref.shape[1]
    heads = run_ref.shape[1]
    head_width = half // heads
    own, other = read_ref[...], read_other_ref[...]
    read = jnp.concatenate([jnp.where(first, own, other), jnp.where(first, other, own)], axis=1).T
    read_out[...] = read
    gram = jnp.dot(read, write_ref[...], preferred_element_type=F32)
    skip = jnp.where(first, skip_ref[:, :heads], skip_ref[:, heads:])
    mask = iota((rows, rows), 0) >= iota((rows, rows), 1)
    for chunk in range(2):
        at, count = chunk * rows, (chunk + 1) * rows
        lane = iota((count, LANES), 1)
        for pair in range(heads // 2):
            lanes = slice(pair * LANES, (pair + 1) * LANES)
            weights = []
            for head in (2 * pair, 2 * pair + 1):
                for back in range(chunk + 1):
                    seen = slice(back * rows, (back + 1) * rows)
                    spread = run_ref[at:count, head : head + 1] - run_t_ref[head : head + 1, seen]
                    if back == chunk:
                        spread = jnp.where(mask, spread, -jnp.inf)
                    weights.append((jnp.exp(spread) * gram[at:count, seen]).astype(BF16))
            x = x_ref[:count, lanes]
            zero = jnp.zeros_like(x)
            split = jnp.concatenate(
                [jnp.where(lane < head_width, x, zero), jnp.where(lane < head_width, zero, x)], axis=0
            )
            inner = jnp.dot(jnp.concatenate(weights, axis=1), split, preferred_element_type=F32)
            factor = two_heads(skip, pair, head_width, (1, LANES))
            out_ref[at:count, lanes] = inner + factor * x[at:count].astype(F32)


def stage_kernel(bit, has_prefix, head_width, mine_ref, group_ref, aux_ref, got_ref, prefix_ref, prefix_out, send_ref, aux_out, *group_out):
    state_size, half = group_ref.shape
    count = 1 << bit
    later = (mine_ref[0] >> bit) % 2 == 1
    new_decay, new_wanted = read_meta(got_ref, count, half, state_size)
    decay, prefix_decay = aux_ref[0:1], aux_ref[1:2]
    wanted = aux_ref[2 : 2 + count]
    into, across = spread_rows([prefix_decay, jnp.where(later, decay, new_decay)], half, head_width)
    group, got = group_ref[...], got_ref[:, :half].astype(F32)
    moved = into * got
    if has_prefix:
        moved = prefix_ref[...] + moved
        prefix_out[...] = jnp.where(later, moved, prefix_ref[...])
    else:
        prefix_out[...] = jnp.where(later, moved, jnp.zeros_like(moved))
    total = jnp.where(later, got, group) * across + jnp.where(later, group, got)
    for ref in group_out:
        ref[...] = total
    send_ref[:, :half] = total.astype(BF16)
    wanted = jnp.concatenate(
        [jnp.where(later, new_wanted, wanted), jnp.where(later, wanted, new_wanted)], axis=0
    )
    write_meta(send_ref, decay * new_decay, wanted, half, state_size)
    aux_out[...] = stack_rows(
        [decay * new_decay, jnp.where(later, prefix_decay * new_decay, prefix_decay), wanted], aux_out.shape[0]
    )


def last_stage(bit, rows, head_width, order, mine_ref, prefix_ref, aux_ref, got_ref, carry_ref, pick_ref):
    state_size, half = prefix_ref.shape
    count = 1 << bit
    mine = mine_ref[0]
    later = (mine >> bit) % 2 == 1
    _, new_wanted = read_meta(got_ref, count, half, state_size)
    (into,) = spread_rows([aux_ref[1:2]], half, head_width)
    prefix = prefix_ref[...]
    carry_ref[...] = jnp.where(later, prefix + into * got_ref[:, :half].astype(F32), prefix).astype(BF16)
    wanted = aux_ref[2 : 2 + count]
    wanted = jnp.concatenate(
        [jnp.where(later, new_wanted, wanted), jnp.where(later, wanted, new_wanted)], axis=0
    )
    peers = 2 * count
    picks = pick_ref.shape[0]
    both = picks // peers
    table = stack_rows([wanted], LANES) if peers < LANES else wanted
    device = iota((picks, LANES), 0) // both
    if order:
        chip = looked_up(device % len(order), order) ^ (mine // 2)
        device = chip * 2 + (device // len(order) + mine) % 2
    asker = mask16(device == iota((picks, LANES), 1))
    by_slot = jnp.dot(asker, table.astype(BF16), preferred_element_type=F32)
    turn = iota((picks, LANES), 0) % both
    here = iota((picks, LANES), 1) == (mine // 2) * both + turn
    asked = jnp.sum(jnp.where(here, by_slot + ((turn // (both // 2)) * rows).astype(F32), 0.0), axis=1, keepdims=True)
    pick_ref[...] = mask16(asked == iota(pick_ref.shape, 1).astype(F32))


def normalize(mine_ref, local_ref, read_ref, run_ref, carry_ref, gain_ref, mixed_ref, total_ref, post_ref):
    core = mine_ref[0] % 2
    rows, half = local_ref.shape
    heads = run_ref.shape[1]
    head_width = half // heads
    entered = jnp.exp(run_ref[...])
    square = (LANES, LANES)
    same_head = mask16(iota(square, 0) // head_width == iota(square, 1) // head_width)
    gain = jnp.where(core == 0, gain_ref[:, :half], gain_ref[:, half:])
    blocks = [slice(k * LANES, (k + 1) * LANES) for k in range(half // LANES)]
    total_ref[...] = jnp.dot(read_ref[...], carry_ref[...], preferred_element_type=F32)
    for pair, lanes in enumerate(blocks):
        mixed_ref[:, lanes] = local_ref[:, lanes] + total_ref[:, lanes] * two_heads(
            entered, pair, head_width, (rows, LANES)
        )
    for lanes in blocks:
        mixed = mixed_ref[:, lanes]
        squares = mixed * mixed
        high = squares.astype(BF16)
        low = (squares - high.astype(F32)).astype(BF16)
        total_ref[:, lanes] = jnp.dot(high, same_head, preferred_element_type=F32) + jnp.dot(
            low, same_head, preferred_element_type=F32
        )
    for lanes in blocks:
        scale = lax.rsqrt(total_ref[:, lanes] * (1.0 / head_width) + 1e-05)
        post_ref[:, lanes] = (mixed_ref[:, lanes] * scale * gain[:, lanes]).astype(BF16)


def picked_rows(pick, post_ref):
    return jnp.dot(pick, post_ref[...], preferred_element_type=F32).astype(BF16)


def after_kernel(
    bit, order, mine_ref, prefix_ref, aux_ref, arrived_ref, token_ref, local_ref, read_ref, run_ref, gain_ref,
    pick_ref, post_ref, sent_ref, carry_ref, mixed_ref, total_ref,
):
    rows, half = local_ref.shape
    last_stage(
        bit, rows // 2, half // run_ref.shape[1], order, mine_ref, prefix_ref, aux_ref, arrived_ref, carry_ref, pick_ref
    )
    normalize(mine_ref, local_ref, read_ref, run_ref, carry_ref, gain_ref, mixed_ref, total_ref, post_ref)
    count = sent_ref.shape[0]
    first = 0 if count == pick_ref.shape[0] else pick_ref.shape[0] // 2
    sent_ref[...] = picked_rows(pick_ref[first : first + count, :], post_ref)


def share_kernel(mine_ref, post_ref, stay_ref, go_ref):
    core = mine_ref[0] % 2
    rows = stay_ref.shape[0]
    stay_ref[...] = post_ref[pl.ds(pl.multiple_of(core * rows, rows), rows), :]
    go_ref[...] = post_ref[pl.ds(pl.multiple_of((1 - core) * rows, rows), rows), :]


def rest_kernel(mine_ref, post_ref, pick_ref, keep_ref, stay_ref, go_ref):
    keep_ref[...] = picked_rows(pick_ref[: keep_ref.shape[0], :], post_ref)
    share_kernel(mine_ref, post_ref, stay_ref, go_ref)


def merge_kernel(mine_ref, keep_ref, got_ref, *block_refs):
    first = mine_ref[0] % 2 == 0
    half = keep_ref.shape[1]
    keep, got = keep_ref[...], got_ref[...]
    left, right = jnp.where(first, keep, got), jnp.where(first, got, keep)
    size = block_refs[0].shape[0]
    for k, ref in enumerate(block_refs):
        ref[:, :half] = left[k * size : (k + 1) * size]
        ref[:, half:] = right[k * size : (k + 1) * size]


def fetch_kernel(token_ref, *refs):
    count = (len(refs) - 1) // 2
    sems = refs[-1]
    copies = [pltpu.make_async_copy(refs[k], refs[count + k], sems.at[k]) for k in range(count)]
    for copy in copies:
        copy.start()
    for copy in copies:
        copy.wait()


def folded(array):
    total = array[:, :LANES]
    for k in range(1, array.shape[1] // LANES):
        total = total + array[:, k * LANES : (k + 1) * LANES]
    return total


def imagined_steps(held_refs, squares, noise_ref, act_ref, dyn_ref, act_in_ref, out_ref, value_ref, hidden_ref, steps, emit=None, announce=None):
    width, inside = dyn_ref.shape
    chunk = 256
    columns = []
    for step in steps:
        latent_ref, next_ref = held_refs
        scale = lax.rsqrt(jnp.sum(squares, axis=1, keepdims=True) * (1.0 / width) + 1e-06)
        latent = latent_ref[...]
        action = jnp.dot(latent, act_ref[...], preferred_element_type=F32)
        action = jnp.tanh(action * scale).astype(BF16)
        value = None
        for at in range(0, inside, chunk):
            part = slice(at, at + chunk)
            inner = jnp.dot(latent, dyn_ref[:, part], preferred_element_type=F32) * scale + jnp.dot(
                action, act_in_ref[:, part], preferred_element_type=F32
            )
            hidden = (inner / (1.0 + jnp.exp(-inner)) + noise_ref[step, :, part].astype(F32)).astype(BF16)
            hidden_ref[:, part] = hidden
            worth = folded(hidden.astype(F32) * value_ref[:, part].astype(F32))
            value = worth if value is None else value + worth
        columns.append(jnp.sum(value, axis=1, keepdims=True))
        if announce is not None:
            announce(columns)
        hidden = hidden_ref[...]
        squares = None
        for at in range(0, width, chunk):
            part = slice(at, at + chunk)
            moved = latent_ref[:, part].astype(F32) + jnp.dot(hidden, out_ref[:, part], preferred_element_type=F32)
            rounded = moved.astype(BF16)
            next_ref[:, part] = rounded
            wide = rounded.astype(F32)
            square = folded(wide * wide)
            squares = square if squares is None else squares + square
            if emit is not None and at:
                emit(at - chunk, chunk)
        if emit is not None:
            emit(width - chunk, chunk)
        held_refs = (next_ref, latent_ref)
    return held_refs, squares, columns


def imagine_kernel(
    mine_ref, stay_ref, got_ref, perm_ref, noise_ref, act_ref, dyn_ref, act_in_ref, out_ref, value_ref, *refs
):
    *landed_refs, post_hbm, values_hbm, final_hbm, spare_ref, hidden_ref, values_ref, sems, final_sems = refs
    core = mine_ref[0] % 2
    half = stay_ref.shape[1]
    copies = [
        pltpu.make_async_copy(source, post_hbm.at[:, pl.ds(pl.multiple_of(side * half, LANES), half)], sems.at[k])
        for k, (source, side) in enumerate(((stay_ref, core), (got_ref, 1 - core)))
    ]
    for copy in copies:
        copy.start()
    starts = perm_ref.shape[0]
    perm = perm_ref[...]
    squares = None
    for side in range(2):
        lanes = slice(side * half, (side + 1) * half)
        if len(landed_refs) == 1:
            landed = landed_refs[0][:, side].reshape(starts, half)
        else:
            landed = jnp.concatenate([ref[:, lanes] for ref in landed_refs], axis=0)
        wide = jnp.dot(perm, landed, preferred_element_type=F32)
        spare_ref[1, :, lanes] = wide.astype(BF16)
        square = folded(wide * wide)
        squares = square if squares is None else squares + square
    horizon = noise_ref.shape[0]
    refs, columns = (spare_ref.at[1], None), []

    def emit(at, count):
        columns_here = slice(at, at + count)
        copies.append(
            pltpu.make_async_copy(
                spare_ref.at[(horizon - 1) % 2, :, columns_here],
                final_hbm.at[:, columns_here],
                final_sems.at[at // count],
            )
        )
        copies[-1].start()

    def announce(last):
        lane = iota((starts, LANES), 1)
        table = jnp.zeros((starts, LANES), F32)
        for k, column in enumerate(columns + last):
            table = jnp.where(lane == k, column, table)
        values_ref[...] = table.T[:horizon]
        copies.append(pltpu.make_async_copy(values_ref, values_hbm, sems.at[2]))
        copies[-1].start()

    for step in range(horizon):
        target = spare_ref.at[step % 2]
        refs, squares, new = imagined_steps(
            (refs[0], target),
            squares,
            noise_ref,
            act_ref,
            dyn_ref,
            act_in_ref,
            out_ref,
            value_ref,
            hidden_ref,
            range(step, step + 1),
            *((emit, announce) if step == horizon - 1 else ()),
        )
        columns += new
    for copy in copies:
        copy.wait()


def cost(flops, read):
    return pl.CostEstimate(flops=flops, bytes_accessed=read, transcendentals=0)


def in_hbm(array):
    return pltpu.with_memory_space_constraint(array, pltpu.HBM)


def per_device(
    peer_count,
    features,
    state_write,
    state_read,
    log_decay,
    skip_gain,
    post_gain,
    start_index,
    step_noise,
    act_weight,
    dyn_weight,
    act_in_weight,
    out_weight,
    value_weight,
):
    rows, width = features.shape
    head_count = log_decay.shape[1]
    head_width = width // head_count
    state_size = state_write.shape[1]
    half = width // 2
    heads = head_count // 2
    starts = start_index.shape[0]
    cap = starts // peer_count
    bits = peer_count.bit_length() - 1
    mine = lax.axis_index("seq").reshape(1)
    params = pltpu.CompilerParams(vmem_limit_bytes=12 << 20)
    held = pltpu.VMEM

    chips = peer_count // 2
    direct = chips <= 8 and cap % 8 == 0
    far, near = partner_order(chips) if direct else ([], [])
    order = far + near
    places = [order.index(k) for k in range(len(order))]

    def exchange(array, mask):
        return lax.ppermute(array, "seq", [(i, i ^ mask) for i in range(peer_count)])

    def swap(array, bit):
        return exchange(array, 1 << bit)

    def payload(count):
        blocks = -(-(2 + count) // state_size)
        return held((state_size, half + blocks * LANES), BF16)

    def auxiliary(count):
        return held((-(-(2 + count) // 8) * 8, LANES), F32)

    write_t, read_t, decay_t = state_write.T, state_read.T, log_decay.T
    start_row = start_index.reshape(1, starts)
    x_other = swap(features, 0)
    decay_other, write_other = swap(decay_t, 0), swap(write_t, 0)
    start_other, read_other = swap(start_row, 0), swap(read_t, 0)

    x_own, write_own, sums, perm, wanted = pl.pallas_call(
        functools.partial(own_kernel, cap, places),
        out_shape=(
            held((rows, half), BF16),
            held((state_size, rows), BF16),
            held((heads, rows), F32),
            held((starts, starts), BF16),
            held((1, starts), F32),
        ),
        in_specs=[SMEM] + [HBM] * 4,
        out_specs=(VMEM,) * 5,
        scratch_shapes=[
            pltpu.VMEM((head_count, rows), F32),
            pltpu.VMEM((1, starts), jnp.int32),
            pltpu.SemaphoreType.DMA((4,)),
        ],
        compiler_params=params,
        cost_estimate=cost(0, 4 * rows * width),
    )(mine, in_hbm(features), in_hbm(write_t), in_hbm(decay_t), in_hbm(start_row))

    send, group, chip_x, write, run, run_t, aux = pl.pallas_call(
        functools.partial(before_kernel, cap),
        out_shape=(
            payload(2),
            held((state_size, half), F32),
            held((2 * rows, half), BF16),
            held((state_size, 2 * rows), BF16),
            held((2 * rows, heads), F32),
            held((heads, 2 * rows), F32),
            auxiliary(2),
        ),
        in_specs=[SMEM] + [VMEM] * 8,
        out_specs=(VMEM,) * 7,
        compiler_params=params,
    )(mine, x_own, x_other, write_own, write_other, sums, decay_other, wanted, start_other)

    local_out, read = pl.pallas_call(
        local_kernel,
        out_shape=(held((2 * rows, half), F32), held((2 * rows, state_size), BF16)),
        in_specs=[SMEM, VMEM, VMEM, HBM, VMEM, VMEM, VMEM, HBM],
        out_specs=(VMEM, VMEM),
        scratch_shapes=[
            pltpu.VMEM((state_size, rows), BF16),
            pltpu.VMEM((1, head_count), F32),
            pltpu.SemaphoreType.DMA((2,)),
        ],
        compiler_params=params,
        cost_estimate=cost(8 * rows * rows * width, 4 * rows * width),
    )(mine, chip_x, write, in_hbm(read_t), read_other, run, run_t, in_hbm(skip_gain[None, :]))

    def fetch(token, *weights):
        return pl.pallas_call(
            fetch_kernel,
            out_shape=tuple(held(weight.shape, weight.dtype) for weight in weights),
            in_specs=[ANY] + [HBM] * len(weights),
            out_specs=(VMEM,) * len(weights),
            scratch_shapes=[pltpu.SemaphoreType.DMA((len(weights),))],
            compiler_params=params,
            cost_estimate=cost(0, 2 * sum(weight.size * 2 for weight in weights)),
        )(token, *(in_hbm(weight) for weight in weights))

    prefix, group = local_out, [group]
    for bit in range(1, bits - 1):
        got = swap(send, bit)
        if bit == 2:
            (dyn,) = fetch(aux, dyn_weight)
            aux, _ = lax.optimization_barrier((aux, dyn))
        goes_on = int(bit < bits - 2)
        prefix, send, aux, *group = pl.pallas_call(
            functools.partial(stage_kernel, bit, bit > 1, head_width),
            out_shape=(
                held((state_size, half), F32),
                payload(2 << bit),
                auxiliary(2 << bit),
            )
            + (held((state_size, half), F32),) * goes_on,
            in_specs=[SMEM] + [VMEM] * 3 + [VMEM if bit > 1 else ANY],
            out_specs=(VMEM,) * (3 + goes_on),
            compiler_params=params,
        )(mine, *group, aux, got, prefix)
    got = swap(send, bits - 1)
    out, act, act_in, noise = fetch(aux, out_weight, act_weight, act_in_weight, step_noise)
    block = 2 * cap
    now = starts if direct else 2 * starts
    pick, post, sent = pl.pallas_call(
        functools.partial(after_kernel, bits - 1, order),
        out_shape=(
            held((2 * starts, 2 * rows), BF16),
            held((2 * rows, half), BF16),
            held((now, half), BF16),
        ),
        in_specs=[SMEM] + [VMEM] * 3 + [ANY] + [VMEM] * 4,
        out_specs=(VMEM,) * 3,
        scratch_shapes=[
            pltpu.VMEM((state_size, half), BF16),
            pltpu.VMEM((2 * rows, half), F32),
            pltpu.VMEM((2 * rows, half), F32),
        ],
        compiler_params=params,
    )(mine, prefix, aux, got, act_in, local_out, read, run, post_gain[None, :])
    shares = (held((rows, half), BF16),) * 2
    if direct:
        given = swap(sent, 0)
        keep, stay, go = pl.pallas_call(
            rest_kernel,
            out_shape=(held((starts, half), BF16),) + shares,
            in_specs=[SMEM, VMEM, VMEM],
            out_specs=(VMEM,) * 3,
            compiler_params=params,
            cost_estimate=cost(4 * starts * rows * half, 2 * rows * width),
        )(mine, post, pick)
        blocks = pl.pallas_call(
            merge_kernel,
            out_shape=(held((block, width), BF16),) * chips,
            in_specs=[SMEM, VMEM, VMEM],
            out_specs=(VMEM,) * chips,
            compiler_params=params,
        )(mine, keep, given)
        landed = [exchange(array, 2 * k) if k else array for array, k in zip(blocks, order)]
    else:
        stay, go = pl.pallas_call(
            share_kernel,
            out_shape=shares,
            in_specs=[SMEM, VMEM],
            out_specs=(VMEM,) * 2,
            compiler_params=params,
        )(mine, post)
        landed = [
            lax.all_to_all(
                sent.reshape(peer_count, block, half), "seq", split_axis=0, concat_axis=0, tiled=True
            ).reshape(chips, 2, block, half)
        ]
    horizon = step_noise.shape[0]
    posterior, values, final_latent = pl.pallas_call(
        imagine_kernel,
        out_shape=(
            jax.ShapeDtypeStruct((rows, width), BF16),
            jax.ShapeDtypeStruct((horizon, starts), F32),
            jax.ShapeDtypeStruct((starts, width), BF16),
        ),
        in_specs=[SMEM] + [VMEM] * (9 + len(landed)),
        out_specs=(HBM, HBM, HBM),
        scratch_shapes=[
            pltpu.VMEM((2, starts, width), BF16),
            pltpu.VMEM((starts, dyn_weight.shape[1]), BF16),
            pltpu.VMEM((horizon, starts), F32),
            pltpu.SemaphoreType.DMA((3,)),
            pltpu.SemaphoreType.DMA((width // 256,)),
        ],
        compiler_params=pltpu.CompilerParams(vmem_limit_bytes=16 << 20),
    )(mine, stay, swap(go, 0), perm, noise, act, dyn, act_in, out, value_weight[None, :], *landed)
    return (posterior, values, final_latent)


def solution(mesh):
    whole = P()
    by_row = P(("groups", "seq"), None)
    placed = (
        by_row,
        by_row,
        by_row,
        by_row,
        whole,
        whole,
        P(("groups", "seq")),
        P(None, ("groups", "seq"), None),
        whole,
        whole,
        whole,
        whole,
        whole,
    )
    return jax.shard_map(
        functools.partial(per_device, mesh.shape["seq"]),
        mesh=mesh,
        in_specs=placed,
        out_specs=(by_row, P(None, ("groups", "seq")), by_row),
        check_vma=False,
    )
```
